32 devices in a mesh: expert: 8 (over z, core), shard: 4 (over y, x).
Axes of the slice: x: 2, y: 2, z: 4, core: 2. Of those that a mesh axis runs over, the one named last changes fastest.
Arguments:
- inputs: float32 [16384, 768], P(('expert', 'shard')), may hold values from -6 to 6
- cotangent: float32 [16384, 768], P(('expert', 'shard')), may hold values from -6 to 6
- norm_one: bfloat16 [768], P('shard'), may hold values from 0.5 to 1.5
- qkv_weight: bfloat16 [768, 2304], P('shard'), may hold values from -0.21875 to 0.21875
- out_weight: bfloat16 [768, 768], P('shard'), may hold values from -3.5 to 3.5
- norm_two: bfloat16 [768], P('shard'), may hold values from 0.5 to 1.5
- shared_gate: bfloat16 [768, 2048], P(None, 'shard'), may hold values from -0.21875 to 0.21875
- shared_up: bfloat16 [768, 2048], P(None, 'shard'), may hold values from -0.21875 to 0.21875
- shared_down: bfloat16 [2048, 768], P('shard'), may hold values from -0.125 to 0.125
- expert_gate: bfloat16 [8, 768, 2048], P('expert'), may hold values from -0.21875 to 0.21875
- expert_up: bfloat16 [8, 768, 2048], P('expert'), may hold values from -0.21875 to 0.21875
- expert_down: bfloat16 [8, 2048, 768], P('expert'), may hold values from -0.125 to 0.125
- gate_weights: float32 [16384, 2], P(('expert', 'shard')), may hold values from 0.25 to 1
- routes: int32 [16384, 2], P(('expert', 'shard')), may hold values from 0 to 7, all different within a row; in each aligned block of 512 rows (0 to 511, 512 to 1023, ...) at most 256 rows name the same one
- prefix: int32 [32], P(('expert', 'shard')), may hold values from 51 to 256
Outputs:
- output: float32 [16384, 768], P(('expert', 'shard'))
- input_grad: float32 [16384, 768], P(('expert', 'shard'))
- norm_one_grad: float32 [768], P('shard')
- qkv_grad: float32 [768, 2304], P('shard')
- out_grad: float32 [768, 768], P('shard')
- norm_two_grad: float32 [768], P('shard')
- shared_gate_grad: float32 [768, 2048], P(None, 'shard')
- shared_up_grad: float32 [768, 2048], P(None, 'shard')
- shared_down_grad: float32 [2048, 768], P('shard')
- expert_gate_grad: float32 [8, 768, 2048], P('expert', None, 'shard')
- expert_up_grad: float32 [8, 768, 2048], P('expert', None, 'shard')
- expert_down_grad: float32 [8, 2048, 768], P('expert', 'shard')
- gate_weights_grad: float32 [16384, 2], P(('expert', 'shard'))
The draws below stay inside these ranges and needn't reach their ends.
Inputs may be any that keep to these rules, and one draw needn't show every extreme that they name: `routes`: each row names 2 different experts. Among the 512 rows of one device no expert is named more than 256 times, and some device names some expert exactly 256 times. `prefix`: leading tokens of a sequence that all its tokens attend to.
All inputs are finite; a program needn't handle non-finite values.
Results may differ from the reference program's by a relative error of at most 0.02.
Values may be sent and summed in bfloat16 or wider, within the bound.
A program may use at most 256 MiB of HBM per device.

```python
import math
from functools import partial
import jax
import jax.numpy as jnp
import numpy as np
from jax import lax

D = 768
HEADS = 12
HEAD_DIM = 64
FF = 2048
EFF = 2048
TOP = 2
TOK_DEV = 512
EXPERTS = 8
SEQS = 32
TOKENS = 16384
CAP = 256


def place_ends(array, key, smallest, high):
    shape = array.shape
    index_at = [jax.random.randint(jax.random.fold_in(key, axis), (), 0, shape[axis]) for axis in range(len(shape))]
    array = array.at[tuple(index_at)].set(smallest)
    longest = shape.index(max(shape))
    index_at[longest] = (index_at[longest] + 1) % shape[longest]
    return array.at[tuple(index_at)].set(high)


def level_of(stream_key, extent, cuts, low, top_value):
    def one(dim, blocks):
        draws = jax.random.uniform(jax.random.fold_in(jax.random.fold_in(stream_key, 6), dim), (blocks,), jnp.float32, low / len(cuts), top_value / len(cuts))
        return jnp.repeat(jnp.exp(draws), extent[dim] // blocks).reshape((-1,) + (1,) * (len(extent) - dim - 1))

    loudness = one(*cuts[0])
    for cut in cuts[1:]:
        loudness = loudness * one(*cut)
    return loudness


def deal_out(rng, own, number, rows, amount, top, reach, lean):
    sequence = jax.random.permutation(rng, amount)
    packed, usual = load_shares(amount, rows * top, reach, lean, True), load_shares(amount, rows * top, reach, lean, False)
    places = jnp.arange(amount)

    def named(sizes, turn):
        used = int((sizes > 0).sum())
        fixed = max(1, used // 4)
        shifted = fixed + (places - fixed + turn * (used - fixed)) % max(1, amount - fixed)
        return jnp.zeros((amount,), jnp.int32).at[sequence[jnp.where(places < fixed, places, shifted)]].set(jnp.asarray(sizes, jnp.int32))

    sizes = jnp.where(number % 4 == 0, named(packed, number // 4), named(usual, number - number // 4 - 1))
    mixed = jax.random.permutation(jax.random.fold_in(own, 3), amount)
    donor, taker = mixed[0:amount // 2 * 2:2], mixed[1:amount // 2 * 2:2]
    room = jnp.minimum(sizes[donor] - 1, reach - sizes[taker]) // 2
    room = jnp.where((donor == sequence[0]) | (taker == sequence[0]) | (sizes[taker] == 0), 0, jnp.maximum(room, 0))
    shifted = jax.random.randint(jax.random.fold_in(own, 4), (amount // 2,), 0, 1 << 20) % (room + 1)
    sizes = sizes.at[donor].add(-shifted).at[taker].add(shifted)
    labels = jnp.searchsorted(jnp.cumsum(sizes), jnp.arange(rows * top), side="right").astype(jnp.int32)
    grid = labels.reshape(top, rows).T
    grid = grid[jax.random.permutation(jax.random.fold_in(own, 1), rows)]
    turn = jax.random.randint(jax.random.fold_in(own, 2), (rows, 1), 0, top)
    return jnp.take_along_axis(grid, (jnp.arange(top)[None, :] + turn) % top, axis=1)


def load_shares(amount, total, reach, slope, full):
    loads = [(1 << 20) // math.isqrt(rank ** slope) + 1 for rank in range(1, amount + 1)]
    largest = reach if full else min(reach, max(-(-total // amount), total * loads[0] // sum(loads)))
    least = 1 if total - largest >= amount - 1 else 0
    holding, spare = [largest] + [least] * (amount - 1), total - largest - least * (amount - 1)
    while spare > 0:
        candidates = [i for i in range(1, amount) if holding[i] < largest] or [i for i in range(1, amount) if holding[i] < reach]
        pool, left = sum([loads[i] for i in candidates]), spare
        for i in candidates:
            addition = min(reach - holding[i], max(1, left * loads[i] // pool), spare)
            holding[i] = holding[i] + addition
            spare = spare - addition
    return np.array(holding)


def normal_values(key, extent, scale, reach, cuts=(), held_as=jnp.bfloat16):
    loudness = level_of(key, extent, cuts, -0.22, 0.18) if cuts else 1.0
    entries = jax.random.normal(key, extent, jnp.float32) * scale * loudness
    return jnp.minimum(jnp.maximum(entries, -reach), reach).astype(held_as)


def setup_inputs(seed: int = 0) -> dict:
    key_of = jax.random.split(jax.random.key(seed), 16)
    inputs = normal_values(key_of[0], (TOKENS, D), 1.0, 6.0, ((0, 32),), jnp.float32)
    cotangent = normal_values(key_of[1], (TOKENS, D), 1.0, 6.0, ((0, 32),), jnp.float32)
    norm_one = jnp.clip(1.0 + 0.1 * jax.random.normal(key_of[2], (D,), jnp.float32), 0.5, 1.5).astype(jnp.bfloat16)
    qkv_weight = normal_values(key_of[3], (D, 3 * D), D ** -0.5, 0.21875, ((0, 4),))
    out_weight = normal_values(key_of[4], (D, D), (max(1, 2 * D // TOK_DEV)) ** -0.5, 3.5, ((0, 4),))
    norm_two = jnp.clip(1.0 + 0.1 * jax.random.normal(key_of[5], (D,), jnp.float32), 0.5, 1.5).astype(jnp.bfloat16)
    shared_gate = normal_values(key_of[6], (D, FF), D ** -0.5, 0.21875, ((1, 4),))
    shared_up = normal_values(key_of[7], (D, FF), D ** -0.5, 0.21875, ((1, 4),))
    shared_down = normal_values(key_of[8], (FF, D), FF ** -0.5, 0.125, ((0, 4),))
    expert_gate = normal_values(key_of[9], (EXPERTS, D, EFF), D ** -0.5, 0.21875, ((0, 8),))
    expert_up = normal_values(key_of[10], (EXPERTS, D, EFF), D ** -0.5, 0.21875, ((0, 8),))
    expert_down = normal_values(key_of[11], (EXPERTS, EFF, D), EFF ** -0.5, 0.125, ((0, 8),))
    gate_weights = jnp.clip(0.25 + 0.75 * jax.random.uniform(key_of[12], (TOKENS, TOP), jnp.float32) ** level_of(key_of[12], (TOKENS, TOP), ((0, 32),), -0.2, 0.2), 0.25, 1.0)
    routes_keys = jax.random.split(jax.random.fold_in(key_of[13], 1), TOKENS // TOK_DEV)
    routes_turns = jax.random.permutation(jax.random.fold_in(key_of[13], 3), TOKENS // TOK_DEV)
    routes = jax.vmap(lambda own, number: deal_out(jax.random.fold_in(key_of[13], 2), own, number, TOK_DEV, EXPERTS, TOP, CAP, 2))(routes_keys, routes_turns).reshape((TOKENS, TOP))
    prefix = place_ends(jax.random.randint(key_of[14], (SEQS,), TOK_DEV // 10, TOK_DEV // 2 + 1), jax.random.fold_in(key_of[14], 1), TOK_DEV // 10, (TOK_DEV // 2 + 1) - 1).astype(jnp.int32)
    return {"inputs": inputs, "cotangent": cotangent, "norm_one": norm_one, "qkv_weight": qkv_weight, "out_weight": out_weight, "norm_two": norm_two, "shared_gate": shared_gate, "shared_up": shared_up, "shared_down": shared_down, "expert_gate": expert_gate, "expert_up": expert_up, "expert_down": expert_down, "gate_weights": gate_weights, "routes": routes, "prefix": prefix}


@jax.custom_vjp
def low(v):
    return lax.optimization_barrier(v.astype(jnp.bfloat16)).astype(jnp.float32)

@jax.custom_vjp
def low_back(v):
    return v

def low_keep(v):
    return (low(v), None)

def low_pass(kept, grad):
    return (grad,)

def back_keep(v):
    return (v, None)

def back_low(kept, grad):
    return (low(grad),)
low.defvjp(low_keep, low_pass)
low_back.defvjp(back_keep, back_low)
EPS = 1e-06
PRECISE = lax.Precision.HIGHEST

def matmul(left, right):
    return jnp.dot(left, right, precision=PRECISE)

def rms_scale(source, gain):
    return source * lax.rsqrt(lax.optimization_barrier(jnp.mean(source * source, axis=-1, keepdims=True)) + EPS) * gain

def rope_tables(length):
    half_dim = HEAD_DIM // 2
    frequency = 10000.0 ** (-jnp.arange(half_dim, dtype=jnp.float32) * 2.0 / HEAD_DIM)
    angles = jnp.arange(length, dtype=jnp.float32)[:, None] * frequency[None, :]
    return (jnp.cos(angles)[:, None, :], jnp.sin(angles)[:, None, :])

def rotate(vectors, cosine_table, sine_table):
    half_dim = vectors.shape[-1] // 2
    first_half = vectors[..., :half_dim]
    second = vectors[..., half_dim:]
    return jnp.concatenate([first_half * cosine_table - second * sine_table, second * cosine_table + first_half * sine_table], axis=-1)

def attend_sequence(normed, qkv_weight, out_weight, prefix_len, cosine_table, sine_table):
    length = normed.shape[0]
    projected = low_back(matmul(normed, qkv_weight))
    head_shape = (length, HEADS, HEAD_DIM)
    queries = low(rotate(projected[:, :D].reshape(head_shape), cosine_table, sine_table))
    key_rows = low(rotate(projected[:, D:2 * D].reshape(head_shape), cosine_table, sine_table))
    value_rows = low(projected[:, 2 * D:].reshape(head_shape))
    scores = low_back(jnp.einsum('qhd,khd->hqk', queries, key_rows, precision=PRECISE) * HEAD_DIM ** (-0.5))
    row_pos = jnp.arange(length, dtype=jnp.int32)[:, None]
    col_pos = jnp.arange(length, dtype=jnp.int32)[None, :]
    visible = (col_pos < prefix_len) | (col_pos <= row_pos)
    scores = jnp.where(visible[None], scores, -1e+30)
    probs = low(jax.nn.softmax(scores, axis=-1))
    attended = jnp.einsum('hqk,khd->qhd', probs, value_rows, precision=PRECISE).reshape(length, D)
    attended = low(low_back(attended))
    return low_back(matmul(attended, out_weight))

def route_tables(routes):
    flat_route = routes.reshape(SEQS, TOK_DEV * TOP)
    onehot = (flat_route[:, :, None] == jnp.arange(EXPERTS, dtype=jnp.int32)[None, None, :]).astype(jnp.int32)
    slot_index = lax.optimization_barrier(jnp.sum((jnp.cumsum(onehot, axis=1) - onehot) * onehot, axis=2))
    device_index = jnp.arange(SEQS, dtype=jnp.int32)[:, None]
    position = ((flat_route * SEQS + device_index) * CAP + slot_index).reshape(-1).astype(jnp.int32)
    copies = TOKENS * TOP
    source = jnp.full((EXPERTS * SEQS * CAP,), copies, jnp.int32).at[position].set(jnp.arange(copies, dtype=jnp.int32))
    return (position, source)

def expert_forward(pieces):
    row_block, gate_w, up_w, down_w = pieces
    pre_gate = low_back(matmul(row_block, gate_w))
    pre_up = low_back(matmul(row_block, up_w))
    hidden = low(jax.nn.silu(pre_gate) * pre_up)
    return low(low_back(matmul(hidden, down_w)))

def layer_forward(inputs, norm_one, qkv_weight, out_weight, norm_two, shared_gate, shared_up, shared_down, expert_gate, expert_up, expert_down, gate_weights, routes, prefix):
    cosine_table, sine_table = rope_tables(TOK_DEV)
    group_size = math.gcd(SEQS, max(1, 4096 // TOK_DEV))
    blocks = SEQS // group_size

    def attention_block(carry, pieces):
        block_inputs, block_prefix = pieces
        normed = low(rms_scale(block_inputs, norm_one))

        def one_sequence(seq_rows, seq_prefix):
            return attend_sequence(seq_rows, qkv_weight, out_weight, seq_prefix, cosine_table, sine_table)
        return (carry, block_inputs + jax.vmap(one_sequence)(normed, block_prefix))
    unused, resid = lax.scan(jax.checkpoint(attention_block), None, (inputs.reshape(blocks, group_size, TOK_DEV, D), prefix.reshape(blocks, group_size)))
    resid = resid.reshape(TOKENS, D)
    normed_two = low(rms_scale(resid, norm_two))
    shared_pre = low_back(matmul(normed_two, shared_gate))
    shared_lift = low_back(matmul(normed_two, shared_up))
    shared_hidden = low(jax.nn.silu(shared_pre) * shared_lift)
    shared_out = low_back(matmul(shared_hidden, shared_down))
    position, source = route_tables(routes)
    copy_rows = low_back(jnp.repeat(normed_two, TOP, axis=0))
    padded = jnp.concatenate([copy_rows, jnp.zeros((1, D), jnp.float32)], axis=0)
    buckets = padded[source].reshape(EXPERTS, SEQS * CAP, D)
    results = lax.map(jax.checkpoint(expert_forward), (buckets, expert_gate, expert_up, expert_down))
    picked = results.reshape(EXPERTS * SEQS * CAP, D)[position].reshape(TOKENS, TOP, D)
    mixture = lax.optimization_barrier(jnp.sum(gate_weights[:, :, None] * picked, axis=1))
    return resid + mixture + shared_out

def reference(inputs, cotangent, norm_one, qkv_weight, out_weight, norm_two, shared_gate, shared_up, shared_down, expert_gate, expert_up, expert_down, gate_weights, routes, prefix):
    forward = partial(layer_forward, routes=routes, prefix=prefix)
    output, pullback = jax.vjp(forward, inputs.astype(jnp.float32), norm_one.astype(jnp.float32), qkv_weight.astype(jnp.float32), out_weight.astype(jnp.float32), norm_two.astype(jnp.float32), shared_gate.astype(jnp.float32), shared_up.astype(jnp.float32), shared_down.astype(jnp.float32), expert_gate.astype(jnp.float32), expert_up.astype(jnp.float32), expert_down.astype(jnp.float32), gate_weights.astype(jnp.float32))
    grads = pullback(cotangent.astype(jnp.float32))
    return (output, grads[0], grads[1], grads[2], grads[3], grads[4], grads[5], grads[6], grads[7], grads[8], grads[9], grads[10], grads[11])
```

```python
import functools

import jax
import jax.numpy as jnp
from jax import lax
from jax.experimental import pallas as pl
from jax.experimental.pallas import tpu as pltpu
from jax.sharding import PartitionSpec as P

HEADS = 12
HEAD_DIM = 64
TOP = 2
EPS = 1e-06
MESH = pl.DeviceIdType.MESH
F32 = jnp.float32
BF16 = jnp.bfloat16


def rope_tables(length):
    half_dim = HEAD_DIM // 2
    frequency = 10000.0 ** (-jnp.arange(half_dim, dtype=jnp.float32) * 2.0 / HEAD_DIM)
    angles = jnp.arange(length, dtype=jnp.float32)[:, None] * frequency[None, :]
    return (jnp.cos(angles)[:, None, :], jnp.sin(angles)[:, None, :])


def rotate(vectors, cosine_table, sine_table):
    half_dim = vectors.shape[-1] // 2
    first_half = vectors[..., :half_dim]
    second = vectors[..., half_dim:]
    return jnp.concatenate(
        [
            first_half * cosine_table - second * sine_table,
            second * cosine_table + first_half * sine_table,
        ],
        axis=-1,
    )


def gated_unit(pre_gate):
    sigmoid_value = jax.nn.sigmoid(pre_gate)
    activated = pre_gate * sigmoid_value
    derivative = sigmoid_value * (1.0 + pre_gate * (1.0 - sigmoid_value))
    return (activated, derivative)


def norm_back(source, inverse, gain, grad_in):
    scaled = grad_in * gain
    gain_grad = jnp.sum(grad_in * source * inverse, axis=0)
    input_part = inverse * scaled - source * inverse**3 * jnp.mean(
        scaled * source, axis=-1, keepdims=True
    )
    return (gain_grad, input_part)


def matmul(left, right):
    return jnp.dot(left, right, preferred_element_type=jnp.float32)


def place():
    expert, shard = lax.axis_index("expert"), lax.axis_index("shard")
    core, x, y = expert % 2, shard % 2, shard // 2
    return dict(
        expert=expert,
        shard=shard,
        core=core,
        z=expert // 2,
        sx=2 * y + 1 - x,
        sy=2 * (1 - y) + x,
        sd=2 * (1 - y) + 1 - x,
        dev_x=(expert, 2 * y + 1 - x),
        dev_y=(expert, 2 * (1 - y) + x),
        dev_c=(expert + 1 - 2 * core, shard),
    )


def meet(devices):
    barrier = pltpu.get_barrier_semaphore()
    for device in devices:
        pl.semaphore_signal(barrier, inc=1, device_id=device, device_id_type=MESH)
    pl.semaphore_wait(barrier, len(devices))


def remote(src, dst, send, recv, device):
    return pltpu.make_async_remote_copy(
        src_ref=src, dst_ref=dst, send_sem=send, recv_sem=recv, device_id=device, device_id_type=MESH
    )


class PlaneGather:
    COPIES = 7

    def __init__(self, src, dst, axis, send, recv, local, at):
        self.src, self.dst, self.axis, self.at = src, dst, axis, at
        self.send, self.recv, self.local = send, recv, local
        self.rows, self.cols = src.shape
        self.copies = []

    def view(self, shard, start, count):
        if self.axis == 0:
            return self.dst.at[pl.ds(pl.multiple_of(shard * self.rows + start, 16), count), :]
        return self.dst.at[
            pl.ds(pl.multiple_of(start, 16), count),
            pl.ds(pl.multiple_of(shard * self.cols, 128), self.cols),
        ]

    def copy(self, src, dst, index, device):
        made = remote(src, dst, self.send.at[index], self.recv.at[index], device)
        made.start()
        self.copies.append(made)

    def first(self):
        at, half = self.at, self.rows // 2
        src = self.src.at[pl.ds(pl.multiple_of(at["core"] * half, 16), half), :]
        dst = self.view(at["shard"], at["core"] * half, half)
        self.copy(src, dst, 0, at["dev_x"])
        self.copy(src, dst, 1, at["dev_y"])
        self.own = pltpu.make_async_copy(self.src, self.view(at["shard"], 0, self.rows), self.local)
        self.own.start()

    def second(self):
        at, half, quarter = self.at, self.rows // 2, self.rows // 4
        start = at["core"] * half
        self.copies[0].wait_recv()
        part = self.view(at["sx"], start, quarter)
        self.copy(part, part, 2, at["dev_y"])
        part = self.view(at["sx"], start, half)
        self.copy(part, part, 3, at["dev_c"])
        self.copies[1].wait_recv()
        part = self.view(at["sy"], start + quarter, quarter)
        self.copy(part, part, 4, at["dev_x"])
        part = self.view(at["sy"], start, half)
        self.copy(part, part, 5, at["dev_c"])

    def third(self):
        at, half = self.at, self.rows // 2
        self.copies[2].wait_recv()
        self.copies[4].wait_recv()
        part = self.view(at["sd"], at["core"] * half, half)
        self.copy(part, part, 6, at["dev_c"])

    def finish(self):
        for index in (3, 5, 6):
            self.copies[index].wait_recv()
        for made in self.copies:
            made.wait_send()
        self.own.wait()


def plane_gather_kernel(*refs, axes):
    count = len(axes)
    send, recv, local = refs[2 * count :]
    at = place()
    meet([at["dev_x"], at["dev_y"], at["dev_c"]])
    gathers = [
        PlaneGather(refs[k], refs[count + k], axes[k], send.at[k], recv.at[k], local.at[k], at)
        for k in range(count)
    ]
    for step in ("first", "second", "third", "finish"):
        for gather in gathers:
            getattr(gather, step)()


def plane_gather(arrays, axes, ident):
    if lax.axis_size("shard") != 4:
        return [lax.all_gather(v, "shard", axis=a, tiled=True) for v, a in zip(arrays, axes)]
    count = len(arrays)
    shapes = []
    for array, axis in zip(arrays, axes):
        shape = list(array.shape)
        shape[axis] *= 4
        shapes.append(jax.ShapeDtypeStruct(tuple(shape), array.dtype))
    return pl.pallas_call(
        functools.partial(plane_gather_kernel, axes=axes),
        out_shape=shapes,
        in_specs=[pl.BlockSpec(memory_space=pl.ANY)] * count,
        out_specs=[pl.BlockSpec(memory_space=pl.ANY)] * count,
        scratch_shapes=[
            pltpu.SemaphoreType.DMA((count, PlaneGather.COPIES)),
            pltpu.SemaphoreType.DMA((count, PlaneGather.COPIES)),
            pltpu.SemaphoreType.DMA((count,)),
        ],
        compiler_params=pltpu.CompilerParams(
            collective_id=ident, has_side_effects=True, vmem_limit_bytes=32 << 20
        ),
    )(*arrays)


class PlaneReduce:
    COPIES = 4

    def __init__(self, src, dst, mine, got, hold, last, send, recv, local, at):
        self.src, self.dst, self.mine, self.got, self.hold, self.last = src, dst, mine, got, hold, last
        self.send, self.recv, self.local, self.at = send, recv, local, at
        self.half = src.shape[1] // 2

    @staticmethod
    def scratch(shape):
        half = shape[1] // 2
        return [
            pltpu.VMEM((4, half, shape[2]), BF16),
            pltpu.VMEM((4, half, shape[2]), BF16),
            pltpu.VMEM((2, half, shape[2]), BF16),
            pltpu.VMEM((2, half, shape[2]), BF16),
        ]

    def first(self):
        at, half = self.at, self.half
        upper, lower = pl.ds(0, half), pl.ds(half, half)
        plan = [
            (at["sx"], upper, at["dev_x"], 0),
            (at["sd"], upper, at["dev_x"], 1),
            (at["sy"], lower, at["dev_y"], 2),
            (at["sd"], lower, at["dev_y"], 3),
        ]
        self.out = []
        for shard, rows, device, slot in plan:
            made = remote(
                self.src.at[shard, rows, :], self.got.at[slot], self.send.at[slot], self.recv.at[slot], device
            )
            made.start()
            self.out.append(made)
        self.near = []
        for slot, (shard, rows) in enumerate(
            [(at["shard"], upper), (at["sy"], upper), (at["shard"], lower), (at["sx"], lower)]
        ):
            made = pltpu.make_async_copy(self.src.at[shard, rows, :], self.mine.at[slot], self.local.at[slot])
            made.start()
            self.near.append(made)

    def second(self):
        at = self.at
        for slot in (1, 3):
            self.near[slot].wait()
            self.out[slot].wait_recv()
            self.hold[slot // 2] = (
                self.mine[slot].astype(F32) + self.got[slot].astype(F32)
            ).astype(BF16)
            made = remote(
                self.hold.at[slot // 2],
                self.last.at[slot // 2],
                self.send.at[4 + slot // 2],
                self.recv.at[4 + slot // 2],
                at["dev_y"] if slot == 1 else at["dev_x"],
            )
            made.start()
            self.out.append(made)

    def third(self):
        half = self.half
        for slot in (0, 2):
            self.near[slot].wait()
            self.out[slot].wait_recv()
            self.out[4 + slot // 2].wait_recv()
            self.dst[pl.ds(slot // 2 * half, half), :] = (
                self.mine[slot].astype(F32) + self.got[slot].astype(F32)
            ) + self.last[slot // 2].astype(F32)

    def finish(self):
        for made in self.out:
            made.wait_send()


def plane_reduce_kernel(*refs, count):
    scratch = refs[2 * count :]
    send, recv, local = scratch[4 * count :]
    at = place()
    meet([at["dev_x"], at["dev_y"]])
    reduces = [
        PlaneReduce(
            refs[k], refs[count + k], *scratch[4 * k : 4 * k + 4], send.at[k], recv.at[k], local.at[k], at
        )
        for k in range(count)
    ]
    for step in ("first", "second", "third", "finish"):
        for reduce in reduces:
            getattr(reduce, step)()


def plane_reduce(arrays, ident):
    if lax.axis_size("shard") != 4:
        return [
            lax.psum_scatter(v, "shard", scatter_dimension=0, tiled=True)[0].astype(F32) for v in arrays
        ]
    count = len(arrays)
    scratch = []
    for array in arrays:
        scratch += PlaneReduce.scratch(array.shape)
    return pl.pallas_call(
        functools.partial(plane_reduce_kernel, count=count),
        out_shape=[jax.ShapeDtypeStruct(v.shape[1:], F32) for v in arrays],
        in_specs=[pl.BlockSpec(memory_space=pl.ANY)] * count,
        out_specs=[pl.BlockSpec(memory_space=pltpu.VMEM)] * count,
        scratch_shapes=scratch
        + [
            pltpu.SemaphoreType.DMA((count, 6)),
            pltpu.SemaphoreType.DMA((count, 6)),
            pltpu.SemaphoreType.DMA((count, 4)),
        ],
        compiler_params=pltpu.CompilerParams(
            collective_id=ident, has_side_effects=True, vmem_limit_bytes=48 << 20
        ),
    )(*arrays)


def on_device(
    inputs,
    cotangent,
    norm_one,
    qkv_weight,
    out_weight,
    norm_two,
    shared_gate,
    shared_up,
    shared_down,
    expert_gate,
    expert_up,
    expert_down,
    gate_weights,
    routes,
    prefix,
):
    length, model_width = inputs.shape
    experts = lax.axis_size("expert") * expert_gate.shape[0]
    shards = lax.axis_size("shard")
    me = lax.axis_index("expert")
    out_low = cotangent.astype(BF16)
    cot_all = lax.all_gather(out_low, "expert", axis=0)

    capacity = 4 * length // experts
    copies = length * TOP
    flat_route = routes.reshape(copies)
    onehot = (flat_route[:, None] == jnp.arange(experts, dtype=jnp.int32)[None, :]).astype(jnp.int32)
    before = (jnp.cumsum(onehot, axis=0) - onehot).reshape(length, TOP, experts)
    onehot = onehot.reshape(length, TOP, experts)
    slot = jnp.sum(onehot * (before + 1), axis=1) - 1
    weight = jnp.sum(onehot.astype(F32) * gate_weights[:, :, None], axis=1)
    table = jnp.stack([slot.astype(F32).T, weight.T], axis=0)
    table_all = lax.all_gather(table, "expert", axis=0)
    table_mine = lax.dynamic_index_in_dim(table_all, me, axis=2, keepdims=False)

    gains = jnp.concatenate(
        [jnp.broadcast_to(norm_one, (32, norm_one.shape[0])), jnp.broadcast_to(norm_two, (32, norm_two.shape[0]))],
        axis=0,
    )
    qkv_full, out_full, gains_full = plane_gather([qkv_weight, out_weight, gains], (0, 0, 0), 1)
    gate_full, up_full, down_full = plane_gather([shared_gate, shared_up, shared_down], (1, 1, 0), 2)
    gains_full = gains_full.reshape(shards, 64, -1).astype(F32)
    gain_one = gains_full[:, 0, :].reshape(model_width)
    gain_two = gains_full[:, 32, :].reshape(model_width)

    inverse_one = lax.rsqrt(jnp.mean(inputs * inputs, axis=-1, keepdims=True) + EPS)
    normed_one = (inputs * inverse_one * gain_one).astype(BF16)
    projected = matmul(normed_one, qkv_full)
    cosine_table, sine_table = rope_tables(length)
    head_shape = (length, HEADS, HEAD_DIM)
    queries = rotate(
        projected[:, :model_width].reshape(head_shape), cosine_table, sine_table
    ).astype(BF16)
    key_rows = rotate(
        projected[:, model_width : 2 * model_width].reshape(head_shape), cosine_table, sine_table
    ).astype(BF16)
    value_rows = projected[:, 2 * model_width :].reshape(head_shape).astype(BF16)
    score_scale = HEAD_DIM ** (-0.5)
    row_pos = lax.broadcasted_iota(jnp.int32, (length, length), 0)
    col_pos = lax.broadcasted_iota(jnp.int32, (length, length), 1)
    visible = (col_pos < prefix[0]) | (col_pos <= row_pos)

    def masked_scores():
        raw_scores = (
            jnp.einsum("qhd,khd->hqk", queries, key_rows, preferred_element_type=F32) * score_scale
        )
        return jnp.where(visible[None], raw_scores, -1e30)

    scores = masked_scores()
    row_peak = jnp.max(scores, axis=-1, keepdims=True)
    exponent = jnp.exp(scores - row_peak)
    expsum = jnp.sum(exponent, axis=-1, keepdims=True)
    logsum = row_peak + jnp.log(expsum)
    probs_low = (exponent / expsum).astype(BF16)
    attended = (
        jnp.einsum("hqk,khd->qhd", probs_low, value_rows, preferred_element_type=F32)
        .reshape(length, model_width)
        .astype(BF16)
    )
    resid = inputs + matmul(attended, out_full)
    inverse_two = lax.rsqrt(jnp.mean(resid * resid, axis=-1, keepdims=True) + EPS)
    normed_two = (resid * inverse_two * gain_two).astype(BF16)
    normed_all = lax.all_gather(normed_two, "expert", axis=0)

    shared_pre = matmul(normed_two, gate_full)
    shared_lift = matmul(normed_two, up_full)
    shared_act, shared_slope = gated_unit(shared_pre)
    shared_hidden = (shared_act * shared_lift).astype(BF16)
    shared_out = matmul(shared_hidden, down_full)
    shared_down_grad = matmul(shared_hidden.T, out_low)
    shared_hgrad = matmul(out_low, down_full.T)
    shared_pre_grad = (shared_hgrad * shared_lift * shared_slope).astype(BF16)
    shared_lift_grad = (shared_hgrad * shared_act).astype(BF16)
    shared_gate_grad = matmul(normed_two.T, shared_pre_grad)
    shared_up_grad = matmul(normed_two.T, shared_lift_grad)
    shared_back = matmul(shared_pre_grad, gate_full.T) + matmul(shared_lift_grad, up_full.T)

    pick = (
        jnp.arange(capacity, dtype=F32)[None, :, None] == table_mine[:, 0][:, None, :]
    ).astype(BF16)
    weight_rows = jnp.sum(pick.astype(F32) * table_mine[:, 1][:, None, :], axis=2)

    def to_rows(values):
        return jnp.einsum("ect,etd->ecd", pick, values, preferred_element_type=F32)

    def to_tokens(rows):
        return jnp.einsum("ect,ecd->etd", pick, rows, preferred_element_type=F32)

    gate_local, up_local, down_local = expert_gate[0], expert_up[0], expert_down[0]
    row_count = experts * capacity
    rows = to_rows(normed_all).astype(BF16).reshape(row_count, model_width)
    cot_rows = to_rows(cot_all)
    grad_rows = (cot_rows * weight_rows[:, :, None]).astype(BF16).reshape(row_count, model_width)
    pre_gate = matmul(rows, gate_local)
    pre_up = matmul(rows, up_local)
    activated, derivative = gated_unit(pre_gate)
    hidden = (activated * pre_up).astype(BF16)
    hidden_grad = matmul(grad_rows, down_local.T)
    gate_pre_grad = (hidden_grad * pre_up * derivative).astype(BF16)
    up_pre_grad = (hidden_grad * activated).astype(BF16)
    row_grad = (matmul(gate_pre_grad, gate_local.T) + matmul(up_pre_grad, up_local.T)).astype(BF16)
    back_part = to_tokens(row_grad.reshape(experts, capacity, model_width)).astype(BF16)
    back = lax.psum_scatter(back_part, "expert", scatter_dimension=0, tiled=False).astype(F32)

    result = matmul(hidden, down_local).astype(BF16).reshape(experts, capacity, model_width)
    weighted = (result.astype(F32) * weight_rows[:, :, None]).astype(BF16)
    mix_part = to_tokens(weighted).astype(BF16)
    mixture = lax.psum_scatter(mix_part, "expert", scatter_dimension=0, tiled=False).astype(F32)
    weight_dot = jnp.sum(result.astype(F32) * cot_rows, axis=2)
    weight_back = jnp.einsum("ect,ec->et", pick.astype(F32), weight_dot, precision=lax.Precision.HIGHEST)
    weight_got = lax.all_to_all(weight_back, "expert", split_axis=0, concat_axis=0, tiled=True)
    gate_weights_grad = jnp.sum(onehot.astype(F32) * weight_got.T[:, None, :], axis=2)

    def blocks_of_columns(value):
        width = value.shape[1] // shards
        return value.astype(BF16).reshape(value.shape[0], shards, width).transpose(1, 0, 2)

    def blocks_of_rows(value):
        return value.astype(BF16).reshape(shards, value.shape[0] // shards, value.shape[1])

    gate_term = matmul(rows.T, gate_pre_grad)
    up_term = matmul(rows.T, up_pre_grad)
    down_term = matmul(hidden.T, grad_rows)
    expert_gate_grad, expert_up_grad, expert_down_grad = plane_reduce(
        [blocks_of_columns(gate_term), blocks_of_columns(up_term), blocks_of_rows(down_term)], 3
    )

    output = resid + mixture + shared_out
    normed_two_grad = shared_back + back
    gain_two_grad, resid_extra = norm_back(resid, inverse_two, gain_two, normed_two_grad)
    resid_grad = cotangent + resid_extra
    attn_low = resid_grad.astype(BF16)
    out_weight_grad = matmul(attended.T, attn_low)
    attended_grad = matmul(attn_low, out_full.T).astype(BF16).reshape(head_shape)
    scores = masked_scores()
    probs_full = jnp.exp(scores - logsum)
    value_grad = jnp.einsum(
        "hqk,qhd->khd", probs_full.astype(BF16), attended_grad, preferred_element_type=F32
    )
    probs_grad = jnp.einsum("qhd,khd->hqk", attended_grad, value_rows, preferred_element_type=F32)
    score_grad = (
        probs_full * (probs_grad - jnp.sum(probs_full * probs_grad, axis=-1, keepdims=True))
    ).astype(BF16)
    query_grad = (
        jnp.einsum("hqk,khd->qhd", score_grad, key_rows, preferred_element_type=F32) * score_scale
    )
    key_grad = (
        jnp.einsum("hqk,qhd->khd", score_grad, queries, preferred_element_type=F32) * score_scale
    )
    projected_grad = jnp.concatenate(
        [
            rotate(query_grad, cosine_table, -sine_table).reshape(length, model_width),
            rotate(key_grad, cosine_table, -sine_table).reshape(length, model_width),
            value_grad.reshape(length, model_width),
        ],
        axis=1,
    ).astype(BF16)
    qkv_weight_grad = matmul(normed_one.T, projected_grad)
    normed_one_grad = matmul(projected_grad, qkv_full.T)
    gain_one_grad, input_extra = norm_back(inputs, inverse_one, gain_one, normed_one_grad)
    input_grad = resid_grad + input_extra

    gain_block = jnp.zeros((shards, 32, model_width // shards), BF16)
    gain_block = gain_block.at[:, 0, :].set(gain_one_grad.astype(BF16).reshape(shards, -1))
    gain_block = gain_block.at[:, 1, :].set(gain_two_grad.astype(BF16).reshape(shards, -1))
    pieces = plane_reduce(
        [
            blocks_of_rows(qkv_weight_grad),
            blocks_of_rows(out_weight_grad),
            gain_block,
            blocks_of_columns(shared_gate_grad),
            blocks_of_columns(shared_up_grad),
            blocks_of_rows(shared_down_grad),
        ],
        4,
    )
    summed = [lax.psum(v.astype(BF16), "expert").astype(F32) for v in pieces]
    return (
        output,
        input_grad,
        summed[2][0],
        summed[0],
        summed[1],
        summed[2][1],
        summed[3],
        summed[4],
        summed[5],
        expert_gate_grad[None],
        expert_up_grad[None],
        expert_down_grad[None],
        gate_weights_grad,
    )


def solution(mesh):
    tokens = P(("expert", "shard"), None)
    in_specs = (
        tokens,
        tokens,
        P("shard"),
        P("shard", None),
        P("shard", None),
        P("shard"),
        P(None, "shard"),
        P(None, "shard"),
        P("shard", None),
        P("expert", None, None),
        P("expert", None, None),
        P("expert", None, None),
        tokens,
        tokens,
        P(("expert", "shard")),
    )
    out_specs = (
        tokens,
        tokens,
        P("shard"),
        P("shard", None),
        P("shard", None),
        P("shard"),
        P(None, "shard"),
        P(None, "shard"),
        P("shard", None),
        P("expert", None, "shard"),
        P("expert", None, "shard"),
        P("expert", "shard", None),
        tokens,
    )
    return jax.shard_map(
        on_device, mesh=mesh, in_specs=in_specs, out_specs=out_specs, check_vma=False
    )
```

```python
import functools

import jax
import jax.numpy as jnp
from jax import lax
from jax.experimental import pallas as pl
from jax.experimental.pallas import tpu as pltpu
from jax.sharding import PartitionSpec as P

HEADS = 12
HEAD_DIM = 64
TOP = 2
EPS = 1e-06
MESH = pl.DeviceIdType.MESH
F32 = jnp.float32
BF16 = jnp.bfloat16


def rope_tables(length):
    half_dim = HEAD_DIM // 2
    frequency = 10000.0 ** (-jnp.arange(half_dim, dtype=jnp.float32) * 2.0 / HEAD_DIM)
    angles = jnp.arange(length, dtype=jnp.float32)[:, None] * frequency[None, :]
    return (jnp.cos(angles)[:, None, :], jnp.sin(angles)[:, None, :])


def rotate(vectors, cosine_table, sine_table):
    half_dim = vectors.shape[-1] // 2
    first_half = vectors[..., :half_dim]
    second = vectors[..., half_dim:]
    return jnp.concatenate(
        [
            first_half * cosine_table - second * sine_table,
            second * cosine_table + first_half * sine_table,
        ],
        axis=-1,
    )


def gated_unit(pre_gate):
    sigmoid_value = jax.nn.sigmoid(pre_gate)
    activated = pre_gate * sigmoid_value
    derivative = sigmoid_value * (1.0 + pre_gate * (1.0 - sigmoid_value))
    return (activated, derivative)


def norm_back(source, inverse, gain, grad_in):
    scaled = grad_in * gain
    gain_grad = jnp.sum(grad_in * source * inverse, axis=0)
    input_part = inverse * scaled - source * inverse**3 * jnp.mean(
        scaled * source, axis=-1, keepdims=True
    )
    return (gain_grad, input_part)


def matmul(left, right):
    return jnp.dot(left, right, preferred_element_type=jnp.float32)


def place():
    expert, shard = lax.axis_index("expert"), lax.axis_index("shard")
    core, x, y = expert % 2, shard % 2, shard // 2
    return dict(
        expert=expert,
        shard=shard,
        core=core,
        z=expert // 2,
        sx=2 * y + 1 - x,
        sy=2 * (1 - y) + x,
        sd=2 * (1 - y) + 1 - x,
        dev_x=(expert, 2 * y + 1 - x),
        dev_y=(expert, 2 * (1 - y) + x),
        dev_c=(expert + 1 - 2 * core, shard),
        dev_left=(expert - 2, shard),
        dev_right=(expert + 2, shard),
    )


def meet(devices):
    barrier = pltpu.get_barrier_semaphore()
    for device in devices:
        pl.semaphore_signal(barrier, inc=1, device_id=device, device_id_type=MESH)
    pl.semaphore_wait(barrier, len(devices))


def remote(src, dst, send, recv, device):
    return pltpu.make_async_remote_copy(
        src_ref=src, dst_ref=dst, send_sem=send, recv_sem=recv, device_id=device, device_id_type=MESH
    )


class PlaneGather:
    COPIES = 7

    def __init__(self, src, dst, axis, send, recv, local, at):
        self.src, self.dst, self.axis, self.at = src, dst, axis, at
        self.send, self.recv, self.local = send, recv, local
        self.rows, self.cols = src.shape
        self.copies = []

    def view(self, shard, start, count):
        if self.axis == 0:
            return self.dst.at[pl.ds(pl.multiple_of(shard * self.rows + start, 16), count), :]
        return self.dst.at[
            pl.ds(pl.multiple_of(start, 16), count),
            pl.ds(pl.multiple_of(shard * self.cols, 128), self.cols),
        ]

    def copy(self, src, dst, index, device):
        made = remote(src, dst, self.send.at[index], self.recv.at[index], device)
        made.start()
        self.copies.append(made)

    def first(self):
        at, half = self.at, self.rows // 2
        src = self.src.at[pl.ds(pl.multiple_of(at["core"] * half, 16), half), :]
        dst = self.view(at["shard"], at["core"] * half, half)
        self.copy(src, dst, 0, at["dev_x"])
        self.copy(src, dst, 1, at["dev_y"])
        self.own = pltpu.make_async_copy(self.src, self.view(at["shard"], 0, self.rows), self.local)
        self.own.start()

    def second(self):
        at, half, quarter = self.at, self.rows // 2, self.rows // 4
        start = at["core"] * half
        self.copies[0].wait_recv()
        part = self.view(at["sx"], start, quarter)
        self.copy(part, part, 2, at["dev_y"])
        part = self.view(at["sx"], start, half)
        self.copy(part, part, 3, at["dev_c"])
        self.copies[1].wait_recv()
        part = self.view(at["sy"], start + quarter, quarter)
        self.copy(part, part, 4, at["dev_x"])
        part = self.view(at["sy"], start, half)
        self.copy(part, part, 5, at["dev_c"])

    def third(self):
        at, half = self.at, self.rows // 2
        self.copies[2].wait_recv()
        self.copies[4].wait_recv()
        part = self.view(at["sd"], at["core"] * half, half)
        self.copy(part, part, 6, at["dev_c"])

    def finish(self):
        for index in (3, 5, 6):
            self.copies[index].wait_recv()
        for made in self.copies:
            made.wait_send()
        self.own.wait()


def plane_gather_kernel(*refs, axes):
    count = len(axes)
    send, recv, local = refs[2 * count :]
    at = place()
    meet([at["dev_x"], at["dev_y"], at["dev_c"]])
    gathers = [
        PlaneGather(refs[k], refs[count + k], axes[k], send.at[k], recv.at[k], local.at[k], at)
        for k in range(count)
    ]
    for step in ("first", "second", "third", "finish"):
        for gather in gathers:
            getattr(gather, step)()


def plane_gather(arrays, axes, ident):
    if lax.axis_size("shard") != 4:
        return [lax.all_gather(v, "shard", axis=a, tiled=True) for v, a in zip(arrays, axes)]
    count = len(arrays)
    shapes = []
    for array, axis in zip(arrays, axes):
        shape = list(array.shape)
        shape[axis] *= 4
        shapes.append(jax.ShapeDtypeStruct(tuple(shape), array.dtype))
    return pl.pallas_call(
        functools.partial(plane_gather_kernel, axes=axes),
        out_shape=shapes,
        in_specs=[pl.BlockSpec(memory_space=pl.ANY)] * count,
        out_specs=[pl.BlockSpec(memory_space=pl.ANY)] * count,
        scratch_shapes=[
            pltpu.SemaphoreType.DMA((count, PlaneGather.COPIES)),
            pltpu.SemaphoreType.DMA((count, PlaneGather.COPIES)),
            pltpu.SemaphoreType.DMA((count,)),
        ],
        compiler_params=pltpu.CompilerParams(
            collective_id=ident, has_side_effects=True, vmem_limit_bytes=32 << 20
        ),
    )(*arrays)


class PlaneReduce:
    COPIES = 4

    def __init__(self, src, dst, mine, got, hold, last, send, recv, local, at):
        self.src, self.dst, self.mine, self.got, self.hold, self.last = src, dst, mine, got, hold, last
        self.send, self.recv, self.local, self.at = send, recv, local, at
        self.half = src.shape[1] // 2

    @staticmethod
    def scratch(shape):
        half = shape[1] // 2
        return [
            pltpu.VMEM((4, half, shape[2]), BF16),
            pltpu.VMEM((4, half, shape[2]), BF16),
            pltpu.VMEM((2, half, shape[2]), BF16),
            pltpu.VMEM((2, half, shape[2]), BF16),
        ]

    def first(self):
        at, half = self.at, self.half
        upper, lower = pl.ds(0, half), pl.ds(half, half)
        plan = [
            (at["sx"], upper, at["dev_x"], 0),
            (at["sd"], upper, at["dev_x"], 1),
            (at["sy"], lower, at["dev_y"], 2),
            (at["sd"], lower, at["dev_y"], 3),
        ]
        self.out = []
        for shard, rows, device, slot in plan:
            made = remote(
                self.src.at[shard, rows, :], self.got.at[slot], self.send.at[slot], self.recv.at[slot], device
            )
            made.start()
            self.out.append(made)
        self.near = []
        for slot, (shard, rows) in enumerate(
            [(at["shard"], upper), (at["sy"], upper), (at["shard"], lower), (at["sx"], lower)]
        ):
            made = pltpu.make_async_copy(self.src.at[shard, rows, :], self.mine.at[slot], self.local.at[slot])
            made.start()
            self.near.append(made)

    def second(self):
        at = self.at
        for slot in (1, 3):
            self.near[slot].wait()
            self.out[slot].wait_recv()
            self.hold[slot // 2] = (
                self.mine[slot].astype(F32) + self.got[slot].astype(F32)
            ).astype(BF16)
            made = remote(
                self.hold.at[slot // 2],
                self.last.at[slot // 2],
                self.send.at[4 + slot // 2],
                self.recv.at[4 + slot // 2],
                at["dev_y"] if slot == 1 else at["dev_x"],
            )
            made.start()
            self.out.append(made)

    def third(self):
        half = self.half
        for slot in (0, 2):
            self.near[slot].wait()
            self.out[slot].wait_recv()
            self.out[4 + slot // 2].wait_recv()
            self.dst[pl.ds(slot // 2 * half, half), :] = (
                self.mine[slot].astype(F32) + self.got[slot].astype(F32)
            ) + self.last[slot // 2].astype(F32)

    def finish(self):
        for made in self.out:
            made.wait_send()


def plane_reduce_kernel(*refs, count):
    scratch = refs[2 * count :]
    send, recv, local = scratch[4 * count :]
    at = place()
    meet([at["dev_x"], at["dev_y"]])
    reduces = [
        PlaneReduce(
            refs[k], refs[count + k], *scratch[4 * k : 4 * k + 4], send.at[k], recv.at[k], local.at[k], at
        )
        for k in range(count)
    ]
    for step in ("first", "second", "third", "finish"):
        for reduce in reduces:
            getattr(reduce, step)()


def plane_reduce(arrays, ident):
    if lax.axis_size("shard") != 4:
        return [
            lax.psum_scatter(v, "shard", scatter_dimension=0, tiled=True)[0].astype(F32) for v in arrays
        ]
    count = len(arrays)
    scratch = []
    for array in arrays:
        scratch += PlaneReduce.scratch(array.shape)
    return pl.pallas_call(
        functools.partial(plane_reduce_kernel, count=count),
        out_shape=[jax.ShapeDtypeStruct(v.shape[1:], F32) for v in arrays],
        in_specs=[pl.BlockSpec(memory_space=pl.ANY)] * count,
        out_specs=[pl.BlockSpec(memory_space=pltpu.VMEM)] * count,
        scratch_shapes=scratch
        + [
            pltpu.SemaphoreType.DMA((count, 6)),
            pltpu.SemaphoreType.DMA((count, 6)),
            pltpu.SemaphoreType.DMA((count, 4)),
        ],
        compiler_params=pltpu.CompilerParams(
            collective_id=ident, has_side_effects=True, vmem_limit_bytes=48 << 20
        ),
    )(*arrays)


class ChainGather:
    @staticmethod
    def copies(chips):
        return 4 * chips

    def __init__(self, src, dst, send, recv, local, at, chips):
        self.src, self.dst, self.send, self.recv, self.local = src, dst, send, recv, local
        self.at, self.chips = at, chips

    def copy(self, block, index, device, first=False):
        part = self.dst.at[block]
        return remote(
            self.src if first else part, part, self.send.at[index], self.recv.at[index], self.at[device]
        )

    def right(self, step):
        at = self.at
        return self.copy((at["z"] - step + 1) * 2 + at["core"], step - 1, "dev_right", step == 1)

    def left(self, step):
        at = self.at
        return self.copy(
            (at["z"] + step - 1) * 2 + at["core"], self.chips + step - 1, "dev_left", step == 1
        )

    def over(self, step):
        at = self.at
        return self.copy(
            (at["z"] - step) * 2 + at["core"], (2 if step >= 0 else 3) * self.chips + abs(step), "dev_c", step == 0
        )

    def arrived(self, step, side):
        at = self.at
        if side == "left":
            return self.copy((at["z"] - step) * 2 + at["core"], step - 1, "dev_right")
        return self.copy((at["z"] + step) * 2 + at["core"], self.chips + step - 1, "dev_left")

    def start(self):
        at = self.at
        pl.when(at["z"] < self.chips - 1)(lambda: self.right(1).start())
        pl.when(at["z"] > 0)(lambda: self.left(1).start())
        self.over(0).start()
        self.own = pltpu.make_async_copy(self.src, self.dst.at[at["expert"]], self.local)
        self.own.start()

    def step(self, step):
        at, chips = self.at, self.chips

        @pl.when(at["z"] - step >= 0)
        def _():
            self.arrived(step, "left").wait_recv()
            if step < chips - 1:
                pl.when(at["z"] < chips - 1)(lambda: self.right(step + 1).start())
            self.over(step).start()

        @pl.when(at["z"] + step < chips)
        def _():
            self.arrived(step, "right").wait_recv()
            if step < chips - 1:
                pl.when(at["z"] > 0)(lambda: self.left(step + 1).start())
            self.over(-step).start()

    def finish(self, step):
        at = self.at
        if step == 0:
            self.over(0).wait()
            self.own.wait()
            return
        pl.when(at["z"] - step >= 0)(lambda: self.over(step).wait())
        pl.when(at["z"] + step < self.chips)(lambda: self.over(-step).wait())

    def sent(self):
        at, chips = self.at, self.chips
        for step in range(1, chips):
            pl.when((at["z"] - step + 1 >= 0) & (at["z"] < chips - 1))(lambda: self.right(step).wait_send())
            pl.when((at["z"] + step - 1 < chips) & (at["z"] > 0))(lambda: self.left(step).wait_send())


def chain_meet(at, chips, others):
    barrier = pltpu.get_barrier_semaphore()
    for device in others:
        pl.semaphore_signal(barrier, inc=1, device_id=device, device_id_type=MESH)

    @pl.when(at["z"] > 0)
    def _():
        pl.semaphore_signal(barrier, inc=1, device_id=at["dev_left"], device_id_type=MESH)

    @pl.when(at["z"] < chips - 1)
    def _():
        pl.semaphore_signal(barrier, inc=1, device_id=at["dev_right"], device_id_type=MESH)

    ends = jnp.where(at["z"] == 0, 1, 0) + jnp.where(at["z"] == chips - 1, 1, 0)
    pl.semaphore_wait(barrier, len(others) + 2 - ends)


def dot_nn(left, right):
    return lax.dot_general(left, right, (((1,), (0,)), ((), ())), preferred_element_type=F32)


def dot_nt(left, right):
    return lax.dot_general(left, right, (((1,), (1,)), ((), ())), preferred_element_type=F32)


def dot_tn(left, right):
    return lax.dot_general(left, right, (((0,), (0,)), ((), ())), preferred_element_type=F32)


def columns(start, count):
    return pl.ds(pl.multiple_of(start, 128), count)


def rope_lanes(length):
    half = HEAD_DIM // 2
    frequency = 10000.0 ** (-jnp.arange(half, dtype=F32) * 2.0 / HEAD_DIM)
    angles = jnp.arange(length, dtype=F32)[:, None] * frequency[None, :]
    cosine, sine = jnp.cos(angles), jnp.sin(angles)
    return jnp.concatenate([cosine] * 4, axis=1), jnp.concatenate([-sine, sine] * 2, axis=1)


def partner(values):
    lane = lax.broadcasted_iota(jnp.int32, values.shape, 1)
    half = HEAD_DIM // 2
    ahead = pltpu.roll(values, 128 - half, 1)
    behind = pltpu.roll(values, half, 1)
    return jnp.where(lane % HEAD_DIM < half, ahead, behind)


def front_kernel(*refs, plane, chips):
    (prefix, x_ref, cot_ref, route_ref, weight_ref, cos_ref, sin_ref), refs = refs[:7], refs[7:]
    if plane:
        (qkv_part, out_part, gains_part, sg, su, sd), refs = refs[:6], refs[6:]
    else:
        (qkv_full, out_full, gains_full), refs = refs[:3], refs[3:]
    (cot_all, table_all, h1_ref, rot_ref, att_ref, lse_ref, resid_ref, h2_ref, cot_low), refs = refs[:9], refs[9:]
    if plane:
        (qkv_full, out_full, gains_full, sg_full, su_full, sd_full), refs = refs[:6], refs[6:]
    bias_ref, table_ref, chain_send, chain_recv, chain_local = refs[:5]
    length, width = x_ref.shape
    experts = table_ref.shape[0] // 2
    at = place()
    chain_meet(at, chips, [at["dev_x"], at["dev_y"], at["dev_c"]] if plane else [at["dev_c"]])
    if plane:
        send, recv, local = refs[5:8]
        parts = [(qkv_part, qkv_full), (out_part, out_full), (gains_part, gains_full)]
        shared = [(sg, sg_full), (su, su_full), (sd, sd_full)]
        gathers = [
            PlaneGather(a, b, 0, send.at[k], recv.at[k], local.at[k], at) for k, (a, b) in enumerate(parts + shared)
        ]
        first, later = gathers[2::-1], gathers[3:]
        for gather in first:
            gather.first()
    cot_low[...] = cot_ref[...].astype(BF16)
    names = lax.broadcasted_iota(jnp.int32, (experts, length), 0)
    chosen = [route_ref[pl.ds(k, 1), :] == names for k in range(TOP)]
    member = (chosen[0] | chosen[1]).astype(F32)
    earlier = (
        lax.broadcasted_iota(jnp.int32, (length, length), 0)
        < lax.broadcasted_iota(jnp.int32, (length, length), 1)
    ).astype(F32)
    slot = dot_nn(member.astype(BF16), earlier.astype(BF16))
    table_ref[:experts, :] = jnp.where(member > 0, slot, -1.0)
    table_ref[experts:, :] = sum(
        jnp.where(chosen[k], weight_ref[pl.ds(k, 1), :], 0.0) for k in range(TOP)
    )
    chains = [
        ChainGather(a, b, chain_send.at[k], chain_recv.at[k], chain_local.at[k], at, chips)
        for k, (a, b) in enumerate([(table_ref, table_all), (cot_low, cot_all)])
    ]
    for chain in chains:
        chain.start()
    row = lax.broadcasted_iota(jnp.int32, (length, length), 0)
    col = lax.broadcasted_iota(jnp.int32, (length, length), 1)
    bias_ref[...] = jnp.where((col < prefix[0]) | (col <= row), 0.0, -1e30)
    if plane:
        for step in ("second", "third", "finish"):
            for gather in first:
                getattr(gather, step)()
        for gather in later:
            gather.first()
    blocks = gains_full.shape[0] // 64
    gain_one = sum(gains_full[pl.ds(64 * k, 1), :].astype(F32) for k in range(blocks))
    gain_two = sum(gains_full[pl.ds(64 * k + 32, 1), :].astype(F32) for k in range(blocks))
    x = x_ref[...]
    inverse = lax.rsqrt(jnp.mean(x * x, axis=-1, keepdims=True) + EPS)
    h1_ref[...] = (x * inverse * gain_one).astype(BF16)

    def project(block, turned):
        cols = columns(block * 256, 256)
        part = dot_nn(h1_ref[...], qkv_full[:, cols])
        if turned:
            part = jnp.concatenate(
                [v * cos_ref[...] + partner(v) * sin_ref[...] for v in (part[:, :128], part[:, 128:])], axis=1
            )
        rot_ref[:, cols] = part.astype(BF16)

    pl.loop(0, 2 * width // 256)(lambda block: project(block, True))
    pl.loop(2 * width // 256, 3 * width // 256)(lambda block: project(block, False))
    for chain in chains:
        chain.step(1)
    lse_ref[...] = jnp.zeros_like(lse_ref)
    rows_at_once = min(256, length)

    def pair(j):
        queries, keys, values = (
            rot_ref[:, columns(part * width + j * 128, 128)] for part in range(3)
        )
        low_lanes = lax.broadcasted_iota(jnp.int32, (rows_at_once, 128), 1) < HEAD_DIM
        for start in range(0, length, rows_at_once):
            rows = pl.ds(start, rows_at_once)
            outs = []
            for head in range(2):
                mine = low_lanes if head == 0 else ~low_lanes
                query = jnp.where(mine, queries[start : start + rows_at_once], 0.0) * HEAD_DIM**-0.5
                scores = dot_nt(query.astype(BF16), keys) + bias_ref[rows, :]
                peak = jnp.max(scores, axis=-1, keepdims=True)
                exponent = jnp.exp(scores - peak)
                total = jnp.sum(exponent, axis=-1, keepdims=True)
                outs.append(dot_nn((exponent / total).astype(BF16), values))
                lanes = lax.broadcasted_iota(jnp.int32, (rows_at_once, 128), 1)
                lse_ref[rows, :] = jnp.where(lanes == 2 * j + head, peak + jnp.log(total), lse_ref[rows, :])
            att_ref[rows, columns(j * 128, 128)] = jnp.where(low_lanes, *outs).astype(BF16)

    pairs = width // 128
    pl.loop(0, pairs // 2)(pair)
    for step in range(2, chips - 1):
        for chain in chains:
            chain.step(step)
    if plane:
        for gather in later:
            gather.second()
    pl.loop(pairs // 2, pairs)(pair)
    resid = x_ref[...] + dot_nn(att_ref[...], out_full[...])
    resid_ref[...] = resid
    inverse = lax.rsqrt(jnp.mean(resid * resid, axis=-1, keepdims=True) + EPS)
    h2_ref[...] = (resid * inverse * gain_two).astype(BF16)
    for chain in chains:
        chain.step(chips - 1)
    if plane:
        for step in ("third", "finish"):
            for gather in later:
                getattr(gather, step)()
    for chain in chains:
        for step in range(chips):
            chain.finish(step)
        chain.sent()


def front(prefix, inputs, cotangent, route_rows, weight_rows, qkv_weight, out_weight, gains, shared, ident):
    length, width = inputs.shape
    group = lax.axis_size("expert")
    chips, plane = group // 2, lax.axis_size("shard") == 4
    shards = lax.axis_size("shard")
    cosine, sine = rope_lanes(length)
    operands = [prefix, inputs, cotangent, route_rows, weight_rows, cosine, sine]
    vmem, anywhere = pl.BlockSpec(memory_space=pltpu.VMEM), pl.BlockSpec(memory_space=pl.ANY)
    in_specs = [pl.BlockSpec(memory_space=pltpu.SMEM)] + [vmem] * 6
    weights = [qkv_weight, out_weight, gains]
    if plane:
        operands += weights + shared
        in_specs += [anywhere] * 6
    else:
        weights = [lax.all_gather(v, "shard", axis=0, tiled=True) for v in weights]
        shared = [lax.all_gather(v, "shard", axis=0, tiled=True) for v in shared]
        operands += weights
        in_specs += [vmem] * 3
    shape = jax.ShapeDtypeStruct
    out_shape = [
        shape((group, length, width), BF16),
        shape((group, 2 * group, length), F32),
        shape((length, width), BF16),
        shape((length, 3 * width), BF16),
        shape((length, width), BF16),
        shape((length, 128), F32),
        shape((length, width), F32),
        shape((length, width), BF16),
        shape((length, width), BF16),
    ]
    out_specs = [anywhere] * 2 + [vmem] * 7
    scratch = [
        pltpu.VMEM((length, length), F32),
        pltpu.VMEM((2 * group, length), F32),
        pltpu.SemaphoreType.DMA((2, ChainGather.copies(chips))),
        pltpu.SemaphoreType.DMA((2, ChainGather.copies(chips))),
        pltpu.SemaphoreType.DMA((2,)),
    ]
    if plane:
        out_shape += [shape((shards * v.shape[0], v.shape[1]), BF16) for v in weights + shared]
        out_specs += [vmem] * 3 + [anywhere] * 3
        scratch += [
            pltpu.SemaphoreType.DMA((6, PlaneGather.COPIES)),
            pltpu.SemaphoreType.DMA((6, PlaneGather.COPIES)),
            pltpu.SemaphoreType.DMA((6,)),
        ]
    outs = pl.pallas_call(
        functools.partial(front_kernel, plane=plane, chips=chips),
        out_shape=out_shape,
        in_specs=in_specs,
        out_specs=out_specs,
        scratch_shapes=scratch,
        compiler_params=pltpu.CompilerParams(
            collective_id=ident, has_side_effects=True, vmem_limit_bytes=48 << 20
        ),
    )(*operands)
    if not plane:
        outs = list(outs) + weights + shared
    return outs


def on_device(
    inputs,
    cotangent,
    norm_one,
    qkv_weight,
    out_weight,
    norm_two,
    shared_gate,
    shared_up,
    shared_down,
    expert_gate,
    expert_up,
    expert_down,
    gate_weights,
    routes,
    prefix,
):
    length, model_width = inputs.shape
    experts = lax.axis_size("expert") * expert_gate.shape[0]
    shards = lax.axis_size("shard")
    me = lax.axis_index("expert")
    shards_at = lax.axis_index("shard")
    capacity = 4 * length // experts
    gains = jnp.concatenate(
        [jnp.broadcast_to(v, (32, v.shape[0])) for v in (norm_one, norm_two)], axis=0
    )
    gains = lax.dynamic_update_slice(
        jnp.zeros((64, model_width), BF16), gains, (0, shards_at * norm_one.shape[0])
    )
    (
        cot_all,
        table_all,
        normed_one,
        turned,
        attended,
        logsum,
        resid,
        normed_two,
        out_low,
        qkv_full,
        out_full,
        gains_full,
        gate_blocks,
        up_blocks,
        down_full,
    ) = front(
        prefix,
        inputs,
        cotangent,
        routes.T,
        gate_weights.T,
        qkv_weight,
        out_weight,
        gains,
        [shared_gate, shared_up, shared_down],
        1,
    )
    table_mine = jnp.stack(
        [lax.dynamic_index_in_dim(table_all, me + k * experts, axis=1, keepdims=False) for k in range(2)], axis=1
    )
    gain_rows = jnp.sum(gains_full.reshape(shards, 64, model_width).astype(F32), axis=0)
    gain_one, gain_two = gain_rows[0], gain_rows[32]
    inverse_one = lax.rsqrt(jnp.mean(inputs * inputs, axis=-1, keepdims=True) + EPS)
    inverse_two = lax.rsqrt(jnp.mean(resid * resid, axis=-1, keepdims=True) + EPS)
    normed_all = lax.all_gather(normed_two, "expert", axis=0)
    gate_full = gate_blocks.reshape(shards, model_width, -1).transpose(1, 0, 2).reshape(model_width, -1)
    up_full = up_blocks.reshape(shards, model_width, -1).transpose(1, 0, 2).reshape(model_width, -1)
    cosine_table, sine_table = rope_tables(length)
    head_shape = (length, HEADS, HEAD_DIM)
    queries, key_rows, value_rows = (
        turned[:, k * model_width : (k + 1) * model_width].reshape(head_shape) for k in range(3)
    )
    logsum = logsum[:, :HEADS].T[:, :, None]
    score_scale = HEAD_DIM ** (-0.5)
    row_pos = lax.broadcasted_iota(jnp.int32, (length, length), 0)
    col_pos = lax.broadcasted_iota(jnp.int32, (length, length), 1)
    visible = (col_pos < prefix[0]) | (col_pos <= row_pos)

    def masked_scores():
        raw_scores = (
            jnp.einsum("qhd,khd->hqk", queries, key_rows, preferred_element_type=F32) * score_scale
        )
        return jnp.where(visible[None], raw_scores, -1e30)

    shared_pre = matmul(normed_two, gate_full)
    shared_lift = matmul(normed_two, up_full)
    shared_act, shared_slope = gated_unit(shared_pre)
    shared_hidden = (shared_act * shared_lift).astype(BF16)
    shared_out = matmul(shared_hidden, down_full)
    shared_down_grad = matmul(shared_hidden.T, out_low)
    shared_hgrad = matmul(out_low, down_full.T)
    shared_pre_grad = (shared_hgrad * shared_lift * shared_slope).astype(BF16)
    shared_lift_grad = (shared_hgrad * shared_act).astype(BF16)
    shared_gate_grad = matmul(normed_two.T, shared_pre_grad)
    shared_up_grad = matmul(normed_two.T, shared_lift_grad)
    shared_back = matmul(shared_pre_grad, gate_full.T) + matmul(shared_lift_grad, up_full.T)

    pick = (
        jnp.arange(capacity, dtype=F32)[None, :, None] == table_mine[:, 0][:, None, :]
    ).astype(BF16)
    weight_rows = jnp.sum(pick.astype(F32) * table_mine[:, 1][:, None, :], axis=2)

    def to_rows(values):
        return jnp.einsum("ect,etd->ecd", pick, values, preferred_element_type=F32)

    def to_tokens(rows):
        return jnp.einsum("ect,ecd->etd", pick, rows, preferred_element_type=F32)

    gate_local, up_local, down_local = expert_gate[0], expert_up[0], expert_down[0]
    row_count = experts * capacity
    rows = to_rows(normed_all).astype(BF16).reshape(row_count, model_width)
    cot_rows = to_rows(cot_all)
    grad_rows = (cot_rows * weight_rows[:, :, None]).astype(BF16).reshape(row_count, model_width)
    pre_gate = matmul(rows, gate_local)
    pre_up = matmul(rows, up_local)
    activated, derivative = gated_unit(pre_gate)
    hidden = (activated * pre_up).astype(BF16)
    hidden_grad = matmul(grad_rows, down_local.T)
    gate_pre_grad = (hidden_grad * pre_up * derivative).astype(BF16)
    up_pre_grad = (hidden_grad * activated).astype(BF16)
    row_grad = (matmul(gate_pre_grad, gate_local.T) + matmul(up_pre_grad, up_local.T)).astype(BF16)
    back_part = to_tokens(row_grad.reshape(experts, capacity, model_width)).astype(BF16)
    back = lax.psum_scatter(back_part, "expert", scatter_dimension=0, tiled=False).astype(F32)

    result = matmul(hidden, down_local).astype(BF16).reshape(experts, capacity, model_width)
    weighted = (result.astype(F32) * weight_rows[:, :, None]).astype(BF16)
    mix_part = to_tokens(weighted).astype(BF16)
    mixture = lax.psum_scatter(mix_part, "expert", scatter_dimension=0, tiled=False).astype(F32)
    weight_dot = jnp.sum(result.astype(F32) * cot_rows, axis=2)
    weight_back = jnp.einsum("ect,ec->et", pick.astype(F32), weight_dot, precision=lax.Precision.HIGHEST)
    weight_got = lax.all_to_all(weight_back, "expert", split_axis=0, concat_axis=0, tiled=True)
    onehot = routes[:, :, None] == jnp.arange(experts, dtype=jnp.int32)[None, None, :]
    gate_weights_grad = jnp.sum(jnp.where(onehot, weight_got.T[:, None, :], 0.0), axis=2)

    def blocks_of_columns(value):
        width = value.shape[1] // shards
        return value.astype(BF16).reshape(value.shape[0], shards, width).transpose(1, 0, 2)

    def blocks_of_rows(value):
        return value.astype(BF16).reshape(shards, value.shape[0] // shards, value.shape[1])

    gate_term = matmul(rows.T, gate_pre_grad)
    up_term = matmul(rows.T, up_pre_grad)
    down_term = matmul(hidden.T, grad_rows)
    expert_gate_grad, expert_up_grad, expert_down_grad = plane_reduce(
        [blocks_of_columns(gate_term), blocks_of_columns(up_term), blocks_of_rows(down_term)], 3
    )

    output = resid + mixture + shared_out
    normed_two_grad = shared_back + back
    gain_two_grad, resid_extra = norm_back(resid, inverse_two, gain_two, normed_two_grad)
    resid_grad = cotangent + resid_extra
    attn_low = resid_grad.astype(BF16)
    out_weight_grad = matmul(attended.T, attn_low)
    attended_grad = matmul(attn_low, out_full.T).astype(BF16).reshape(head_shape)
    scores = masked_scores()
    probs_full = jnp.exp(scores - logsum)
    value_grad = jnp.einsum(
        "hqk,qhd->khd", probs_full.astype(BF16), attended_grad, preferred_element_type=F32
    )
    probs_grad = jnp.einsum("qhd,khd->hqk", attended_grad, value_rows, preferred_element_type=F32)
    score_grad = (
        probs_full * (probs_grad - jnp.sum(probs_full * probs_grad, axis=-1, keepdims=True))
    ).astype(BF16)
    query_grad = (
        jnp.einsum("hqk,khd->qhd", score_grad, key_rows, preferred_element_type=F32) * score_scale
    )
    key_grad = (
        jnp.einsum("hqk,qhd->khd", score_grad, queries, preferred_element_type=F32) * score_scale
    )
    projected_grad = jnp.concatenate(
        [
            rotate(query_grad, cosine_table, -sine_table).reshape(length, model_width),
            rotate(key_grad, cosine_table, -sine_table).reshape(length, model_width),
            value_grad.reshape(length, model_width),
        ],
        axis=1,
    ).astype(BF16)
    qkv_weight_grad = matmul(normed_one.T, projected_grad)
    normed_one_grad = matmul(projected_grad, qkv_full.T)
    gain_one_grad, input_extra = norm_back(inputs, inverse_one, gain_one, normed_one_grad)
    input_grad = resid_grad + input_extra

    gain_block = jnp.zeros((shards, 32, model_width // shards), BF16)
    gain_block = gain_block.at[:, 0, :].set(gain_one_grad.astype(BF16).reshape(shards, -1))
    gain_block = gain_block.at[:, 1, :].set(gain_two_grad.astype(BF16).reshape(shards, -1))
    pieces = plane_reduce(
        [
            blocks_of_rows(qkv_weight_grad),
            blocks_of_rows(out_weight_grad),
            gain_block,
            blocks_of_columns(shared_gate_grad),
            blocks_of_columns(shared_up_grad),
            blocks_of_rows(shared_down_grad),
        ],
        4,
    )
    summed = [lax.psum(v.astype(BF16), "expert").astype(F32) for v in pieces]
    return (
        output,
        input_grad,
        summed[2][0],
        summed[0],
        summed[1],
        summed[2][1],
        summed[3],
        summed[4],
        summed[5],
        expert_gate_grad[None],
        expert_up_grad[None],
        expert_down_grad[None],
        gate_weights_grad,
    )


def solution(mesh):
    tokens = P(("expert", "shard"), None)
    in_specs = (
        tokens,
        tokens,
        P("shard"),
        P("shard", None),
        P("shard", None),
        P("shard"),
        P(None, "shard"),
        P(None, "shard"),
        P("shard", None),
        P("expert", None, None),
        P("expert", None, None),
        P("expert", None, None),
        tokens,
        tokens,
        P(("expert", "shard")),
    )
    out_specs = (
        tokens,
        tokens,
        P("shard"),
        P("shard", None),
        P("shard", None),
        P("shard"),
        P(None, "shard"),
        P(None, "shard"),
        P("shard", None),
        P("expert", None, "shard"),
        P("expert", None, "shard"),
        P("expert", "shard", None),
        tokens,
    )
    return jax.shard_map(
        on_device, mesh=mesh, in_specs=in_specs, out_specs=out_specs, check_vma=False
    )
```

```python
import functools

import jax
import jax.numpy as jnp
from jax import lax
from jax.experimental import pallas as pl
from jax.experimental.pallas import tpu as pltpu
from jax.sharding import PartitionSpec as P

HEADS = 12
HEAD_DIM = 64
TOP = 2
EPS = 1e-06
MESH = pl.DeviceIdType.MESH
F32 = jnp.float32
BF16 = jnp.bfloat16


def place():
    expert, shard = lax.axis_index("expert"), lax.axis_index("shard")
    core, x, y = expert % 2, shard % 2, shard // 2
    return dict(
        expert=expert,
        shard=shard,
        core=core,
        z=expert // 2,
        sx=2 * y + 1 - x,
        sy=2 * (1 - y) + x,
        sd=2 * (1 - y) + 1 - x,
        dev_x=(expert, 2 * y + 1 - x),
        dev_y=(expert, 2 * (1 - y) + x),
        dev_c=(expert + 1 - 2 * core, shard),
        dev_left=(expert - 2, shard),
        dev_right=(expert + 2, shard),
    )


def meet(devices):
    barrier = pltpu.get_barrier_semaphore()
    for device in devices:
        pl.semaphore_signal(barrier, inc=1, device_id=device, device_id_type=MESH)
    pl.semaphore_wait(barrier, len(devices))


def remote(src, dst, send, recv, device):
    return pltpu.make_async_remote_copy(
        src_ref=src, dst_ref=dst, send_sem=send, recv_sem=recv, device_id=device, device_id_type=MESH
    )


class PlaneGather:
    COPIES = 7

    def __init__(self, src, dst, axis, send, recv, local, at):
        self.src, self.dst, self.axis, self.at = src, dst, axis, at
        self.send, self.recv, self.local = send, recv, local
        self.rows, self.cols = src.shape
        self.copies = []

    def view(self, shard, start, count):
        if self.axis == 0:
            return self.dst.at[pl.ds(pl.multiple_of(shard * self.rows + start, 16), count), :]
        return self.dst.at[
            pl.ds(pl.multiple_of(start, 16), count),
            pl.ds(pl.multiple_of(shard * self.cols, 128), self.cols),
        ]

    def copy(self, src, dst, index, device):
        made = remote(src, dst, self.send.at[index], self.recv.at[index], device)
        made.start()
        self.copies.append(made)

    def first(self):
        at, half = self.at, self.rows // 2
        src = self.src.at[pl.ds(pl.multiple_of(at["core"] * half, 16), half), :]
        dst = self.view(at["shard"], at["core"] * half, half)
        self.copy(src, dst, 0, at["dev_x"])
        self.copy(src, dst, 1, at["dev_y"])
        self.own = pltpu.make_async_copy(self.src, self.view(at["shard"], 0, self.rows), self.local)
        self.own.start()

    def second(self):
        at, half, quarter = self.at, self.rows // 2, self.rows // 4
        start = at["core"] * half
        self.copies[0].wait_recv()
        part = self.view(at["sx"], start, quarter)
        self.copy(part, part, 2, at["dev_y"])
        part = self.view(at["sx"], start, half)
        self.copy(part, part, 3, at["dev_c"])
        self.copies[1].wait_recv()
        part = self.view(at["sy"], start + quarter, quarter)
        self.copy(part, part, 4, at["dev_x"])
        part = self.view(at["sy"], start, half)
        self.copy(part, part, 5, at["dev_c"])

    def third(self):
        at, half = self.at, self.rows // 2
        self.copies[2].wait_recv()
        self.copies[4].wait_recv()
        part = self.view(at["sd"], at["core"] * half, half)
        self.copy(part, part, 6, at["dev_c"])

    def finish(self):
        for index in (3, 5, 6):
            self.copies[index].wait_recv()
        for made in self.copies:
            made.wait_send()
        self.own.wait()


class ChainGather:
    @staticmethod
    def copies(chips):
        return 4 * chips

    def __init__(self, src, dst, send, recv, local, at, chips):
        self.src, self.dst, self.send, self.recv, self.local = src, dst, send, recv, local
        self.at, self.chips = at, chips

    def copy(self, block, index, device, first=False):
        part = self.dst.at[block]
        return remote(
            self.src if first else part, part, self.send.at[index], self.recv.at[index], self.at[device]
        )

    def right(self, step):
        at = self.at
        return self.copy((at["z"] - step + 1) * 2 + at["core"], step - 1, "dev_right", step == 1)

    def left(self, step):
        at = self.at
        return self.copy(
            (at["z"] + step - 1) * 2 + at["core"], self.chips + step - 1, "dev_left", step == 1
        )

    def over(self, step):
        at = self.at
        return self.copy(
            (at["z"] - step) * 2 + at["core"], (2 if step >= 0 else 3) * self.chips + abs(step), "dev_c", step == 0
        )

    def arrived(self, step, side):
        at = self.at
        if side == "left":
            return self.copy((at["z"] - step) * 2 + at["core"], step - 1, "dev_right")
        return self.copy((at["z"] + step) * 2 + at["core"], self.chips + step - 1, "dev_left")

    def start(self):
        at = self.at
        pl.when(at["z"] < self.chips - 1)(lambda: self.right(1).start())
        pl.when(at["z"] > 0)(lambda: self.left(1).start())
        self.over(0).start()
        self.own = pltpu.make_async_copy(self.src, self.dst.at[at["expert"]], self.local)
        self.own.start()

    def step(self, step):
        at, chips = self.at, self.chips

        @pl.when(at["z"] - step >= 0)
        def _():
            self.arrived(step, "left").wait_recv()
            if step < chips - 1:
                pl.when(at["z"] < chips - 1)(lambda: self.right(step + 1).start())
            self.over(step).start()

        @pl.when(at["z"] + step < chips)
        def _():
            self.arrived(step, "right").wait_recv()
            if step < chips - 1:
                pl.when(at["z"] > 0)(lambda: self.left(step + 1).start())
            self.over(-step).start()

    def finish(self, step):
        at = self.at
        if step == 0:
            self.over(0).wait()
            self.own.wait()
            return
        pl.when(at["z"] - step >= 0)(lambda: self.over(step).wait())
        pl.when(at["z"] + step < self.chips)(lambda: self.over(-step).wait())

    def sent(self):
        at, chips = self.at, self.chips
        for step in range(1, chips):
            pl.when((at["z"] - step + 1 >= 0) & (at["z"] < chips - 1))(lambda: self.right(step).wait_send())
            pl.when((at["z"] + step - 1 < chips) & (at["z"] > 0))(lambda: self.left(step).wait_send())


def chain_meet(at, chips, others):
    barrier = pltpu.get_barrier_semaphore()
    for device in others:
        pl.semaphore_signal(barrier, inc=1, device_id=device, device_id_type=MESH)

    @pl.when(at["z"] > 0)
    def _():
        pl.semaphore_signal(barrier, inc=1, device_id=at["dev_left"], device_id_type=MESH)

    @pl.when(at["z"] < chips - 1)
    def _():
        pl.semaphore_signal(barrier, inc=1, device_id=at["dev_right"], device_id_type=MESH)

    ends = jnp.where(at["z"] == 0, 1, 0) + jnp.where(at["z"] == chips - 1, 1, 0)
    pl.semaphore_wait(barrier, len(others) + 2 - ends)


def dot_nn(left, right):
    return lax.dot_general(left, right, (((1,), (0,)), ((), ())), preferred_element_type=F32)


def dot_nt(left, right):
    return lax.dot_general(left, right, (((1,), (1,)), ((), ())), preferred_element_type=F32)


def dot_tn(left, right):
    return lax.dot_general(left, right, (((0,), (0,)), ((), ())), preferred_element_type=F32)


def columns(start, count):
    return pl.ds(pl.multiple_of(start, 128), count)


def rope_lanes(length):
    half = HEAD_DIM // 2
    frequency = 10000.0 ** (-jnp.arange(half, dtype=F32) * 2.0 / HEAD_DIM)
    angles = jnp.arange(length, dtype=F32)[:, None] * frequency[None, :]
    cosine, sine = jnp.cos(angles), jnp.sin(angles)
    return jnp.concatenate([cosine] * 4, axis=1), jnp.concatenate([-sine, sine] * 2, axis=1)


def partner(values):
    lane = lax.broadcasted_iota(jnp.int32, values.shape, 1)
    half = HEAD_DIM // 2
    ahead = pltpu.roll(values, 128 - half, 1)
    behind = pltpu.roll(values, half, 1)
    return jnp.where(lane % HEAD_DIM < half, ahead, behind)


def front_kernel(*refs, plane, chips):
    (prefix, x_ref, cot_ref, route_ref, weight_ref, cos_ref, sin_ref), refs = refs[:7], refs[7:]
    if plane:
        (qkv_part, out_part, gains_part, sg, su, sd), refs = refs[:6], refs[6:]
    else:
        (qkv_full, out_full, gains_full), refs = refs[:3], refs[3:]
    (cot_all, table_all, h1_ref, rot_ref, att_ref, lse_ref, resid_ref, h2_ref, cot_low), refs = refs[:9], refs[9:]
    if plane:
        (qkv_full, out_full, gains_full, sg_full, su_full, sd_full), refs = refs[:6], refs[6:]
    bias_ref, table_ref, chain_send, chain_recv, chain_local = refs[:5]
    length, width = x_ref.shape
    experts = table_ref.shape[0] // 2
    at = place()
    chain_meet(at, chips, [at["dev_x"], at["dev_y"], at["dev_c"]] if plane else [at["dev_c"]])
    if plane:
        send, recv, local = refs[5:8]
        parts = [(qkv_part, qkv_full), (out_part, out_full), (gains_part, gains_full)]
        shared = [(sg, sg_full), (su, su_full), (sd, sd_full)]
        gathers = [
            PlaneGather(a, b, 0, send.at[k], recv.at[k], local.at[k], at) for k, (a, b) in enumerate(parts + shared)
        ]
        first, later = gathers[2::-1], gathers[3:]
        for gather in first:
            gather.first()
    cot_low[...] = cot_ref[...].astype(BF16)
    names = lax.broadcasted_iota(jnp.int32, (experts, length), 0)
    chosen = [route_ref[pl.ds(k, 1), :] == names for k in range(TOP)]
    member = (chosen[0] | chosen[1]).astype(F32)
    earlier = (
        lax.broadcasted_iota(jnp.int32, (length, length), 0)
        < lax.broadcasted_iota(jnp.int32, (length, length), 1)
    ).astype(F32)
    slot = dot_nn(member.astype(BF16), earlier.astype(BF16))
    table_ref[:experts, :] = jnp.where(member > 0, slot, -1.0)
    table_ref[experts:, :] = sum(
        jnp.where(chosen[k], weight_ref[pl.ds(k, 1), :], 0.0) for k in range(TOP)
    )
    chains = [
        ChainGather(a, b, chain_send.at[k], chain_recv.at[k], chain_local.at[k], at, chips)
        for k, (a, b) in enumerate([(table_ref, table_all), (cot_low, cot_all)])
    ]
    for chain in chains:
        chain.start()
    row = lax.broadcasted_iota(jnp.int32, (length, length), 0)
    col = lax.broadcasted_iota(jnp.int32, (length, length), 1)
    bias_ref[...] = jnp.where((col < prefix[0]) | (col <= row), 0.0, -1e30)
    if plane:
        for step in ("second", "third", "finish"):
            for gather in first:
                getattr(gather, step)()
        for gather in later:
            gather.first()
    blocks = gains_full.shape[0] // 64
    gain_one = sum(gains_full[pl.ds(64 * k, 1), :].astype(F32) for k in range(blocks))
    gain_two = sum(gains_full[pl.ds(64 * k + 32, 1), :].astype(F32) for k in range(blocks))
    x = x_ref[...]
    inverse = lax.rsqrt(jnp.mean(x * x, axis=-1, keepdims=True) + EPS)
    h1_ref[...] = (x * inverse * gain_one).astype(BF16)

    def project(block, turned):
        cols = columns(block * 256, 256)
        part = dot_nn(h1_ref[...], qkv_full[:, cols])
        if turned:
            part = jnp.concatenate(
                [v * cos_ref[...] + partner(v) * sin_ref[...] for v in (part[:, :128], part[:, 128:])], axis=1
            )
        rot_ref[:, cols] = part.astype(BF16)

    pl.loop(0, 2 * width // 256)(lambda block: project(block, True))
    pl.loop(2 * width // 256, 3 * width // 256)(lambda block: project(block, False))
    for chain in chains:
        chain.step(1)
    lse_ref[...] = jnp.zeros_like(lse_ref)
    rows_at_once = min(256, length)

    def pair(j):
        queries, keys, values = (
            rot_ref[:, columns(part * width + j * 128, 128)] for part in range(3)
        )
        low_lanes = lax.broadcasted_iota(jnp.int32, (rows_at_once, 128), 1) < HEAD_DIM
        for start in range(0, length, rows_at_once):
            rows = pl.ds(start, rows_at_once)
            outs = []
            for head in range(2):
                mine = low_lanes if head == 0 else ~low_lanes
                query = jnp.where(mine, queries[start : start + rows_at_once], 0.0) * HEAD_DIM**-0.5
                scores = dot_nt(query.astype(BF16), keys) + bias_ref[rows, :]
                peak = jnp.max(scores, axis=-1, keepdims=True)
                exponent = jnp.exp(scores - peak)
                total = jnp.sum(exponent, axis=-1, keepdims=True)
                outs.append(dot_nn((exponent / total).astype(BF16), values))
                lanes = lax.broadcasted_iota(jnp.int32, (rows_at_once, 128), 1)
                lse_ref[rows, :] = jnp.where(lanes == 2 * j + head, peak + jnp.log(total), lse_ref[rows, :])
            att_ref[rows, columns(j * 128, 128)] = jnp.where(low_lanes, *outs).astype(BF16)

    pairs = width // 128
    pl.loop(0, pairs // 2)(pair)
    for step in range(2, chips - 1):
        for chain in chains:
            chain.step(step)
    if plane:
        for gather in later:
            gather.second()
    pl.loop(pairs // 2, pairs)(pair)
    resid = x_ref[...] + dot_nn(att_ref[...], out_full[...])
    resid_ref[...] = resid
    inverse = lax.rsqrt(jnp.mean(resid * resid, axis=-1, keepdims=True) + EPS)
    h2_ref[...] = (resid * inverse * gain_two).astype(BF16)
    for chain in chains:
        chain.step(chips - 1)
    if plane:
        for step in ("third", "finish"):
            for gather in later:
                getattr(gather, step)()
    for chain in chains:
        for step in range(chips):
            chain.finish(step)
        chain.sent()


def front(prefix, inputs, cotangent, route_rows, weight_rows, qkv_weight, out_weight, gains, shared, ident):
    length, width = inputs.shape
    group = lax.axis_size("expert")
    chips, plane = group // 2, lax.axis_size("shard") == 4
    shards = lax.axis_size("shard")
    cosine, sine = rope_lanes(length)
    operands = [prefix, inputs, cotangent, route_rows, weight_rows, cosine, sine]
    vmem, anywhere = pl.BlockSpec(memory_space=pltpu.VMEM), pl.BlockSpec(memory_space=pl.ANY)
    in_specs = [pl.BlockSpec(memory_space=pltpu.SMEM)] + [vmem] * 6
    weights = [qkv_weight, out_weight, gains]
    if plane:
        operands += weights + shared
        in_specs += [anywhere] * 6
    else:
        weights = [lax.all_gather(v, "shard", axis=0, tiled=True) for v in weights]
        shared = [lax.all_gather(v, "shard", axis=0, tiled=True) for v in shared]
        operands += weights
        in_specs += [vmem] * 3
    shape = jax.ShapeDtypeStruct
    out_shape = [
        shape((group, length, width), BF16),
        shape((group, 2 * group, length), F32),
        shape((length, width), BF16),
        shape((length, 3 * width), BF16),
        shape((length, width), BF16),
        shape((length, 128), F32),
        shape((length, width), F32),
        shape((length, width), BF16),
        shape((length, width), BF16),
    ]
    out_specs = [anywhere] * 2 + [vmem] * 7
    scratch = [
        pltpu.VMEM((length, length), F32),
        pltpu.VMEM((2 * group, length), F32),
        pltpu.SemaphoreType.DMA((2, ChainGather.copies(chips))),
        pltpu.SemaphoreType.DMA((2, ChainGather.copies(chips))),
        pltpu.SemaphoreType.DMA((2,)),
    ]
    if plane:
        out_shape += [shape((shards * v.shape[0], v.shape[1]), BF16) for v in weights + shared]
        out_specs += [vmem] * 3 + [anywhere] * 3
        scratch += [
            pltpu.SemaphoreType.DMA((6, PlaneGather.COPIES)),
            pltpu.SemaphoreType.DMA((6, PlaneGather.COPIES)),
            pltpu.SemaphoreType.DMA((6,)),
        ]
    outs = pl.pallas_call(
        functools.partial(front_kernel, plane=plane, chips=chips),
        out_shape=out_shape,
        in_specs=in_specs,
        out_specs=out_specs,
        scratch_shapes=scratch,
        compiler_params=pltpu.CompilerParams(
            collective_id=ident, has_side_effects=True, vmem_limit_bytes=48 << 20
        ),
    )(*operands)
    if not plane:
        outs = list(outs) + weights + shared
    return outs


def near_order(chips):
    table = []
    for z in range(chips):
        others = sorted(range(chips), key=lambda s: (abs(s - z), abs(2 * s - chips + 1) * -1))
        table.append(others)
    return table


def pick_static(table, step, z):
    return sum(jnp.where(z == k, row[step], 0) for k, row in enumerate(table))


def gated_block(rows, grad, gate, up, down):
    pre_gate = dot_nn(rows, gate)
    pre_up = dot_nn(rows, up)
    sigmoid = 1.0 / (1.0 + jnp.exp(-pre_gate))
    active = pre_gate * sigmoid
    hidden = (active * pre_up).astype(BF16)
    hidden_grad = dot_nt(grad, down)
    gate_grad = (hidden_grad * pre_up * (sigmoid * (1.0 + pre_gate * (1.0 - sigmoid)))).astype(BF16)
    up_grad = (hidden_grad * active).astype(BF16)
    result = dot_nn(hidden, down)
    back = dot_nt(gate_grad, gate) + dot_nt(up_grad, up)
    return hidden, gate_grad, up_grad, result, back


def middle_kernel(*refs, chips, shards, capacity):
    (h2_ref, cot_ref, table_ref, cot_all, gate_hbm, up_hbm, down_hbm, sg_hbm, su_hbm, sd_hbm), refs = refs[:10], refs[10:]
    (rows_out, grad_out, hid_out, da_out, db_out, mix_out, back_out), refs = refs[:7], refs[7:]
    sown, sgot, (dots_out, sy_ref, dh_ref), refs = refs[:3], refs[3:6], refs[6:9], refs[9:]
    (sgg_s, sug_s, sdg_s, sg_sem, sg_send, sg_recv), refs = refs[:6], refs[6:]
    (gate_w, up_w, down_w, sg_w, su_w, sd_w, h2_all, cot_buf, rows_ref, grad_ref, cotr_ref, scale_ref), refs = refs[:12], refs[12:]
    (y_acc, r_acc, stage_f, stage_s, stage_t, got, total), refs = refs[:7], refs[7:]
    w_sem, s_sem, cot_sem, row_sem, f_sem, tot_sem, core_send, core_recv, chain_send, chain_recv, chain_local = refs
    length, width = h2_ref.shape
    experts = 2 * chips
    hidden_width = gate_w.shape[1]
    unit = stage_f.shape[-1]
    units = hidden_width // unit
    block = sg_w.shape[-1]
    at = place()
    me, core, z = at["expert"], at["core"], at["z"]
    order = near_order(chips)
    chain_meet(at, chips, [at["dev_c"]])
    chain = ChainGather(h2_ref, h2_all, chain_send, chain_recv, chain_local, at, chips)
    chain.start()

    def load_cot(step):
        chip = pick_static(order, step, z)
        return pltpu.make_async_copy(
            cot_all.at[pl.ds(2 * chip, 2)], cot_buf.at[step % 2], cot_sem.at[step % 2]
        )

    load_cot(0).start()
    loads = [
        pltpu.make_async_copy(a, b, w_sem.at[k])
        for k, (a, b) in enumerate([(gate_hbm.at[0], gate_w), (up_hbm.at[0], up_w), (down_hbm.at[0], down_w)])
    ]
    for load in loads:
        load.start()

    def load_shared(k, slot):
        return [
            pltpu.make_async_copy(sg_hbm.at[pl.ds(k * width, width), :], sg_w.at[slot], s_sem.at[slot, 0]),
            pltpu.make_async_copy(su_hbm.at[pl.ds(k * width, width), :], su_w.at[slot], s_sem.at[slot, 1]),
            pltpu.make_async_copy(sd_hbm.at[pl.ds(k * block, block), :], sd_w.at[slot], s_sem.at[slot, 2]),
        ]

    for load in load_shared(0, 0):
        load.start()

    def one_hot(source):
        slots = table_ref[source, pl.ds(me, 1), :]
        return lax.broadcasted_iota(jnp.int32, (capacity, length), 0).astype(F32) == slots

    def row_copies(step):
        return [
            pltpu.make_async_copy(rows_ref.at[step % 2], rows_out.at[step], row_sem.at[step % 2, 0]),
            pltpu.make_async_copy(grad_ref.at[step % 2], grad_out.at[step], row_sem.at[step % 2, 1]),
        ]

    def hidden_copies(step, k, slot):
        return [
            pltpu.make_async_copy(
                stage_f.at[slot, n], out.at[step, :, columns(k * unit, unit)], f_sem.at[slot, n]
            )
            for n, out in enumerate([hid_out, da_out, db_out])
        ]

    def core_copies(step):
        return [
            remote(
                stage.at[1 - core], got.at[n, step], core_send.at[n, step], core_recv.at[n, step], at["dev_c"]
            )
            for n, stage in enumerate([stage_s, stage_t])
        ]

    def total_copies(step):
        chip = pick_static(order, step, z)
        return [
            pltpu.make_async_copy(total.at[n], out.at[chip], tot_sem.at[n])
            for n, out in enumerate([mix_out, back_out])
        ]

    def join(step):
        if step > 0:
            for copy in total_copies(step - 1):
                copy.wait()
        for n, (copy, stage) in enumerate(zip(core_copies(step), [stage_s, stage_t])):
            copy.wait()
            total[n] = (stage[core].astype(F32) + got[n, step].astype(F32)).astype(BF16)
        for copy in total_copies(step):
            copy.start()

    def expert_rows(step):
        chip = pick_static(order, step, z)
        slot = step % 2
        load_cot(step).wait()
        if step + 1 < chips:
            load_cot(step + 1).start()
        if step >= 2:
            for copy in row_copies(step - 2):
                copy.wait()
        for d in range(2):
            source, part = 2 * chip + d, pl.ds(d * capacity, capacity)
            chosen = one_hot(source)
            select = chosen.astype(F32).astype(BF16)
            rows_ref[slot, part, :] = dot_nn(select, h2_all[source]).astype(BF16)
            cot_rows = dot_nn(select, cot_buf[slot, d])
            scale = jnp.sum(
                jnp.where(chosen, table_ref[source, pl.ds(experts + me, 1), :], 0.0), axis=1, keepdims=True
            )
            grad_ref[slot, part, :] = (cot_rows * scale).astype(BF16)
            cotr_ref[part, :] = cot_rows.astype(BF16)
            scale_ref[part, :] = scale
        for copy in row_copies(step):
            copy.start()
        y_acc[...] = jnp.zeros_like(y_acc)
        r_acc[...] = jnp.zeros_like(r_acc)
        if step == 0:
            for load in loads:
                load.wait()

        @pl.loop(0, units)
        def _(k):
            cols = columns(k * unit, unit)
            hidden, gate_grad, up_grad, result, back = gated_block(
                rows_ref[slot], grad_ref[slot], gate_w[:, cols], up_w[:, cols],
                down_w[pl.ds(pl.multiple_of(k * unit, unit), unit), :],
            )
            turn = k % 2

            def settle():
                for copy in hidden_copies(step, k, turn):
                    copy.wait()

            if step == 0:
                pl.when(k >= 2)(settle)
            else:
                settle()
            stage_f[turn, 0] = hidden
            stage_f[turn, 1] = gate_grad
            stage_f[turn, 2] = up_grad
            for copy in hidden_copies(step, k, turn):
                copy.start()
            y_acc[...] += result
            r_acc[...] += back

        if step > 0:
            join(step - 1)
        result = y_acc[...].astype(BF16).astype(F32)
        dots = jnp.sum(result * cotr_ref[...].astype(F32), axis=1, keepdims=True)
        weighted = (result * scale_ref[...]).astype(BF16)
        back = r_acc[...].astype(BF16)
        for d in range(2):
            source = 2 * chip + d
            chosen = one_hot(source)
            select = chosen.astype(F32).astype(BF16)
            part = slice(d * capacity, (d + 1) * capacity)
            stage_s[d] = dot_tn(select, weighted[part]).astype(BF16)
            stage_t[d] = dot_tn(select, back[part]).astype(BF16)
            dots_out[source] = jnp.sum(jnp.where(chosen, dots[part], 0.0), axis=0, keepdims=True)
        for copy in core_copies(step):
            copy.start()

    sy_ref[...] = jnp.zeros_like(sy_ref)
    dh_ref[...] = jnp.zeros_like(dh_ref)

    def shared_copies(k, arrival=False):
        copies = []
        for n, held in enumerate((sgg_s, sug_s, sdg_s)):
            half = held.shape[0] // 2
            mine, other = (pl.ds(pl.multiple_of(c * half, 16), half) for c in (core, 1 - core))
            over = remote(held.at[other, :], sgot[n].at[k], sg_send.at[n], sg_recv.at[n, k], at["dev_c"])
            if arrival:
                copies.append(over)
            else:
                copies += [pltpu.make_async_copy(held.at[mine, :], sown[n].at[k], sg_sem.at[n]), over]
        return copies

    def shared_settle(k):
        for copy in shared_copies(k)[::2]:
            copy.wait()
        for copy in shared_copies(k, True):
            copy.wait_send()

    def shared_block(k):
        slot = k % 2
        for load in load_shared(k, slot):
            load.wait()

        @pl.when(k + 1 < shards)
        def _():
            for load in load_shared(k + 1, 1 - slot):
                load.start()

        hidden, gate_grad, up_grad, result, back = gated_block(
            h2_ref[...], cot_ref[...], sg_w[slot], su_w[slot], sd_w[slot]
        )
        sy_ref[...] += result
        dh_ref[...] += back
        pl.when(k > 0)(lambda: shared_settle(k - 1))
        sgg_s[...] = dot_tn(h2_ref[...], gate_grad).astype(BF16)
        sug_s[...] = dot_tn(h2_ref[...], up_grad).astype(BF16)
        sdg_s[...] = dot_tn(hidden, cot_ref[...]).astype(BF16)
        for copy in shared_copies(k):
            copy.start()

    chain.finish(0)
    expert_rows(0)
    pl.loop(0, shards // 2)(shared_block)
    chain.step(1)
    pl.loop(shards // 2, shards)(shared_block)
    for step in range(1, chips):
        if step > 1:
            chain.step(step)
        chain.finish(step)
        expert_rows(step)
    join(chips - 1)
    shared_settle(shards - 1)

    @pl.loop(0, shards)
    def _(k):
        for copy in shared_copies(k, True):
            copy.wait_recv()

    for copy in total_copies(chips - 1):
        copy.wait()
    for step in range(max(0, chips - 2), chips):
        for copy in row_copies(step):
            copy.wait()
    for k in range(max(0, units - 2), units):
        for copy in hidden_copies(chips - 1, k, k % 2):
            copy.wait()
    chain.sent()


def middle(h2, cot_low, table_all, cot_all, expert_weights, shared_full, ident):
    length, width = h2.shape
    group, shards = lax.axis_size("expert"), lax.axis_size("shard")
    chips = group // 2
    capacity = 4 * length // group
    hidden_width = expert_weights[0].shape[2]
    block = shared_full[0].shape[1]
    unit = min(512, hidden_width)
    vmem, anywhere = pl.BlockSpec(memory_space=pltpu.VMEM), pl.BlockSpec(memory_space=pl.ANY)
    shape = jax.ShapeDtypeStruct
    both = 2 * capacity
    out_shape = [
        shape((chips, both, width), BF16),
        shape((chips, both, width), BF16),
        shape((chips, both, hidden_width), BF16),
        shape((chips, both, hidden_width), BF16),
        shape((chips, both, hidden_width), BF16),
        shape((chips, length, width), BF16),
        shape((chips, length, width), BF16),
        *[shape((shards, width // 2, block), BF16)] * 2,
        shape((shards, block // 2, width), BF16),
        *[shape((shards, width // 2, block), BF16)] * 2,
        shape((shards, block // 2, width), BF16),
        shape((group, 1, length), F32),
        shape((length, width), F32),
        shape((length, width), F32),
    ]
    dma = pltpu.SemaphoreType.DMA
    scratch = [
        pltpu.VMEM((width, block), BF16),
        pltpu.VMEM((width, block), BF16),
        pltpu.VMEM((block, width), BF16),
        dma((3,)),
        dma((3,)),
        dma((3, shards)),
        pltpu.VMEM((width, hidden_width), BF16),
        pltpu.VMEM((width, hidden_width), BF16),
        pltpu.VMEM((hidden_width, width), BF16),
        pltpu.VMEM((2, width, block), BF16),
        pltpu.VMEM((2, width, block), BF16),
        pltpu.VMEM((2, block, width), BF16),
        pltpu.VMEM((group, length, width), BF16),
        pltpu.VMEM((2, 2, length, width), BF16),
        pltpu.VMEM((2, both, width), BF16),
        pltpu.VMEM((2, both, width), BF16),
        pltpu.VMEM((both, width), BF16),
        pltpu.VMEM((both, 1), F32),
        pltpu.VMEM((both, width), F32),
        pltpu.VMEM((both, width), F32),
        pltpu.VMEM((2, 3, both, unit), BF16),
        pltpu.VMEM((2, length, width), BF16),
        pltpu.VMEM((2, length, width), BF16),
        pltpu.VMEM((2, chips, length, width), BF16),
        pltpu.VMEM((2, length, width), BF16),
        dma((3,)),
        dma((2, 3)),
        dma((2,)),
        dma((2, 2)),
        dma((2, 3)),
        dma((2,)),
        dma((2, chips)),
        dma((2, chips)),
        dma((ChainGather.copies(chips),)),
        dma((ChainGather.copies(chips),)),
        dma,
    ]
    return pl.pallas_call(
        functools.partial(middle_kernel, chips=chips, shards=shards, capacity=capacity),
        out_shape=out_shape,
        in_specs=[vmem] * 3 + [anywhere] * 7,
        out_specs=[anywhere] * 13 + [vmem] * 3,
        scratch_shapes=scratch,
        compiler_params=pltpu.CompilerParams(
            collective_id=ident, has_side_effects=True, vmem_limit_bytes=60 << 20
        ),
    )(h2, cot_low, table_all, cot_all, *expert_weights, *shared_full)


class ChainReduce:
    def __init__(self, own, from_left, from_right, send, recv, at, chips):
        self.own, self.from_left, self.from_right = own, from_left, from_right
        self.send, self.recv, self.at, self.chips = send, recv, at, chips

    @staticmethod
    def scratch(shape):
        return [pltpu.VMEM(shape, BF16)] * 3

    def copy(self, block, right):
        index = block if right else self.chips + block
        landing = self.from_left if right else self.from_right
        return remote(
            self.own.at[block],
            landing.at[block],
            self.send.at[index],
            self.recv.at[index],
            self.at["dev_right" if right else "dev_left"],
        )

    def move(self, step):
        z, chips = self.at["z"], self.chips
        far = chips - step

        @pl.when(z < far)
        def _():
            @pl.when(z > 0)
            def _():
                self.copy(far, True).wait_recv()
                self.own[far] = (self.own[far].astype(F32) + self.from_left[far].astype(F32)).astype(BF16)

            self.copy(far, True).start()

        near = step - 1

        @pl.when(z > near)
        def _():
            @pl.when(z < chips - 1)
            def _():
                self.copy(near, False).wait_recv()
                self.own[near] = (self.own[near].astype(F32) + self.from_right[near].astype(F32)).astype(BF16)

            self.copy(near, False).start()

    def result(self, dst):
        z, chips = self.at["z"], self.chips
        dst[...] += self.own[z].astype(F32)

        @pl.when(z > 0)
        def _():
            self.copy(z, True).wait_recv()
            dst[...] += self.from_left[z].astype(F32)

        @pl.when(z < chips - 1)
        def _():
            self.copy(z, False).wait_recv()
            dst[...] += self.from_right[z].astype(F32)

    def sent(self):
        for step in range(1, self.chips):
            pl.when(self.at["z"] < self.chips - step)(lambda: self.copy(self.chips - step, True).wait_send())
            pl.when(self.at["z"] > step - 1)(lambda: self.copy(step - 1, False).wait_send())


class PlaneReduce:
    COPIES = 6

    def __init__(self, src, got, hold, last, send, recv, at):
        self.src, self.got, self.hold, self.last = src, got, hold, last
        self.send, self.recv, self.at = send, recv, at
        self.half = src.shape[1] // 2

    @staticmethod
    def scratch(shape):
        half = shape[1] // 2
        return [
            pltpu.VMEM((4, half, shape[2]), BF16),
            pltpu.VMEM((2, half, shape[2]), BF16),
            pltpu.VMEM((2, half, shape[2]), BF16),
        ]

    def send_to(self, src, dst, index, device):
        made = remote(src, dst, self.send.at[index], self.recv.at[index], device)
        made.start()
        return made

    def first(self):
        at, half = self.at, self.half
        upper, lower = pl.ds(0, half), pl.ds(half, half)
        self.out = [
            self.send_to(self.src.at[shard, rows, :], self.got.at[slot], slot, device)
            for slot, (shard, rows, device) in enumerate(
                [
                    (at["sx"], upper, at["dev_x"]),
                    (at["sd"], upper, at["dev_x"]),
                    (at["sy"], lower, at["dev_y"]),
                    (at["sd"], lower, at["dev_y"]),
                ]
            )
        ]

    def second(self):
        at, half = self.at, self.half
        for slot, shard, device in ((1, at["sy"], at["dev_y"]), (3, at["sx"], at["dev_x"])):
            self.out[slot].wait_recv()
            turn = slot // 2
            mine = self.src[shard, pl.ds(turn * half, half), :]
            self.hold[turn] = (mine.astype(F32) + self.got[slot].astype(F32)).astype(BF16)
            self.out.append(self.send_to(self.hold.at[turn], self.last.at[turn], 4 + turn, device))

    def value(self, turn):
        half = self.half
        self.out[2 * turn].wait_recv()
        self.out[4 + turn].wait_recv()
        mine = self.src[self.at["shard"], pl.ds(turn * half, half), :]
        return (mine.astype(F32) + self.got[2 * turn].astype(F32)) + self.last[turn].astype(F32)

    def sent(self):
        for made in self.out:
            made.wait_send()


def plane_blocks(at, index, plane):
    if not plane:
        return index
    order = [at["sd"], at["sx"], at["sy"], at["shard"]]
    return sum(jnp.where(index == k, shard, 0) for k, shard in enumerate(order))


def weights_kernel(*refs, plane, chips, shards):
    (rows_ref, grad_ref, dh_ref, hid_hbm, da_hbm, db_hbm, back_hbm), refs = refs[:7], refs[7:]
    (gate_out, up_out, down_out, sum_ref), refs = refs[:4], refs[4:]
    (chunk, own, from_left, from_right), refs = refs[:4], refs[4:]
    own_sem, chunk_sem, chain_send, chain_recv = refs[:4]
    block = chunk.shape[-1]
    at = place()
    chain_meet(at, chips, [at["dev_x"], at["dev_y"]] if plane else [])
    load = pltpu.make_async_copy(back_hbm, own, own_sem)
    load.start()
    if plane:
        send, recv = refs[4:6]
        work = refs[6:]
        reduces = [
            PlaneReduce(work[4 * k], *work[4 * k + 1 : 4 * k + 4], send.at[k], recv.at[k], at) for k in range(2)
        ]
        targets = [work[0], work[4], down_out]
    else:
        targets = [gate_out, up_out, down_out]
    sources = [da_hbm, db_hbm, hid_hbm]

    def fetch(array, index):
        shard = plane_blocks(at, index, plane)
        slot = index % 2
        return pltpu.make_async_copy(
            sources[array].at[:, columns(shard * block, block)], chunk.at[slot], chunk_sem.at[slot]
        )

    def make(array):
        @pl.loop(0, shards)
        def _(index):
            fetch(array, index).wait()
            pl.when(index + 1 < shards)(lambda: fetch(array, index + 1).start())
            if array < 2:
                pl.when(index + 1 == shards)(lambda: fetch(array + 1, 0).start())
            shard = plane_blocks(at, index, plane)
            held = chunk[index % 2]
            if array < 2:
                targets[array][shard] = dot_tn(rows_ref[...], held).astype(BF16)
            else:
                targets[array][shard] = dot_tn(held, grad_ref[...]).astype(BF16)

    fetch(0, 0).start()
    chain = ChainReduce(own, from_left, from_right, chain_send, chain_recv, at, chips)
    load.wait()
    chain.move(1)
    for array in range(3):
        make(array)
        if plane and array < 2:
            reduces[array].first()
        if array == 1:
            for step in range(2, chips - 1):
                chain.move(step)
    if plane:
        reduces[0].second()
    chain.move(chips - 1)
    if plane:
        reduces[1].second()
    sum_ref[...] = dh_ref[...]
    chain.result(sum_ref)
    chain.sent()
    if plane:
        for reduce, out in zip(reduces, (gate_out, up_out)):
            for turn in range(2):
                out[pl.ds(turn * reduce.half, reduce.half), :] = reduce.value(turn)
            reduce.sent()


def weights(rows, grad_rows, shared_back, hidden, gate_grad, up_grad, back_part, ident):
    chips, length, width = back_part.shape
    shards = lax.axis_size("shard")
    plane = shards == 4
    count, hidden_width = hidden.shape
    block = hidden_width // shards
    vmem, anywhere = pl.BlockSpec(memory_space=pltpu.VMEM), pl.BlockSpec(memory_space=pl.ANY)
    shape, dma = jax.ShapeDtypeStruct, pltpu.SemaphoreType.DMA
    wide = (shards, width, block)
    scratch = [pltpu.VMEM((2, count, block), BF16)] + ChainReduce.scratch((chips, length, width))
    scratch += [dma, dma((2,)), dma((2 * chips,)), dma((2 * chips,))]
    if plane:
        out_shape = [shape((width, block), F32)] * 2
        scratch += [dma((2, PlaneReduce.COPIES))] * 2
        scratch += ([pltpu.VMEM(wide, BF16)] + PlaneReduce.scratch(wide)) * 2
    else:
        out_shape = [shape(wide, BF16)] * 2
    out_shape += [shape((shards, block, width), BF16), shape((length, width), F32)]
    return pl.pallas_call(
        functools.partial(weights_kernel, plane=plane, chips=chips, shards=shards),
        out_shape=out_shape,
        in_specs=[vmem] * 3 + [anywhere] * 4,
        out_specs=[vmem] * 4,
        scratch_shapes=scratch,
        compiler_params=pltpu.CompilerParams(
            collective_id=ident, has_side_effects=True, vmem_limit_bytes=60 << 20
        ),
    )(rows, grad_rows, shared_back, hidden, gate_grad, up_grad, back_part)


def norm_back(source, inverse, gain, grad_in):
    scaled = grad_in * gain
    gain_grad = jnp.sum(grad_in * source * inverse, axis=0, keepdims=True)
    input_part = inverse * scaled - source * inverse**3 * jnp.mean(
        scaled * source, axis=-1, keepdims=True
    )
    return (gain_grad, input_part)


def rear_kernel(*refs, plane, chips, shards):
    (prefix, x_ref, cot_ref, resid_ref, dh_ref, gains_ref, rot_ref, att_ref, h1_ref, lse_ref), refs = refs[:10], refs[10:]
    (qkv_ref, out_ref, cos_ref, sin_ref, mix_hbm), refs = refs[:5], refs[5:]
    if plane:
        halves, refs = refs[:6], refs[6:]
    (mix_out, input_grad_ref, qkv_grad_ref, out_grad_ref), refs = refs[:4], refs[4:]
    if plane:
        pieces, refs = refs[:3], refs[3:]
    (bias_ref, dres_ref, datt_ref, dqkv_ref, own, from_left, from_right), refs = refs[:7], refs[7:]
    own_sem, chain_send, chain_recv = refs[:3]
    length, width = x_ref.shape
    at = place()
    chain_meet(at, chips, [at["dev_x"], at["dev_y"]] if plane else [])
    load = pltpu.make_async_copy(mix_hbm, own, own_sem)
    load.start()
    if plane:
        send, recv, half_sem = refs[3:6]
        work = [refs[6 + 5 * k : 11 + 5 * k] for k in range(3)]
        loads = [
            [
                pltpu.make_async_copy(halves[2 * k + n], work[k][n], half_sem.at[k, n])
                for n in range(2)
            ]
            for k in range(3)
        ]
        for two in loads:
            for made in two:
                made.start()
        reduces = [PlaneReduce(work[k][0], *work[k][2:], send.at[k], recv.at[k], at) for k in range(3)]
    chain = ChainReduce(own, from_left, from_right, chain_send, chain_recv, at, chips)
    load.wait()
    chain.move(1)
    if plane:
        for k in range(3):
            for made in loads[k]:
                made.wait()

            @pl.loop(0, shards)
            def _(shard):
                work[k][0][shard] = (
                    work[k][0][shard].astype(F32) + work[k][1][shard].astype(F32)
                ).astype(BF16)

            reduces[k].first()
    blocks = gains_ref.shape[0] // 64
    gain_one = sum(gains_ref[pl.ds(64 * k, 1), :].astype(F32) for k in range(blocks))
    gain_two = sum(gains_ref[pl.ds(64 * k + 32, 1), :].astype(F32) for k in range(blocks))
    resid = resid_ref[...]
    inverse = lax.rsqrt(jnp.mean(resid * resid, axis=-1, keepdims=True) + EPS)
    gain_two_grad, extra = norm_back(resid, inverse, gain_two, dh_ref[...])
    dres = cot_ref[...] + extra
    dres_ref[...] = dres
    low = dres.astype(BF16)
    datt_ref[...] = dot_nt(low, out_ref[...]).astype(BF16)
    out_grad = dot_tn(att_ref[...], low).astype(BF16)
    rows = width // shards
    for k in range(shards):
        out_grad_ref[k, :rows, :] = out_grad[k * rows : (k + 1) * rows]
    row = lax.broadcasted_iota(jnp.int32, (length, length), 0)
    col = lax.broadcasted_iota(jnp.int32, (length, length), 1)
    bias_ref[...] = jnp.where((col < prefix[0]) | (col <= row), 0.0, -1e30)
    scale = HEAD_DIM**-0.5

    def pair(j):
        cols = columns(j * 128, 128)
        queries, keys, values = (
            rot_ref[:, columns(part * width + j * 128, 128)] for part in range(3)
        )
        grads = datt_ref[:, cols]
        low_lanes = lax.broadcasted_iota(jnp.int32, (length, 128), 1) < HEAD_DIM
        lanes = lax.broadcasted_iota(jnp.int32, (length, 128), 1)
        parts = []
        for head in range(2):
            mine = low_lanes if head == 0 else ~low_lanes
            query = jnp.where(mine, queries, 0.0) * scale
            grad = jnp.where(mine, grads, 0.0).astype(BF16)
            logsum = jnp.sum(jnp.where(lanes == 2 * j + head, lse_ref[...], 0.0), axis=1, keepdims=True)
            probs = jnp.exp(dot_nt(query.astype(BF16), keys) + bias_ref[...] - logsum)
            probs_grad = dot_nt(grad, values)
            inner = jnp.sum(probs * probs_grad, axis=-1, keepdims=True)
            score_grad = (probs * (probs_grad - inner)).astype(BF16)
            parts.append(
                (
                    dot_nn(score_grad, keys) * scale,
                    dot_tn(score_grad, queries) * scale,
                    dot_tn(probs.astype(BF16), grads),
                )
            )
        for part in range(3):
            both = jnp.where(low_lanes, parts[0][part], parts[1][part])
            if part < 2:
                both = both * cos_ref[...] - partner(both) * sin_ref[...]
            dqkv_ref[:, columns(part * width + j * 128, 128)] = both.astype(BF16)

    pairs = width // 128
    pl.loop(0, pairs // 2)(pair)
    for step in range(2, chips - 1):
        chain.move(step)
    if plane:
        reduces[0].second()
    pl.loop(pairs // 2, pairs)(pair)
    chain.move(chips - 1)
    if plane:
        reduces[1].second()
        reduces[2].second()

    @pl.loop(0, 3 * width // 256)
    def _(k):
        cols = columns(k * 256, 256)
        qkv_grad_ref[:, cols] = dot_tn(h1_ref[...], dqkv_ref[:, cols]).astype(BF16)

    dh1 = dot_nt(dqkv_ref[...], qkv_ref[...])
    x = x_ref[...]
    inverse = lax.rsqrt(jnp.mean(x * x, axis=-1, keepdims=True) + EPS)
    gain_one_grad, extra = norm_back(x, inverse, gain_one, dh1)
    input_grad_ref[...] = dres_ref[...] + extra
    index = lax.broadcasted_iota(jnp.int32, (64, width), 0)
    gain_rows = jnp.where(index == 0, gain_one_grad, jnp.where(index == 1, gain_two_grad, 0.0)).astype(BF16)
    for k in range(shards):
        out_grad_ref[k, rows:, :] = gain_rows
    mix_out[...] = jnp.zeros_like(mix_out)
    chain.result(mix_out)
    chain.sent()
    if plane:
        for reduce, piece in zip(reduces, pieces):
            count = piece.shape[1]
            both = jnp.concatenate([reduce.value(0), reduce.value(1)], axis=0)
            for k in range(chips):
                piece[k] = both[k * count : (k + 1) * count].astype(BF16)
            reduce.sent()


def rear(prefix, inputs, cotangent, resid, dh2, gains_full, kept, full, mix_part, halves, ident):
    length, width = inputs.shape
    chips, shards = mix_part.shape[0], lax.axis_size("shard")
    plane = shards == 4
    cosine, sine = rope_lanes(length)
    vmem, anywhere = pl.BlockSpec(memory_space=pltpu.VMEM), pl.BlockSpec(memory_space=pl.ANY)
    shape, dma = jax.ShapeDtypeStruct, pltpu.SemaphoreType.DMA
    operands = [prefix, inputs, cotangent, resid, dh2, gains_full, *kept, *full, cosine, sine, mix_part]
    in_specs = [pl.BlockSpec(memory_space=pltpu.SMEM)] + [vmem] * 13 + [anywhere]
    out_shape = [
        shape((length, width), F32),
        shape((length, width), F32),
        shape((width, 3 * width), BF16),
        shape((shards, width // shards + 64, width), BF16),
    ]
    scratch = [
        pltpu.VMEM((length, length), F32),
        pltpu.VMEM((length, width), F32),
        pltpu.VMEM((length, width), BF16),
        pltpu.VMEM((length, 3 * width), BF16),
        *ChainReduce.scratch((chips, length, width)),
        dma,
        dma((2 * chips,)),
        dma((2 * chips,)),
    ]
    if plane:
        operands += halves
        in_specs += [anywhere] * 6
        scratch += [dma((3, PlaneReduce.COPIES))] * 2 + [dma((3, 2))]
        for half in halves[::2]:
            out_shape.append(shape((chips, half.shape[1] // chips, half.shape[2]), BF16))
            scratch += [pltpu.VMEM(half.shape, BF16)] * 2 + PlaneReduce.scratch(half.shape)
    return pl.pallas_call(
        functools.partial(rear_kernel, plane=plane, chips=chips, shards=shards),
        out_shape=out_shape,
        in_specs=in_specs,
        out_specs=[vmem] * len(out_shape),
        scratch_shapes=scratch,
        compiler_params=pltpu.CompilerParams(
            collective_id=ident, has_side_effects=True, vmem_limit_bytes=60 << 20
        ),
    )(*operands)


def last_kernel(*refs, chips, shards):
    (resid_ref, mix_ref, sy_ref), refs = refs[:3], refs[3:]
    attention, pieces, down_hbm, refs = refs[:2], refs[2:5], refs[5], refs[6:]
    output_ref, grads, refs = refs[0], refs[1:7], refs[7:]
    halves, refs = refs[:4], refs[4:]
    plane_work, refs = refs[:10], refs[10:]
    chain_work, refs = refs[:25], refs[25:]
    load_sem, core_send, core_recv, plane_send, plane_recv, sums_send, sums_recv, all_send, all_recv, all_local = refs
    at = place()
    core = at["core"]
    chain_meet(at, chips, [at["dev_x"], at["dev_y"], at["dev_c"]])
    swaps, loads = [], []
    for k in range(2):
        rows = attention[k].shape[1] // 2
        part = lambda c: attention[k].at[:, pl.ds(pl.multiple_of(c * rows, 16), rows), :]
        swaps.append(
            remote(part(1 - core), halves[2 * k + 1], core_send.at[k], core_recv.at[k], at["dev_c"])
        )
        loads.append(pltpu.make_async_copy(part(core), halves[2 * k], load_sem.at[k]))
    chain_work = [chain_work[5 * k : 5 * k + 5] for k in range(5)]
    loads += [pltpu.make_async_copy(pieces[k], chain_work[2 + k][0], load_sem.at[2 + k]) for k in range(3)]
    loads.append(pltpu.make_async_copy(down_hbm, plane_work[0], load_sem.at[5]))
    for made in swaps + loads:
        made.start()
    sums = [
        ChainReduce(*chain_work[k][:3], sums_send.at[k], sums_recv.at[k], at, chips) for k in range(5)
    ]
    alls = [
        ChainGather(chain_work[k][3], chain_work[k][4], all_send.at[k], all_recv.at[k], all_local.at[k], at, chips)
        for k in range(5)
    ]
    planes = [
        PlaneReduce(src, *plane_work[1 + 3 * k : 4 + 3 * k], plane_send.at[k], plane_recv.at[k], at)
        for k, src in enumerate([plane_work[0], halves[0], halves[2]])
    ]
    ahead = (2, 3, 4)
    for k in ahead:
        loads[k].wait()
        sums[k].move(1)
    for k in range(2):
        swaps[k].wait()
        loads[k].wait()

        @pl.loop(0, shards)
        def _(shard):
            halves[2 * k][shard] = (
                halves[2 * k][shard].astype(F32) + halves[2 * k + 1][shard].astype(F32)
            ).astype(BF16)

        planes[1 + k].first()
    loads[5].wait()
    planes[0].first()
    output_ref[...] = resid_ref[...] + mix_ref[...] + sy_ref[...]
    for step in range(2, chips):
        for k in ahead:
            sums[k].move(step)
        if step == 2:
            planes[1].second()
            planes[2].second()

    def total(k):
        total_ref = chain_work[k][3]
        z = at["z"]
        value = sums[k].own[z].astype(F32)
        pl.when(z > 0)(lambda: sums[k].copy(z, True).wait_recv())
        pl.when(z < chips - 1)(lambda: sums[k].copy(z, False).wait_recv())
        value += jnp.where(z > 0, sums[k].from_left[z].astype(F32), 0.0)
        value += jnp.where(z < chips - 1, sums[k].from_right[z].astype(F32), 0.0)
        total_ref[...] = value.astype(BF16)
        alls[k].start()

    for k in ahead:
        total(k)
    for k in range(2):
        count = chain_work[k][0].shape[1]
        both = jnp.concatenate([planes[1 + k].value(0), planes[1 + k].value(1)], axis=0)
        for n in range(chips):
            sums[k].own[n] = both[n * count : (n + 1) * count].astype(BF16)
        sums[k].move(1)
    for step in range(2, chips):
        for k in range(2):
            sums[k].move(step)
        for k in ahead:
            alls[k].step(step - 1)
    for k in range(2):
        total(k)
    for k in ahead:
        alls[k].step(chips - 1)
    planes[0].second()
    for step in range(1, chips):
        for k in range(2):
            alls[k].step(step)

    def spread(k):
        for step in range(chips):
            alls[k].finish(step)
        alls[k].sent()
        sums[k].sent()
        count = chain_work[k][0].shape[1]
        for n in range(chips):
            for c in range(2):
                grads[k][pl.ds((c * chips + n) * count, count), :] = chain_work[k][4][2 * n + c].astype(F32)

    for k in ahead:
        spread(k)
    for turn in range(2):
        grads[5][pl.ds(turn * planes[0].half, planes[0].half), :] = planes[0].value(turn)
    for k in range(2):
        spread(k)
    for reduce in planes:
        reduce.sent()


def last(resid, mixture, shared_out, qkv_grad, out_grad, pieces, down_blocks, ident):
    length, width = resid.shape
    shards, chips = lax.axis_size("shard"), lax.axis_size("expert") // 2
    vmem, anywhere = pl.BlockSpec(memory_space=pltpu.VMEM), pl.BlockSpec(memory_space=pl.ANY)
    shape, dma = jax.ShapeDtypeStruct, pltpu.SemaphoreType.DMA
    attention = [qkv_grad, out_grad]
    half_shapes = [(shards, v.shape[1] // 2, v.shape[2]) for v in attention]
    chain_shapes = [(chips, v.shape[1] // 2 // chips, v.shape[2]) for v in attention] + [v.shape for v in pieces]
    out_shape = [shape((length, width), F32)]
    out_shape += [shape((2 * s[0] * s[1], s[2]), F32) for s in chain_shapes]
    out_shape.append(shape(down_blocks.shape[1:], F32))
    scratch = []
    for s in half_shapes:
        scratch += [pltpu.VMEM(s, BF16)] * 2
    scratch.append(pltpu.VMEM(down_blocks.shape, BF16))
    for s in [down_blocks.shape] + half_shapes:
        scratch += PlaneReduce.scratch(s)
    for s in chain_shapes:
        scratch += ChainReduce.scratch(s)
        scratch += [pltpu.VMEM(s[1:], BF16), pltpu.VMEM((2 * chips,) + s[1:], BF16)]
    scratch += [
        dma((6,)),
        dma((2,)),
        dma((2,)),
        dma((3, PlaneReduce.COPIES)),
        dma((3, PlaneReduce.COPIES)),
        dma((5, 2 * chips)),
        dma((5, 2 * chips)),
        dma((5, ChainGather.copies(chips))),
        dma((5, ChainGather.copies(chips))),
        dma((5,)),
    ]
    return pl.pallas_call(
        functools.partial(last_kernel, chips=chips, shards=shards),
        out_shape=out_shape,
        in_specs=[vmem] * 3 + [anywhere] * 6,
        out_specs=[vmem] * 7,
        scratch_shapes=scratch,
        compiler_params=pltpu.CompilerParams(
            collective_id=ident, has_side_effects=True, vmem_limit_bytes=60 << 20
        ),
    )(resid, mixture, shared_out, qkv_grad, out_grad, *pieces, down_blocks)


def on_device(
    inputs,
    cotangent,
    norm_one,
    qkv_weight,
    out_weight,
    norm_two,
    shared_gate,
    shared_up,
    shared_down,
    expert_gate,
    expert_up,
    expert_down,
    gate_weights,
    routes,
    prefix,
):
    length, width = inputs.shape
    experts, shards = lax.axis_size("expert"), lax.axis_size("shard")
    me, shard = lax.axis_index("expert"), lax.axis_index("shard")
    gains = jnp.concatenate(
        [jnp.broadcast_to(v, (32, v.shape[0])) for v in (norm_one, norm_two)], axis=0
    )
    gains = lax.dynamic_update_slice(
        jnp.zeros((64, width), BF16), gains, (0, shard * norm_one.shape[0])
    )
    (
        cot_all,
        table_all,
        normed_one,
        turned,
        attended,
        logsum,
        resid,
        normed_two,
        cot_low,
        qkv_full,
        out_full,
        gains_full,
        gate_blocks,
        up_blocks,
        down_full,
    ) = front(
        prefix,
        inputs,
        cotangent,
        routes.T,
        gate_weights.T,
        qkv_weight,
        out_weight,
        gains,
        [shared_gate, shared_up, shared_down],
        1,
    )
    (
        rows,
        grad_rows,
        hidden,
        gate_pre_grad,
        up_pre_grad,
        mix_part,
        back_part,
        *shared_halves,
        weight_back,
        shared_out,
        shared_back,
    ) = middle(
        normed_two,
        cot_low,
        table_all,
        cot_all,
        [expert_gate, expert_up, expert_down],
        [gate_blocks, up_blocks, down_full],
        2,
    )
    shared_halves = [shared_halves[k + n] for k in range(3) for n in (0, 3)]
    weight_got = lax.all_to_all(
        weight_back.reshape(experts, length), "expert", split_axis=0, concat_axis=0, tiled=True
    )
    chosen = routes[:, :, None] == jnp.arange(experts, dtype=jnp.int32)[None, None, :]
    gate_weights_grad = jnp.sum(jnp.where(chosen, weight_got.T[:, None, :], 0.0), axis=2)
    rows, grad_rows, hidden, gate_pre_grad, up_pre_grad = (
        v.reshape(-1, v.shape[-1]) for v in (rows, grad_rows, hidden, gate_pre_grad, up_pre_grad)
    )
    gate_term, up_term, down_term, normed_two_grad = weights(
        rows, grad_rows, shared_back, hidden, gate_pre_grad, up_pre_grad, back_part, 3
    )
    mixture, input_grad, qkv_grad, out_grad, *pieces = rear(
        prefix,
        inputs,
        cotangent,
        resid,
        normed_two_grad,
        gains_full,
        [turned, attended, normed_one, logsum],
        [qkv_full, out_full],
        mix_part,
        shared_halves,
        4,
    )
    qkv_grad = qkv_grad.reshape(shards, width // shards, 3 * width)
    if shards == 4:
        output, qkv_sum, out_sum, *shared_sums, down_term = last(
            resid, mixture, shared_out, qkv_grad, out_grad, pieces, down_term, 5
        )
    else:

        def over_plane(value):
            return lax.psum_scatter(value, "shard", scatter_dimension=0, tiled=True)[0]

        def over_all(value):
            return lax.psum(over_plane(value), "expert").astype(F32)

        output = resid + mixture + shared_out
        gate_term, up_term, down_term = (
            over_plane(v).astype(F32) for v in (gate_term, up_term, down_term)
        )
        qkv_sum, out_sum = over_all(qkv_grad), over_all(out_grad)
        shared_sums = []
        for own, got in zip(shared_halves[::2], shared_halves[1::2]):
            half = (own.astype(F32) + got.astype(F32)).astype(BF16)
            both = jnp.concatenate([jnp.where(me % 2 == c, half, 0) for c in range(2)], axis=1)
            shared_sums.append(over_all(both))
    part = width // shards
    gain_grads = lax.dynamic_slice(out_sum[part : part + 2], (0, shard * part), (2, part))
    return (
        output,
        input_grad,
        gain_grads[0],
        qkv_sum,
        out_sum[:part],
        gain_grads[1],
        *shared_sums,
        gate_term[None],
        up_term[None],
        down_term[None],
        gate_weights_grad,
    )


def solution(mesh):
    tokens = P(("expert", "shard"), None)
    in_specs = (
        tokens,
        tokens,
        P("shard"),
        P("shard", None),
        P("shard", None),
        P("shard"),
        P(None, "shard"),
        P(None, "shard"),
        P("shard", None),
        P("expert", None, None),
        P("expert", None, None),
        P("expert", None, None),
        tokens,
        tokens,
        P(("expert", "shard")),
    )
    out_specs = (
        tokens,
        tokens,
        P("shard"),
        P("shard", None),
        P("shard", None),
        P("shard"),
        P(None, "shard"),
        P(None, "shard"),
        P("shard", None),
        P("expert", None, "shard"),
        P("expert", None, "shard"),
        P("expert", "shard", None),
        tokens,
    )
    return jax.shard_map(
        on_device, mesh=mesh, in_specs=in_specs, out_specs=out_specs, check_vma=False
    )
```

```python
import functools

import jax
import jax.numpy as jnp
import numpy as np
from jax import lax
from jax.experimental import pallas as pl
from jax.experimental.pallas import tpu as pltpu
from jax.sharding import PartitionSpec as P

HEADS = 12
HEAD_DIM = 64
TOP = 2
EPS = 1e-06
MESH = pl.DeviceIdType.MESH
F32 = jnp.float32
BF16 = jnp.bfloat16
VMEM_BYTES = 61 << 20


def place():
    expert, shard = lax.axis_index("expert"), lax.axis_index("shard")
    core, x, y = expert % 2, shard % 2, shard // 2
    return dict(
        expert=expert,
        shard=shard,
        core=core,
        z=expert // 2,
        sx=2 * y + 1 - x,
        sy=2 * (1 - y) + x,
        sd=2 * (1 - y) + 1 - x,
        dev_x=(expert, 2 * y + 1 - x),
        dev_y=(expert, 2 * (1 - y) + x),
        dev_c=(expert + 1 - 2 * core, shard),
        dev_left=(expert - 2, shard),
        dev_right=(expert + 2, shard),
    )


def meet(devices):
    barrier = pltpu.get_barrier_semaphore()
    for device in devices:
        pl.semaphore_signal(barrier, inc=1, device_id=device, device_id_type=MESH)
    pl.semaphore_wait(barrier, len(devices))


def remote(src, dst, send, recv, device):
    return pltpu.make_async_remote_copy(
        src_ref=src, dst_ref=dst, send_sem=send, recv_sem=recv, device_id=device, device_id_type=MESH
    )


class PlaneGather:
    COPIES = 7

    def __init__(self, src, dst, send, recv, local, at):
        self.src, self.dst, self.at = src, dst, at
        self.send, self.recv, self.local = send, recv, local
        self.rows = src.shape[0]
        self.copies = []

    def view(self, shard, start, count):
        return self.dst.at[pl.ds(pl.multiple_of(shard * self.rows + start, 16), count), :]

    def copy(self, part, index, device):
        made = remote(part, part, self.send.at[index], self.recv.at[index], device)
        made.start()
        self.copies.append(made)

    def load(self):
        self.own = pltpu.make_async_copy(self.src, self.view(self.at["shard"], 0, self.rows), self.local)
        self.own.start()

    def first(self):
        at, half = self.at, self.rows // 2
        self.own.wait()
        part = self.view(at["shard"], at["core"] * half, half)
        self.copy(part, 0, at["dev_x"])
        self.copy(part, 1, at["dev_y"])

    def second(self):
        at, half, quarter = self.at, self.rows // 2, self.rows // 4
        start = at["core"] * half
        self.copies[0].wait_recv()
        self.copy(self.view(at["sx"], start, quarter), 2, at["dev_y"])
        self.copy(self.view(at["sx"], start, half), 3, at["dev_c"])
        self.copies[1].wait_recv()
        self.copy(self.view(at["sy"], start + quarter, quarter), 4, at["dev_x"])
        self.copy(self.view(at["sy"], start, half), 5, at["dev_c"])

    def third(self):
        at, half = self.at, self.rows // 2
        self.copies[2].wait_recv()
        self.copies[4].wait_recv()
        self.copy(self.view(at["sd"], at["core"] * half, half), 6, at["dev_c"])

    def finish(self):
        for index in (3, 5, 6):
            self.copies[index].wait_recv()
        for made in self.copies:
            made.wait_send()


class ChainGather:
    @staticmethod
    def copies(chips):
        return 4 * chips

    def __init__(self, src, dst, send, recv, local, at, chips):
        self.src, self.dst, self.send, self.recv, self.local = src, dst, send, recv, local
        self.at, self.chips = at, chips

    def copy(self, block, index, device, first=False):
        part = self.dst.at[block]
        return remote(
            self.src if first else part, part, self.send.at[index], self.recv.at[index], self.at[device]
        )

    def right(self, step):
        at = self.at
        return self.copy((at["z"] - step + 1) * 2 + at["core"], step - 1, "dev_right", step == 1)

    def left(self, step):
        at = self.at
        return self.copy(
            (at["z"] + step - 1) * 2 + at["core"], self.chips + step - 1, "dev_left", step == 1
        )

    def over(self, step):
        at = self.at
        return self.copy(
            (at["z"] - step) * 2 + at["core"], (2 if step >= 0 else 3) * self.chips + abs(step), "dev_c", step == 0
        )

    def arrived(self, step, side):
        at = self.at
        if side == "left":
            return self.copy((at["z"] - step) * 2 + at["core"], step - 1, "dev_right")
        return self.copy((at["z"] + step) * 2 + at["core"], self.chips + step - 1, "dev_left")

    def start(self):
        at = self.at
        pl.when(at["z"] < self.chips - 1)(lambda: self.right(1).start())
        pl.when(at["z"] > 0)(lambda: self.left(1).start())
        self.over(0).start()
        self.own = pltpu.make_async_copy(self.src, self.dst.at[at["expert"]], self.local)
        self.own.start()

    def step(self, step):
        at, chips = self.at, self.chips

        @pl.when(at["z"] - step >= 0)
        def _():
            self.arrived(step, "left").wait_recv()
            if step < chips - 1:
                pl.when(at["z"] < chips - 1)(lambda: self.right(step + 1).start())
            self.over(step).start()

        @pl.when(at["z"] + step < chips)
        def _():
            self.arrived(step, "right").wait_recv()
            if step < chips - 1:
                pl.when(at["z"] > 0)(lambda: self.left(step + 1).start())
            self.over(-step).start()

    def finish(self, step):
        at = self.at
        if step == 0:
            self.over(0).wait()
            self.own.wait()
            return
        pl.when(at["z"] - step >= 0)(lambda: self.over(step).wait())
        pl.when(at["z"] + step < self.chips)(lambda: self.over(-step).wait())

    def sent(self):
        at, chips = self.at, self.chips
        for step in range(1, chips):
            pl.when((at["z"] - step + 1 >= 0) & (at["z"] < chips - 1))(lambda: self.right(step).wait_send())
            pl.when((at["z"] + step - 1 < chips) & (at["z"] > 0))(lambda: self.left(step).wait_send())


def chain_meet(at, chips, others):
    barrier = pltpu.get_barrier_semaphore()
    for device in others:
        pl.semaphore_signal(barrier, inc=1, device_id=device, device_id_type=MESH)

    @pl.when(at["z"] > 0)
    def _():
        pl.semaphore_signal(barrier, inc=1, device_id=at["dev_left"], device_id_type=MESH)

    @pl.when(at["z"] < chips - 1)
    def _():
        pl.semaphore_signal(barrier, inc=1, device_id=at["dev_right"], device_id_type=MESH)

    ends = jnp.where(at["z"] == 0, 1, 0) + jnp.where(at["z"] == chips - 1, 1, 0)
    pl.semaphore_wait(barrier, len(others) + 2 - ends)


def dot_nn(left, right):
    return lax.dot_general(left, right, (((1,), (0,)), ((), ())), preferred_element_type=F32)


def dot_nt(left, right):
    return lax.dot_general(left, right, (((1,), (1,)), ((), ())), preferred_element_type=F32)


def dot_tn(left, right):
    return lax.dot_general(left, right, (((0,), (0,)), ((), ())), preferred_element_type=F32)


def columns(start, count):
    return pl.ds(pl.multiple_of(start, 128), count)


def rope_lanes(length):
    half = HEAD_DIM // 2
    frequency = 10000.0 ** (-np.arange(half) * 2.0 / HEAD_DIM)
    angles = np.arange(length)[:, None] * frequency[None, :]
    cosine, sine = np.cos(angles), np.sin(angles)
    return (
        jnp.asarray(np.concatenate([cosine] * 4, axis=1), F32),
        jnp.asarray(np.concatenate([-sine, sine] * 2, axis=1), F32),
    )


def partner(values):
    lane = lax.broadcasted_iota(jnp.int32, values.shape, 1)
    half = HEAD_DIM // 2
    ahead = pltpu.roll(values, 128 - half, 1)
    behind = pltpu.roll(values, half, 1)
    return jnp.where(lane % HEAD_DIM < half, ahead, behind)


def set_bias(bias_ref, prefix):
    shape = bias_ref.shape
    row = lax.broadcasted_iota(jnp.int32, shape, 0)
    col = lax.broadcasted_iota(jnp.int32, shape, 1)
    bias_ref[...] = jnp.where((col < prefix[0]) | (col <= row), 0.0, -1e30)


def two_heads(values):
    low = lax.broadcasted_iota(jnp.int32, values.shape, 1) < HEAD_DIM
    zero = jnp.zeros_like(values)
    return jnp.concatenate([jnp.where(low, values, zero), jnp.where(low, zero, values)], axis=0)


def front_kernel(*refs, plane, chips):
    (prefix, x_ref, cot_ref, route_ref, weight_ref, cos_ref, sin_ref), refs = refs[:7], refs[7:]
    (one_ref, two_ref), refs = refs[:2], refs[2:]
    weights, refs = (refs[:5], refs[5:]) if plane else (refs[:2], refs[2:])
    (cot_out, table_out, h1_ref, rot_ref, att_ref, lse_ref, resid_ref, h2_ref, cot_low, gains_ref), refs = refs[:10], refs[10:]
    full_out, refs = (refs[:5], refs[5:]) if plane else ([], refs)
    (bias_ref, table_ref, table_all, cot_all, out_sem, chain_send, chain_recv, chain_local), refs = refs[:8], refs[8:]
    length, width = x_ref.shape
    experts = table_ref.shape[0] // 2
    at = place()
    if plane:
        gains_src, gains_full, full, (send, recv, local, full_sem) = refs[0], refs[1], refs[2:7], refs[7:]
        gathers = [
            PlaneGather(a, b, send.at[k], recv.at[k], local.at[k], at)
            for k, (a, b) in enumerate(zip([*weights, gains_src], [*full, gains_full]))
        ]
        first, later = [gathers[5], gathers[1], gathers[0]], gathers[2:5]
        gains_src[:32, :] = jnp.broadcast_to(one_ref[...], (32, one_ref.shape[1]))
        gains_src[32:, :] = jnp.broadcast_to(two_ref[...], (32, two_ref.shape[1]))
        for gather in first + later:
            gather.load()
        qkv_full, out_full = full[:2]
    else:
        qkv_full, out_full = weights
    chain_meet(at, chips, [at["dev_x"], at["dev_y"], at["dev_c"]] if plane else [at["dev_c"]])
    if plane:
        for gather in first:
            gather.first()
    cot_low[...] = cot_ref[...].astype(BF16)
    names = lax.broadcasted_iota(jnp.int32, (experts, length), 0)
    chosen = [route_ref[pl.ds(k, 1), :] == names for k in range(TOP)]
    member = (chosen[0] | chosen[1]).astype(F32)
    earlier = (
        lax.broadcasted_iota(jnp.int32, (length, length), 0)
        < lax.broadcasted_iota(jnp.int32, (length, length), 1)
    ).astype(F32)
    slot = dot_nn(member.astype(BF16), earlier.astype(BF16))
    table_ref[:experts, :] = jnp.where(member > 0, slot, -1.0)
    table_ref[experts:, :] = sum(
        jnp.where(chosen[k], weight_ref[pl.ds(k, 1), :], 0.0) for k in range(TOP)
    )
    chains = [
        ChainGather(a, b, chain_send.at[k], chain_recv.at[k], chain_local.at[k], at, chips)
        for k, (a, b) in enumerate([(table_ref, table_all), (cot_low, cot_all)])
    ]
    for chain in chains:
        chain.start()
    set_bias(bias_ref, prefix)
    if plane:
        for step in ("second", "third", "finish"):
            for gather in first:
                getattr(gather, step)()
        for gather in later:
            gather.first()
        outs = [pltpu.make_async_copy(a, b, full_sem.at[k]) for k, (a, b) in enumerate(zip(full, full_out))]
        for made in outs[:2]:
            made.start()
        blocks = range(gains_full.shape[0] // 64)
        for k in range(2):
            row = [gains_full[pl.ds(64 * n + 32 * k, 1), :].astype(F32) for n in blocks]
            gains_ref[pl.ds(k, 1), :] = jnp.concatenate(row, axis=1)
    else:
        gains_ref[pl.ds(0, 1), :] = one_ref[...].astype(F32)
        gains_ref[pl.ds(1, 1), :] = two_ref[...].astype(F32)
    x = x_ref[...]
    inverse = lax.rsqrt(jnp.mean(x * x, axis=-1, keepdims=True) + EPS)
    h1_ref[...] = (x * inverse * gains_ref[pl.ds(0, 1), :]).astype(BF16)

    def project(block, turned):
        cols = columns(block * 256, 256)
        part = dot_nn(h1_ref[...], qkv_full[:, cols])
        if turned:
            part = jnp.concatenate(
                [v * cos_ref[...] + partner(v) * sin_ref[...] for v in (part[:, :128], part[:, 128:])], axis=1
            )
        rot_ref[:, cols] = part.astype(BF16)

    pl.loop(0, 2 * width // 256)(lambda block: project(block, True))
    pl.loop(2 * width // 256, 3 * width // 256)(lambda block: project(block, False))
    for chain in chains:
        chain.step(1)
    lse_ref[...] = jnp.zeros_like(lse_ref)
    count = length // 2

    def pair(j):
        queries, keys, values = (
            rot_ref[:, columns(part * width + j * 128, 128)] for part in range(3)
        )
        low = lax.broadcasted_iota(jnp.int32, (count, 128), 1) < HEAD_DIM
        lanes = lax.broadcasted_iota(jnp.int32, (count, 128), 1)
        for start in range(0, length, count):
            rows, seen = pl.ds(start, count), start + count
            scores = dot_nt(two_heads(queries[start:seen] * HEAD_DIM**-0.5), keys[:seen])
            bias = bias_ref[rows, :seen]
            scores = jnp.concatenate([scores[:count] + bias, scores[count:] + bias], axis=0)
            peak = jnp.max(scores, axis=-1, keepdims=True)
            exponent = jnp.exp(scores - peak)
            total = jnp.sum(exponent, axis=-1, keepdims=True)
            out = dot_nn(exponent.astype(BF16), values[:seen]) * (1.0 / total)
            att_ref[rows, columns(j * 128, 128)] = jnp.where(low, out[:count], out[count:]).astype(BF16)
            logsum = peak + jnp.log(total)
            lse_ref[rows, :] = jnp.where(
                lanes == 2 * j,
                logsum[:count],
                jnp.where(lanes == 2 * j + 1, logsum[count:], lse_ref[rows, :]),
            )

    pairs = width // 128
    pl.loop(0, pairs // 2)(pair)
    for step in range(2, chips - 1):
        for chain in chains:
            chain.step(step)
    pl.loop(pairs // 2, pairs)(pair)
    if plane:
        for gather in later:
            gather.second()
    resid = x_ref[...] + dot_nn(att_ref[...], out_full[...])
    resid_ref[...] = resid
    inverse = lax.rsqrt(jnp.mean(resid * resid, axis=-1, keepdims=True) + EPS)
    h2_ref[...] = (resid * inverse * gains_ref[pl.ds(1, 1), :]).astype(BF16)
    for chain in chains:
        chain.step(chips - 1)
    if plane:
        for step in ("third", "finish"):
            for gather in later:
                getattr(gather, step)()
        for made in outs[2:]:
            made.start()
    for chain in chains:
        for step in range(chips):
            chain.finish(step)
    keep = [
        pltpu.make_async_copy(a, b, out_sem.at[k])
        for k, (a, b) in enumerate([(table_all, table_out), (cot_all, cot_out)])
    ]
    for made in keep:
        made.start()
    for chain in chains:
        chain.sent()
    for made in keep + (outs if plane else []):
        made.wait()


def front(prefix, inputs, cotangent, route_rows, weight_rows, gains, weights, ident):
    length, width = inputs.shape
    group, shards = lax.axis_size("expert"), lax.axis_size("shard")
    chips, plane = group // 2, shards == 4
    cosine, sine = rope_lanes(length)
    vmem, anywhere = pl.BlockSpec(memory_space=pltpu.VMEM), pl.BlockSpec(memory_space=pl.ANY)
    gains = [v[None, :] for v in gains]
    if not plane:
        gains = [lax.all_gather(v, "shard", axis=1, tiled=True) for v in gains]
        weights = [lax.all_gather(v, "shard", axis=0, tiled=True) for v in weights]
    operands = [prefix, inputs, cotangent, route_rows, weight_rows, cosine, sine, *gains]
    in_specs = [pl.BlockSpec(memory_space=pltpu.SMEM)] + [vmem] * 8
    operands += weights if plane else weights[:2]
    in_specs += [anywhere] * 5 if plane else [vmem] * 2
    shape, dma = jax.ShapeDtypeStruct, pltpu.SemaphoreType.DMA
    out_shape = [
        shape((group, length, width), BF16),
        shape((group, 2 * group, length), F32),
        shape((length, width), BF16),
        shape((length, 3 * width), BF16),
        shape((length, width), BF16),
        shape((length, 128), F32),
        shape((length, width), F32),
        shape((length, width), BF16),
        shape((length, width), BF16),
        shape((8, width), F32),
    ]
    out_specs = [anywhere] * 2 + [vmem] * 8
    scratch = [
        pltpu.VMEM((length, length), F32),
        pltpu.VMEM((2 * group, length), F32),
        pltpu.VMEM((group, 2 * group, length), F32),
        pltpu.VMEM((group, length, width), BF16),
        dma((2,)),
        dma((2, ChainGather.copies(chips))),
        dma((2, ChainGather.copies(chips))),
        dma((2,)),
    ]
    if plane:
        full = [(shards * v.shape[0], v.shape[1]) for v in weights]
        out_shape += [shape(s, BF16) for s in full]
        out_specs += [anywhere] * 5
        part = gains[0].shape[1]
        scratch += [pltpu.VMEM((64, part), BF16), pltpu.VMEM((64 * shards, part), BF16)]
        scratch += [pltpu.VMEM(s, BF16) for s in full]
        scratch += [dma((6, PlaneGather.COPIES)), dma((6, PlaneGather.COPIES)), dma((6,)), dma((5,))]
    outs = pl.pallas_call(
        functools.partial(front_kernel, plane=plane, chips=chips),
        out_shape=out_shape,
        in_specs=in_specs,
        out_specs=out_specs,
        scratch_shapes=scratch,
        compiler_params=pltpu.CompilerParams(
            collective_id=ident, has_side_effects=True, vmem_limit_bytes=VMEM_BYTES
        ),
    )(*operands)
    return outs if plane else [*outs, *weights]


def near_order(chips):
    table = []
    for z in range(chips):
        others = sorted(range(chips), key=lambda s: (abs(s - z), abs(2 * s - chips + 1) * -1))
        table.append(others)
    return table


def pick_static(table, step, z):
    return sum(jnp.where(z == k, row[step], 0) for k, row in enumerate(table))


def gated_block(rows, grad, gate, up, down):
    pre_gate = dot_nn(rows, gate)
    pre_up = dot_nn(rows, up)
    sigmoid = 1.0 / (1.0 + jnp.exp(-pre_gate))
    active = pre_gate * sigmoid
    hidden = (active * pre_up).astype(BF16)
    hidden_grad = dot_nt(grad, down)
    gate_grad = (hidden_grad * pre_up * (sigmoid * (1.0 + pre_gate * (1.0 - sigmoid)))).astype(BF16)
    up_grad = (hidden_grad * active).astype(BF16)
    result = dot_nn(hidden, down)
    back = dot_nt(gate_grad, gate) + dot_nt(up_grad, up)
    return hidden, gate_grad, up_grad, result, back


def middle_kernel(*refs, chips, shards, capacity):
    (h2_ref, cot_ref, table_ref, cot_all, gate_hbm, up_hbm, down_hbm, sg_hbm, su_hbm, sd_hbm), refs = refs[:10], refs[10:]
    (rows_out, grad_out, hid_out, da_out, db_out, mix_out, back_out), refs = refs[:7], refs[7:]
    sown, sgot, (dots_out, sy_ref, dh_ref), refs = refs[:3], refs[3:6], refs[6:9], refs[9:]
    (sgg_s, sug_s, sdg_s, sg_sem, sg_send, sg_recv), refs = refs[:6], refs[6:]
    (gate_w, up_w, down_w, sg_w, su_w, sd_w, h2_all, cot_buf, rows_ref, grad_ref, cotr_ref, scale_ref), refs = refs[:12], refs[12:]
    (y_acc, r_acc, stage_f, stage_s, stage_t, got, total), refs = refs[:7], refs[7:]
    w_sem, s_sem, cot_sem, row_sem, f_sem, tot_sem, core_send, core_recv, chain_send, chain_recv, chain_local = refs
    length, width = h2_ref.shape
    experts = 2 * chips
    hidden_width = gate_w.shape[1]
    unit = stage_f.shape[-1]
    units = hidden_width // unit
    block = sg_w.shape[-1]
    at = place()
    me, core, z = at["expert"], at["core"], at["z"]
    order = near_order(chips)
    chain_meet(at, chips, [at["dev_c"]])
    chain = ChainGather(h2_ref, h2_all, chain_send, chain_recv, chain_local, at, chips)
    chain.start()

    def load_cot(step):
        chip = pick_static(order, step, z)
        return pltpu.make_async_copy(
            cot_all.at[pl.ds(2 * chip, 2)], cot_buf.at[step % 2], cot_sem.at[step % 2]
        )

    load_cot(0).start()
    loads = [
        pltpu.make_async_copy(a, b, w_sem.at[k])
        for k, (a, b) in enumerate([(gate_hbm.at[0], gate_w), (up_hbm.at[0], up_w), (down_hbm.at[0], down_w)])
    ]
    for load in loads:
        load.start()

    def load_shared(k, slot):
        return [
            pltpu.make_async_copy(sg_hbm.at[pl.ds(k * width, width), :], sg_w.at[slot], s_sem.at[slot, 0]),
            pltpu.make_async_copy(su_hbm.at[pl.ds(k * width, width), :], su_w.at[slot], s_sem.at[slot, 1]),
            pltpu.make_async_copy(sd_hbm.at[pl.ds(k * block, block), :], sd_w.at[slot], s_sem.at[slot, 2]),
        ]

    for load in load_shared(0, 0):
        load.start()

    def one_hot(source):
        slots = table_ref[source, pl.ds(me, 1), :]
        return lax.broadcasted_iota(jnp.int32, (capacity, length), 0).astype(F32) == slots

    def row_copies(step):
        return [
            pltpu.make_async_copy(rows_ref.at[step % 2], rows_out.at[step], row_sem.at[step % 2, 0]),
            pltpu.make_async_copy(grad_ref.at[step % 2], grad_out.at[step], row_sem.at[step % 2, 1]),
        ]

    def hidden_copies(step, k, slot):
        return [
            pltpu.make_async_copy(
                stage_f.at[slot, n], out.at[step, :, columns(k * unit, unit)], f_sem.at[slot, n]
            )
            for n, out in enumerate([hid_out, da_out, db_out])
        ]

    def core_copies(step):
        return [
            remote(
                stage.at[1 - core], got.at[n, step], core_send.at[n, step], core_recv.at[n, step], at["dev_c"]
            )
            for n, stage in enumerate([stage_s, stage_t])
        ]

    def total_copies(step):
        chip = pick_static(order, step, z)
        return [
            pltpu.make_async_copy(total.at[n], out.at[chip], tot_sem.at[n])
            for n, out in enumerate([mix_out, back_out])
        ]

    def join(step):
        if step > 0:
            for copy in total_copies(step - 1):
                copy.wait()
        for n, (copy, stage) in enumerate(zip(core_copies(step), [stage_s, stage_t])):
            copy.wait()
            total[n] = (stage[core].astype(F32) + got[n, step].astype(F32)).astype(BF16)
        for copy in total_copies(step):
            copy.start()

    def expert_rows(step):
        chip = pick_static(order, step, z)
        slot = step % 2
        load_cot(step).wait()
        if step + 1 < chips:
            load_cot(step + 1).start()
        if step >= 2:
            for copy in row_copies(step - 2):
                copy.wait()
        for d in range(2):
            source, part = 2 * chip + d, pl.ds(d * capacity, capacity)
            chosen = one_hot(source)
            select = chosen.astype(F32).astype(BF16)
            rows_ref[slot, part, :] = dot_nn(select, h2_all[source]).astype(BF16)
            cot_rows = dot_nn(select, cot_buf[slot, d])
            scale = jnp.sum(
                jnp.where(chosen, table_ref[source, pl.ds(experts + me, 1), :], 0.0), axis=1, keepdims=True
            )
            grad_ref[slot, part, :] = (cot_rows * scale).astype(BF16)
            cotr_ref[part, :] = cot_rows.astype(BF16)
            scale_ref[part, :] = scale
        for copy in row_copies(step):
            copy.start()
        y_acc[...] = jnp.zeros_like(y_acc)
        r_acc[...] = jnp.zeros_like(r_acc)
        if step == 0:
            for load in loads:
                load.wait()

        @pl.loop(0, units)
        def _(k):
            cols = columns(k * unit, unit)
            hidden, gate_grad, up_grad, result, back = gated_block(
                rows_ref[slot], grad_ref[slot], gate_w[:, cols], up_w[:, cols],
                down_w[pl.ds(pl.multiple_of(k * unit, unit), unit), :],
            )
            turn = k % 2

            def settle():
                for copy in hidden_copies(step, k, turn):
                    copy.wait()

            if step == 0:
                pl.when(k >= 2)(settle)
            else:
                settle()
            stage_f[turn, 0] = hidden
            stage_f[turn, 1] = gate_grad
            stage_f[turn, 2] = up_grad
            for copy in hidden_copies(step, k, turn):
                copy.start()
            y_acc[...] += result
            r_acc[...] += back

        if step > 0:
            join(step - 1)
        result = y_acc[...].astype(BF16).astype(F32)
        dots = jnp.sum(result * cotr_ref[...].astype(F32), axis=1, keepdims=True)
        weighted = (result * scale_ref[...]).astype(BF16)
        back = r_acc[...].astype(BF16)
        for d in range(2):
            source = 2 * chip + d
            chosen = one_hot(source)
            select = chosen.astype(F32).astype(BF16)
            part = slice(d * capacity, (d + 1) * capacity)
            stage_s[d] = dot_tn(select, weighted[part]).astype(BF16)
            stage_t[d] = dot_tn(select, back[part]).astype(BF16)
            dots_out[source] = jnp.sum(jnp.where(chosen, dots[part], 0.0), axis=0, keepdims=True)
        for copy in core_copies(step):
            copy.start()

    sy_ref[...] = jnp.zeros_like(sy_ref)
    dh_ref[...] = jnp.zeros_like(dh_ref)

    def shared_copies(k):
        stay, over = [], []
        for n, held in enumerate((sgg_s, sug_s, sdg_s)):
            half = held.shape[0] // 2
            mine, other = (held.at[pl.ds(pl.multiple_of(c * half, 16), half), :] for c in (core, 1 - core))
            stay.append((mine, sown[n].at[k], sg_sem.at[n]))
            over.append((other, sgot[n].at[k], sg_send.at[n], sg_recv.at[n, k], at["dev_c"]))
        return stay, over

    def shared_settle(k):
        stay, over = shared_copies(k)
        for copy in stay:
            pltpu.make_async_copy(*copy).wait()
        for copy in over:
            remote(*copy).wait_send()

    def shared_block(k):
        slot = k % 2
        for load in load_shared(k, slot):
            load.wait()

        @pl.when(k + 1 < shards)
        def _():
            for load in load_shared(k + 1, 1 - slot):
                load.start()

        hidden, gate_grad, up_grad, result, back = gated_block(
            h2_ref[...], cot_ref[...], sg_w[slot], su_w[slot], sd_w[slot]
        )
        sy_ref[...] += result
        dh_ref[...] += back
        pl.when(k > 0)(lambda: shared_settle(k - 1))
        sgg_s[...] = dot_tn(h2_ref[...], gate_grad).astype(BF16)
        sug_s[...] = dot_tn(h2_ref[...], up_grad).astype(BF16)
        sdg_s[...] = dot_tn(hidden, cot_ref[...]).astype(BF16)
        stay, over = shared_copies(k)
        for copy in stay:
            pltpu.make_async_copy(*copy).start()
        for copy in over:
            remote(*copy).start()

    chain.finish(0)
    expert_rows(0)
    pl.loop(0, shards // 2)(shared_block)
    chain.step(1)
    pl.loop(shards // 2, shards)(shared_block)
    for step in range(1, chips):
        if step > 1:
            chain.step(step)
        chain.finish(step)
        expert_rows(step)
    join(chips - 1)
    shared_settle(shards - 1)

    @pl.loop(0, shards)
    def _(k):
        for copy in shared_copies(k)[1]:
            remote(*copy).wait_recv()

    for copy in total_copies(chips - 1):
        copy.wait()
    for step in range(max(0, chips - 2), chips):
        for copy in row_copies(step):
            copy.wait()
    for k in range(max(0, units - 2), units):
        for copy in hidden_copies(chips - 1, k, k % 2):
            copy.wait()
    chain.sent()


def middle(h2, cot_low, table_all, cot_all, expert_weights, shared_full, ident):
    length, width = h2.shape
    group, shards = lax.axis_size("expert"), lax.axis_size("shard")
    chips = group // 2
    capacity = 4 * length // group
    hidden_width = expert_weights[0].shape[2]
    block = shared_full[0].shape[1]
    unit = min(512, hidden_width)
    vmem, anywhere = pl.BlockSpec(memory_space=pltpu.VMEM), pl.BlockSpec(memory_space=pl.ANY)
    shape = jax.ShapeDtypeStruct
    both = 2 * capacity
    out_shape = [
        shape((chips, both, width), BF16),
        shape((chips, both, width), BF16),
        shape((chips, both, hidden_width), BF16),
        shape((chips, both, hidden_width), BF16),
        shape((chips, both, hidden_width), BF16),
        shape((chips, length, width), BF16),
        shape((chips, length, width), BF16),
        *[shape((shards, width // 2, block), BF16)] * 2,
        shape((shards, block // 2, width), BF16),
        *[shape((shards, width // 2, block), BF16)] * 2,
        shape((shards, block // 2, width), BF16),
        shape((group, 1, length), F32),
        shape((length, width), F32),
        shape((length, width), F32),
    ]
    dma = pltpu.SemaphoreType.DMA
    scratch = [
        pltpu.VMEM((width, block), BF16),
        pltpu.VMEM((width, block), BF16),
        pltpu.VMEM((block, width), BF16),
        dma((3,)),
        dma((3,)),
        dma((3, shards)),
        pltpu.VMEM((width, hidden_width), BF16),
        pltpu.VMEM((width, hidden_width), BF16),
        pltpu.VMEM((hidden_width, width), BF16),
        pltpu.VMEM((2, width, block), BF16),
        pltpu.VMEM((2, width, block), BF16),
        pltpu.VMEM((2, block, width), BF16),
        pltpu.VMEM((group, length, width), BF16),
        pltpu.VMEM((2, 2, length, width), BF16),
        pltpu.VMEM((2, both, width), BF16),
        pltpu.VMEM((2, both, width), BF16),
        pltpu.VMEM((both, width), BF16),
        pltpu.VMEM((both, 1), F32),
        pltpu.VMEM((both, width), F32),
        pltpu.VMEM((both, width), F32),
        pltpu.VMEM((2, 3, both, unit), BF16),
        pltpu.VMEM((2, length, width), BF16),
        pltpu.VMEM((2, length, width), BF16),
        pltpu.VMEM((2, chips, length, width), BF16),
        pltpu.VMEM((2, length, width), BF16),
        dma((3,)),
        dma((2, 3)),
        dma((2,)),
        dma((2, 2)),
        dma((2, 3)),
        dma((2,)),
        dma((2, chips)),
        dma((2, chips)),
        dma((ChainGather.copies(chips),)),
        dma((ChainGather.copies(chips),)),
        dma,
    ]
    return pl.pallas_call(
        functools.partial(middle_kernel, chips=chips, shards=shards, capacity=capacity),
        out_shape=out_shape,
        in_specs=[vmem] * 3 + [anywhere] * 7,
        out_specs=[anywhere] * 13 + [vmem] * 3,
        scratch_shapes=scratch,
        compiler_params=pltpu.CompilerParams(
            collective_id=ident, has_side_effects=True, vmem_limit_bytes=VMEM_BYTES
        ),
    )(h2, cot_low, table_all, cot_all, *expert_weights, *shared_full)


class ChainReduce:
    def __init__(self, own, from_left, from_right, send, recv, at, chips):
        self.own, self.from_left, self.from_right = own, from_left, from_right
        self.send, self.recv, self.at, self.chips = send, recv, at, chips

    @staticmethod
    def scratch(shape):
        return [pltpu.VMEM(shape, BF16)] * 3

    def copy(self, block, right):
        index = block if right else self.chips + block
        landing = self.from_left if right else self.from_right
        return remote(
            self.own.at[block],
            landing.at[block],
            self.send.at[index],
            self.recv.at[index],
            self.at["dev_right" if right else "dev_left"],
        )

    def tick(self, step):
        z, chips = self.at["z"], self.chips

        @pl.when(step >= z)
        def _():
            far = chips - 1 - step + z

            @pl.when(z > 0)
            def _():
                self.copy(far, True).wait_recv()
                self.own[far] = (self.own[far].astype(F32) + self.from_left[far].astype(F32)).astype(BF16)

            self.copy(far, True).start()

        @pl.when(step >= chips - 1 - z)
        def _():
            near = step - (chips - 1 - z)

            @pl.when(z < chips - 1)
            def _():
                self.copy(near, False).wait_recv()
                self.own[near] = (self.own[near].astype(F32) + self.from_right[near].astype(F32)).astype(BF16)

            self.copy(near, False).start()

    def value(self):
        z, chips = self.at["z"], self.chips
        pl.when(z > 0)(lambda: self.copy(z, True).wait_recv())
        pl.when(z < chips - 1)(lambda: self.copy(z, False).wait_recv())
        total = self.own[z].astype(F32)
        total += jnp.where(z > 0, self.from_left[z].astype(F32), 0.0)
        return total + jnp.where(z < chips - 1, self.from_right[z].astype(F32), 0.0)

    def sent(self):
        for step in range(1, self.chips):
            pl.when(self.at["z"] < self.chips - step)(lambda: self.copy(self.chips - step, True).wait_send())
            pl.when(self.at["z"] > step - 1)(lambda: self.copy(step - 1, False).wait_send())


class PlaneReduce:
    COPIES = 6

    def __init__(self, src, got, hold, last, send, recv, at):
        self.src, self.got, self.hold, self.last = src, got, hold, last
        self.send, self.recv, self.at = send, recv, at
        self.half = src.shape[1] // 2

    @staticmethod
    def scratch(shape):
        half = shape[1] // 2
        return [
            pltpu.VMEM((4, half, shape[2]), BF16),
            pltpu.VMEM((2, half, shape[2]), BF16),
            pltpu.VMEM((2, half, shape[2]), BF16),
        ]

    def send_to(self, src, dst, index, device):
        made = remote(src, dst, self.send.at[index], self.recv.at[index], device)
        made.start()
        return made

    def first(self):
        at, half = self.at, self.half
        upper, lower = pl.ds(0, half), pl.ds(half, half)
        self.out = [
            self.send_to(self.src.at[shard, rows, :], self.got.at[slot], slot, device)
            for slot, (shard, rows, device) in enumerate(
                [
                    (at["sx"], upper, at["dev_x"]),
                    (at["sd"], upper, at["dev_x"]),
                    (at["sy"], lower, at["dev_y"]),
                    (at["sd"], lower, at["dev_y"]),
                ]
            )
        ]

    def second(self):
        at, half = self.at, self.half
        for slot, shard, device in ((1, at["sy"], at["dev_y"]), (3, at["sx"], at["dev_x"])):
            self.out[slot].wait_recv()
            turn = slot // 2
            mine = self.src[shard, pl.ds(turn * half, half), :]
            self.hold[turn] = (mine.astype(F32) + self.got[slot].astype(F32)).astype(BF16)
            self.out.append(self.send_to(self.hold.at[turn], self.last.at[turn], 4 + turn, device))

    def value(self, turn):
        half = self.half
        self.out[2 * turn].wait_recv()
        self.out[4 + turn].wait_recv()
        mine = self.src[self.at["shard"], pl.ds(turn * half, half), :]
        return (mine.astype(F32) + self.got[2 * turn].astype(F32)) + self.last[turn].astype(F32)

    def sent(self):
        for made in self.out:
            made.wait_send()


def plane_blocks(at, index, plane):
    if not plane:
        return index
    order = [at["sd"], at["sx"], at["sy"], at["shard"]]
    return sum(jnp.where(index == k, shard, 0) for k, shard in enumerate(order))


def weights_kernel(*refs, plane, chips, shards):
    (rows_ref, grad_ref, dh_ref, dots_ref, route_ref, hid_hbm, da_hbm, db_hbm, back_hbm), refs = refs[:9], refs[9:]
    (gate_out, up_out, down_out, sum_ref, chosen_ref), refs = refs[:5], refs[5:]
    (chunk, own, from_left, from_right, dots_got), refs = refs[:5], refs[5:]
    (own_sem, chunk_sem, dots_send, dots_recv, chain_send, chain_recv), refs = refs[:6], refs[6:]
    block = chunk.shape[-1]
    at = place()
    me, group = at["expert"], 2 * chips
    load = pltpu.make_async_copy(back_hbm, own, own_sem)
    load.start()
    peers = [(lax.rem(me + k, group), at["shard"]) for k in range(1, group)]
    meet(peers + ([at["dev_x"], at["dev_y"]] if plane else []))
    if plane:
        send, recv, *work = refs
        reduces = [
            PlaneReduce(work[4 * k], *work[4 * k + 1 : 4 * k + 4], send.at[k], recv.at[k], at) for k in range(2)
        ]
        targets = [work[0], work[4], down_out]
    else:
        targets = [gate_out, up_out, down_out]
    sources = [da_hbm, db_hbm, hid_hbm]
    dots = [
        remote(dots_ref.at[peer[0]], dots_got.at[me], dots_send.at[k], dots_recv.at[k], peer)
        for k, peer in enumerate(peers)
    ]

    def fetch(array, index):
        shard = plane_blocks(at, index, plane)
        slot = index % 2
        return pltpu.make_async_copy(
            sources[array].at[:, columns(shard * block, block)], chunk.at[slot], chunk_sem.at[slot]
        )

    def make(array, low, high):
        @pl.loop(low, high)
        def _(index):
            fetch(array, index).wait()
            pl.when(index + 1 < shards)(lambda: fetch(array, index + 1).start())
            if array < 2:
                pl.when(index + 1 == shards)(lambda: fetch(array + 1, 0).start())
            shard = plane_blocks(at, index, plane)
            held = chunk[index % 2]
            if array < 2:
                targets[array][shard] = dot_tn(rows_ref[...], held).astype(BF16)
            else:
                targets[array][shard] = dot_tn(held, grad_ref[...]).astype(BF16)

    fetch(0, 0).start()
    chain = ChainReduce(own, from_left, from_right, chain_send, chain_recv, at, chips)
    load.wait()
    chain.tick(0)
    for made in dots:
        made.start()
    dots_got[me] = dots_ref[me]
    make(0, 0, shards)
    if plane:
        reduces[0].first()
    make(1, 0, shards // 2)
    for step in range(1, chips - 2):
        chain.tick(step)
    make(1, shards // 2, shards)
    if plane:
        reduces[1].first()
    make(2, 0, shards)
    if plane:
        reduces[0].second()
    chain.tick(chips - 2)
    for made in dots:
        made.wait()
    for k in range(TOP):
        chosen_ref[pl.ds(k, 1), :] = sum(
            jnp.where(route_ref[pl.ds(k, 1), :] == e, dots_got[e], 0.0) for e in range(group)
        )
    if plane:
        reduces[1].second()
        for turn in range(2):
            gate_out[pl.ds(turn * reduces[0].half, reduces[0].half), :] = reduces[0].value(turn)
    sum_ref[...] = dh_ref[...] + chain.value()
    chain.sent()
    if plane:
        for turn in range(2):
            up_out[pl.ds(turn * reduces[1].half, reduces[1].half), :] = reduces[1].value(turn)
        for reduce in reduces:
            reduce.sent()


def weights(rows, grad_rows, shared_back, dots, route_rows, hidden, gate_grad, up_grad, back_part, ident):
    chips, length, width = back_part.shape
    shards = lax.axis_size("shard")
    plane = shards == 4
    count, hidden_width = hidden.shape
    block = hidden_width // shards
    vmem, anywhere = pl.BlockSpec(memory_space=pltpu.VMEM), pl.BlockSpec(memory_space=pl.ANY)
    shape, dma = jax.ShapeDtypeStruct, pltpu.SemaphoreType.DMA
    wide = (shards, width, block)
    scratch = [pltpu.VMEM((2, count, block), BF16)] + ChainReduce.scratch((chips, length, width))
    scratch += [pltpu.VMEM(dots.shape, F32)]
    scratch += [dma, dma((2,)), dma((2 * chips - 1,)), dma((2 * chips - 1,)), dma((2 * chips,)), dma((2 * chips,))]
    if plane:
        out_shape = [shape((width, block), F32)] * 2
        scratch += [dma((2, PlaneReduce.COPIES))] * 2
        scratch += ([pltpu.VMEM(wide, BF16)] + PlaneReduce.scratch(wide)) * 2
    else:
        out_shape = [shape(wide, BF16)] * 2
    out_shape += [shape((shards, block, width), BF16), shape((length, width), F32), shape((TOP, length), F32)]
    return pl.pallas_call(
        functools.partial(weights_kernel, plane=plane, chips=chips, shards=shards),
        out_shape=out_shape,
        in_specs=[vmem] * 5 + [anywhere] * 4,
        out_specs=[vmem] * 5,
        scratch_shapes=scratch,
        compiler_params=pltpu.CompilerParams(
            collective_id=ident, has_side_effects=True, vmem_limit_bytes=VMEM_BYTES
        ),
    )(rows, grad_rows, shared_back, dots, route_rows, hidden, gate_grad, up_grad, back_part)


def norm_back(source, inverse, gain, grad_in):
    scaled = grad_in * gain
    gain_grad = jnp.sum(grad_in * source * inverse, axis=0, keepdims=True)
    input_part = inverse * scaled - source * inverse**3 * jnp.mean(
        scaled * source, axis=-1, keepdims=True
    )
    return (gain_grad, input_part)


def rear_kernel(*refs, plane, chips, shards):
    (prefix, x_ref, cot_ref, resid_ref, dh_ref, gains_ref, rot_ref, att_ref, h1_ref, lse_ref), refs = refs[:10], refs[10:]
    (qkv_ref, out_ref, cos_ref, sin_ref, mix_hbm), refs = refs[:5], refs[5:]
    halves, refs = (refs[:6], refs[6:]) if plane else ([], refs)
    (mix_out, input_grad_ref, qkv_grad_ref, out_grad_ref), refs = refs[:4], refs[4:]
    pieces, refs = (refs[:3], refs[3:]) if plane else ([], refs)
    (bias_ref, dres_ref, datt_ref, dqkv_ref, own, from_left, from_right), refs = refs[:7], refs[7:]
    (own_sem, chain_send, chain_recv), refs = refs[:3], refs[3:]
    length, width = x_ref.shape
    at = place()
    load = pltpu.make_async_copy(mix_hbm, own, own_sem)
    load.start()
    reduces = []
    if plane:
        send, recv, half_sem = refs[:3]
        work = [refs[3 + 5 * k : 8 + 5 * k] for k in range(3)]
        loads = [
            [pltpu.make_async_copy(halves[2 * k + n], work[k][n], half_sem.at[k, n]) for n in range(2)]
            for k in range(3)
        ]
        for two in loads:
            for made in two:
                made.start()
        reduces = [PlaneReduce(work[k][0], *work[k][2:], send.at[k], recv.at[k], at) for k in range(3)]
    chain_meet(at, chips, [at["dev_x"], at["dev_y"]] if plane else [])
    chain = ChainReduce(own, from_left, from_right, chain_send, chain_recv, at, chips)
    load.wait()
    chain.tick(0)
    for k, reduce in enumerate(reduces):
        for made in loads[k]:
            made.wait()

        @pl.loop(0, shards)
        def _(shard):
            work[k][0][shard] = (
                work[k][0][shard].astype(F32) + work[k][1][shard].astype(F32)
            ).astype(BF16)

        reduce.first()
    resid = resid_ref[...]
    inverse = lax.rsqrt(jnp.mean(resid * resid, axis=-1, keepdims=True) + EPS)
    gain_two_grad, extra = norm_back(resid, inverse, gains_ref[pl.ds(1, 1), :], dh_ref[...])
    dres = cot_ref[...] + extra
    dres_ref[...] = dres
    low_dres = dres.astype(BF16)
    datt_ref[...] = dot_nt(low_dres, out_ref[...]).astype(BF16)
    out_grad = dot_tn(att_ref[...], low_dres).astype(BF16)
    rows = width // shards
    for k in range(shards):
        out_grad_ref[k, :rows, :] = out_grad[k * rows : (k + 1) * rows]
    set_bias(bias_ref, prefix)
    scale = HEAD_DIM**-0.5
    count = length // 2

    def pair(j):
        queries, keys, values = (
            rot_ref[:, columns(part * width + j * 128, 128)] for part in range(3)
        )
        grads = datt_ref[:, columns(j * 128, 128)]
        low = lax.broadcasted_iota(jnp.int32, (count, 128), 1) < HEAD_DIM
        lanes = lax.broadcasted_iota(jnp.int32, (count, 128), 1)

        def keep(part, rows, value):
            if part < 2:
                value = value * cos_ref[rows, :] - partner(value) * sin_ref[rows, :]
            dqkv_ref[rows, columns(part * width + j * 128, 128)] = value.astype(BF16)

        sums = []
        for start in range(0, length, count):
            rows, seen = pl.ds(start, count), start + count
            query = two_heads(queries[start:seen] * scale)
            grad = two_heads(grads[start:seen])
            bias, lse = bias_ref[rows, :seen], lse_ref[rows, :]
            logsum = jnp.concatenate(
                [
                    jnp.sum(jnp.where(lanes == 2 * j + head, lse, 0.0), axis=1, keepdims=True)
                    for head in range(2)
                ],
                axis=0,
            )
            scores = dot_nt(query, keys[:seen])
            scores = jnp.concatenate([scores[:count] + bias, scores[count:] + bias], axis=0)
            probs = jnp.exp(scores - logsum)
            probs_grad = dot_nt(grad, values[:seen])
            inner = jnp.sum(probs * probs_grad, axis=-1, keepdims=True)
            score_grad = (probs * (probs_grad - inner)).astype(BF16)
            query_grad = dot_nn(score_grad, keys[:seen]) * scale
            keep(0, rows, jnp.where(low, query_grad[:count], query_grad[count:]))
            sums.append((dot_tn(score_grad, query), dot_tn(probs.astype(BF16), grad)))
        for part in range(2):
            keep(1 + part, pl.ds(0, count), sums[0][part] + sums[1][part][:count])
            keep(1 + part, pl.ds(count, count), sums[1][part][count:])

    pairs = width // 128
    pl.loop(0, pairs // 2)(pair)
    for step in range(1, chips - 2):
        chain.tick(step)
    pl.loop(pairs // 2, pairs)(pair)
    for reduce in reduces[:2]:
        reduce.second()
    chain.tick(chips - 2)

    @pl.loop(0, 3 * width // 256)
    def _(k):
        cols = columns(k * 256, 256)
        qkv_grad_ref[:, cols] = dot_tn(h1_ref[...], dqkv_ref[:, cols]).astype(BF16)

    for reduce in reduces[2:]:
        reduce.second()
    dh1 = dot_nt(dqkv_ref[...], qkv_ref[...])
    x = x_ref[...]
    inverse = lax.rsqrt(jnp.mean(x * x, axis=-1, keepdims=True) + EPS)
    gain_one_grad, extra = norm_back(x, inverse, gains_ref[pl.ds(0, 1), :], dh1)
    input_grad_ref[...] = dres_ref[...] + extra
    index = lax.broadcasted_iota(jnp.int32, (64, width), 0)
    gain_rows = jnp.where(index == 0, gain_one_grad, jnp.where(index == 1, gain_two_grad, 0.0)).astype(BF16)
    for k in range(shards):
        out_grad_ref[k, rows:, :] = gain_rows
    for reduce, piece in zip(reduces, pieces):
        count = piece.shape[1]
        both = jnp.concatenate([reduce.value(0), reduce.value(1)], axis=0)
        for k in range(chips):
            piece[k] = both[k * count : (k + 1) * count].astype(BF16)
        reduce.sent()
    mix_out[...] = chain.value()
    chain.sent()


def rear(prefix, inputs, cotangent, resid, dh2, gains, kept, full, mix_part, halves, ident):
    length, width = inputs.shape
    chips, shards = mix_part.shape[0], lax.axis_size("shard")
    plane = shards == 4
    cosine, sine = rope_lanes(length)
    vmem, anywhere = pl.BlockSpec(memory_space=pltpu.VMEM), pl.BlockSpec(memory_space=pl.ANY)
    shape, dma = jax.ShapeDtypeStruct, pltpu.SemaphoreType.DMA
    operands = [prefix, inputs, cotangent, resid, dh2, gains, *kept, *full, cosine, sine, mix_part]
    in_specs = [pl.BlockSpec(memory_space=pltpu.SMEM)] + [vmem] * 13 + [anywhere]
    out_shape = [
        shape((length, width), F32),
        shape((length, width), F32),
        shape((width, 3 * width), BF16),
        shape((shards, width // shards + 64, width), BF16),
    ]
    scratch = [
        pltpu.VMEM((length, length), F32),
        pltpu.VMEM((length, width), F32),
        pltpu.VMEM((length, width), BF16),
        pltpu.VMEM((length, 3 * width), BF16),
        *ChainReduce.scratch((chips, length, width)),
        dma,
        dma((2 * chips,)),
        dma((2 * chips,)),
    ]
    if plane:
        operands += halves
        in_specs += [anywhere] * 6
        scratch += [dma((3, PlaneReduce.COPIES))] * 2 + [dma((3, 2))]
        for half in halves[::2]:
            out_shape.append(shape((chips, half.shape[1] // chips, half.shape[2]), BF16))
            scratch += [pltpu.VMEM(half.shape, BF16)] * 2 + PlaneReduce.scratch(half.shape)
    return pl.pallas_call(
        functools.partial(rear_kernel, plane=plane, chips=chips, shards=shards),
        out_shape=out_shape,
        in_specs=in_specs,
        out_specs=[vmem] * len(out_shape),
        scratch_shapes=scratch,
        compiler_params=pltpu.CompilerParams(
            collective_id=ident, has_side_effects=True, vmem_limit_bytes=VMEM_BYTES
        ),
    )(*operands)


def last_kernel(*refs, chips, shards):
    (attention, pieces, down_hbm), refs = (refs[:2], refs[2:5], refs[5]), refs[6:]
    alls_out, down_out, refs = refs[:5], refs[5], refs[6:]
    halves, refs = [refs[3 * k : 3 * k + 3] for k in range(2)], refs[6:]
    plane_work, refs = refs[:10], refs[10:]
    chain_work, refs = [refs[4 * k : 4 * k + 4] for k in range(5)], refs[20:]
    load_sem, core_send, core_recv, plane_send, plane_recv, sums_send, sums_recv, all_send, all_recv, all_local = refs
    at = place()
    core = at["core"]
    loads, swaps = [], []
    for k in range(2):
        rows = attention[k].shape[1] // 2
        for n, c in enumerate((core, 1 - core)):
            part = attention[k].at[:, pl.ds(pl.multiple_of(c * rows, 16), rows), :]
            loads.append(pltpu.make_async_copy(part, halves[k][n], load_sem.at[2 * k + n]))
        swaps.append(remote(halves[k][1], halves[k][2], core_send.at[k], core_recv.at[k], at["dev_c"]))
    loads += [pltpu.make_async_copy(pieces[k], chain_work[2 + k][0], load_sem.at[4 + k]) for k in range(3)]
    loads.append(pltpu.make_async_copy(down_hbm, plane_work[0], load_sem.at[7]))
    for made in loads:
        made.start()
    sums = [
        ChainReduce(*chain_work[k][:3], sums_send.at[k], sums_recv.at[k], at, chips) for k in range(5)
    ]
    alls = [
        ChainGather(chain_work[k][3], alls_out[k], all_send.at[k], all_recv.at[k], all_local.at[k], at, chips)
        for k in range(5)
    ]
    planes = [
        PlaneReduce(src, *plane_work[1 + 3 * k : 4 + 3 * k], plane_send.at[k], plane_recv.at[k], at)
        for k, src in enumerate([plane_work[0], halves[0][0], halves[1][0]])
    ]
    shared, attn = (2, 3, 4), (0, 1)
    chain_meet(at, chips, [at["dev_x"], at["dev_y"], at["dev_c"]])
    for k in attn:
        loads[2 * k].wait()
        loads[2 * k + 1].wait()
        swaps[k].start()

    def tick(group, step):
        for k in group:
            sums[k].tick(step)

    def step_all(group, step):
        for k in group:
            alls[k].step(step)

    def total(group):
        for k in group:
            chain_work[k][3][...] = sums[k].value().astype(BF16)
            alls[k].start()

    for k in range(4, 8):
        loads[k].wait()
    tick(shared, 0)
    for k in attn:
        swaps[k].wait()

        @pl.loop(0, shards)
        def _(shard):
            halves[k][0][shard] = (
                halves[k][0][shard].astype(F32) + halves[k][2][shard].astype(F32)
            ).astype(BF16)

        planes[1 + k].first()
    for step in range(1, chips - 1):
        tick(shared, step)
    for k in attn:
        planes[1 + k].second()
    planes[0].first()
    total(shared)
    step_all(shared, 1)
    for k in attn:
        count = chain_work[k][0].shape[1]
        both = jnp.concatenate([planes[1 + k].value(0), planes[1 + k].value(1)], axis=0)
        for n in range(chips):
            sums[k].own[n] = both[n * count : (n + 1) * count].astype(BF16)
    for step in range(chips - 1):
        tick(attn, step)
        if step:
            step_all(shared, step + 1)
    total(attn)
    planes[0].second()
    for step in range(1, chips):
        step_all(attn, step)
    for turn in range(2):
        down_out[pl.ds(turn * planes[0].half, planes[0].half), :] = planes[0].value(turn)
    for k in shared + attn:
        for step in range(chips):
            alls[k].finish(step)
        alls[k].sent()
        sums[k].sent()
    for reduce in planes:
        reduce.sent()


def last(qkv_grad, out_grad, pieces, down_blocks, ident):
    shards, chips = lax.axis_size("shard"), lax.axis_size("expert") // 2
    vmem, anywhere = pl.BlockSpec(memory_space=pltpu.VMEM), pl.BlockSpec(memory_space=pl.ANY)
    shape, dma = jax.ShapeDtypeStruct, pltpu.SemaphoreType.DMA
    attention = [qkv_grad, out_grad]
    half_shapes = [(shards, v.shape[1] // 2, v.shape[2]) for v in attention]
    chain_shapes = [(chips, v.shape[1] // 2 // chips, v.shape[2]) for v in attention] + [v.shape for v in pieces]
    out_shape = [shape((2 * chips,) + s[1:], BF16) for s in chain_shapes]
    out_shape.append(shape(down_blocks.shape[1:], F32))
    scratch = []
    for s in half_shapes:
        scratch += [pltpu.VMEM(s, BF16)] * 3
    scratch.append(pltpu.VMEM(down_blocks.shape, BF16))
    for s in [down_blocks.shape] + half_shapes:
        scratch += PlaneReduce.scratch(s)
    for s in chain_shapes:
        scratch += ChainReduce.scratch(s) + [pltpu.VMEM(s[1:], BF16)]
    scratch += [
        dma((8,)),
        dma((2,)),
        dma((2,)),
        dma((3, PlaneReduce.COPIES)),
        dma((3, PlaneReduce.COPIES)),
        dma((5, 2 * chips)),
        dma((5, 2 * chips)),
        dma((5, ChainGather.copies(chips))),
        dma((5, ChainGather.copies(chips))),
        dma((5,)),
    ]
    return pl.pallas_call(
        functools.partial(last_kernel, chips=chips, shards=shards),
        out_shape=out_shape,
        in_specs=[anywhere] * 6,
        out_specs=[vmem] * 6,
        scratch_shapes=scratch,
        compiler_params=pltpu.CompilerParams(
            collective_id=ident, has_side_effects=True, vmem_limit_bytes=VMEM_BYTES
        ),
    )(qkv_grad, out_grad, *pieces, down_blocks)


def finish_kernel(*refs, chips):
    (summands, sums, plain), refs = (refs[:3], refs[3:8], refs[8:12]), refs[12:]
    (output, grads, plain_out), refs = (refs[0], refs[1:6], refs[6:10]), refs[10:]
    (add_in, sum_in, plain_in, add_out, sum_out), (load_sem, store_sem) = (
        (refs[:3], refs[3:8], refs[8:12], refs[12], refs[13:18]),
        refs[18:],
    )
    held = [*plain_in, *sum_in, *add_in]
    loads = [
        pltpu.make_async_copy(a, b, load_sem.at[k]) for k, (a, b) in enumerate(zip([*plain, *sums, *summands], held))
    ]
    stores = [
        pltpu.make_async_copy(a, b, store_sem.at[k])
        for k, (a, b) in enumerate(zip([*plain_in, *sum_out, add_out], [*plain_out, *grads, output]))
    ]
    for made in loads:
        made.start()
    for k in range(4):
        loads[k].wait()
        stores[k].start()
    for k in range(5):
        loads[4 + k].wait()
        count = sum_in[k].shape[1]
        for n in range(chips):
            for c in range(2):
                sum_out[k][pl.ds((c * chips + n) * count, count), :] = sum_in[k][2 * n + c].astype(F32)
        stores[4 + k].start()
    for made in loads[9:]:
        made.wait()
    add_out[...] = add_in[0][...] + add_in[1][...] + add_in[2][...]
    stores[9].start()
    for made in stores:
        made.wait()


def finish(summands, sums, plain):
    chips = sums[0].shape[0] // 2
    shape, dma = jax.ShapeDtypeStruct, pltpu.SemaphoreType.DMA
    anywhere = pl.BlockSpec(memory_space=pl.ANY)
    inputs = [*summands, *sums, *plain]
    out_shape = [shape(summands[0].shape, F32)]
    out_shape += [shape((v.shape[0] * v.shape[1], v.shape[2]), F32) for v in sums]
    scratch = [pltpu.VMEM(v.shape, v.dtype) for v in inputs] + [pltpu.VMEM(s.shape, F32) for s in out_shape]
    out_shape += [shape(v.shape, F32) for v in plain]
    return pl.pallas_call(
        functools.partial(finish_kernel, chips=chips),
        out_shape=out_shape,
        in_specs=[anywhere] * len(inputs),
        out_specs=[anywhere] * len(out_shape),
        scratch_shapes=scratch + [dma((len(inputs),)), dma((len(out_shape),))],
        compiler_params=pltpu.CompilerParams(vmem_limit_bytes=VMEM_BYTES),
    )(*inputs)


def on_device(
    inputs,
    cotangent,
    norm_one,
    qkv_weight,
    out_weight,
    norm_two,
    shared_gate,
    shared_up,
    shared_down,
    expert_gate,
    expert_up,
    expert_down,
    gate_weights,
    routes,
    prefix,
):
    length, width = inputs.shape
    experts, shards = lax.axis_size("expert"), lax.axis_size("shard")
    me, shard = lax.axis_index("expert"), lax.axis_index("shard")
    route_rows = routes.T
    (
        cot_all,
        table_all,
        normed_one,
        turned,
        attended,
        logsum,
        resid,
        normed_two,
        cot_low,
        gains,
        qkv_full,
        out_full,
        gate_blocks,
        up_blocks,
        down_full,
    ) = front(
        prefix,
        inputs,
        cotangent,
        route_rows,
        gate_weights.T,
        [norm_one, norm_two],
        [qkv_weight, out_weight, shared_gate, shared_up, shared_down],
        1,
    )
    (
        rows,
        grad_rows,
        hidden,
        gate_pre_grad,
        up_pre_grad,
        mix_part,
        back_part,
        *shared_halves,
        weight_back,
        shared_out,
        shared_back,
    ) = middle(
        normed_two,
        cot_low,
        table_all,
        cot_all,
        [expert_gate, expert_up, expert_down],
        [gate_blocks, up_blocks, down_full],
        2,
    )
    shared_halves = [shared_halves[k + n] for k in range(3) for n in (0, 3)]
    rows, grad_rows, hidden, gate_pre_grad, up_pre_grad = (
        v.reshape(-1, v.shape[-1]) for v in (rows, grad_rows, hidden, gate_pre_grad, up_pre_grad)
    )
    gate_term, up_term, down_term, normed_two_grad, gate_weights_grad = weights(
        rows, grad_rows, shared_back, weight_back, route_rows, hidden, gate_pre_grad, up_pre_grad, back_part, 3
    )
    mixture, input_grad, qkv_grad, out_grad, *pieces = rear(
        prefix,
        inputs,
        cotangent,
        resid,
        normed_two_grad,
        gains,
        [turned, attended, normed_one, logsum],
        [qkv_full, out_full],
        mix_part,
        shared_halves,
        4,
    )
    qkv_grad = qkv_grad.reshape(shards, width // shards, 3 * width)
    if shards == 4:
        *sums, down_term = last(qkv_grad, out_grad, pieces, down_term, 5)
        output, qkv_sum, out_sum, *shared_sums, input_grad, gate_term, up_term, down_term = finish(
            [resid, mixture, shared_out], sums, [input_grad, gate_term, up_term, down_term]
        )
    else:

        def over_plane(value):
            return lax.psum_scatter(value, "shard", scatter_dimension=0, tiled=True)[0]

        def over_all(value):
            return lax.psum(over_plane(value), "expert").astype(F32)

        output = resid + mixture + shared_out
        gate_term, up_term, down_term = (
            over_plane(v).astype(F32) for v in (gate_term, up_term, down_term)
        )
        qkv_sum, out_sum = over_all(qkv_grad), over_all(out_grad)
        shared_sums = []
        for own, got in zip(shared_halves[::2], shared_halves[1::2]):
            half = (own.astype(F32) + got.astype(F32)).astype(BF16)
            both = jnp.concatenate([jnp.where(me % 2 == c, half, 0) for c in range(2)], axis=1)
            shared_sums.append(over_all(both))
    part = width // shards
    gain_grads = lax.dynamic_slice(out_sum[part : part + 2], (0, shard * part), (2, part))
    return (
        output,
        input_grad,
        gain_grads[0],
        qkv_sum,
        out_sum[:part],
        gain_grads[1],
        *shared_sums,
        gate_term[None],
        up_term[None],
        down_term[None],
        gate_weights_grad.T,
    )


def solution(mesh):
    tokens = P(("expert", "shard"), None)
    in_specs = (
        tokens,
        tokens,
        P("shard"),
        P("shard", None),
        P("shard", None),
        P("shard"),
        P(None, "shard"),
        P(None, "shard"),
        P("shard", None),
        P("expert", None, None),
        P("expert", None, None),
        P("expert", None, None),
        tokens,
        tokens,
        P(("expert", "shard")),
    )
    out_specs = (
        tokens,
        tokens,
        P("shard"),
        P("shard", None),
        P("shard", None),
        P("shard"),
        P(None, "shard"),
        P(None, "shard"),
        P("shard", None),
        P("expert", None, "shard"),
        P("expert", None, "shard"),
        P("expert", "shard", None),
        tokens,
    )
    return jax.shard_map(
        on_device, mesh=mesh, in_specs=in_specs, out_specs=out_specs, check_vma=False
    )
```

```python
import functools

import jax
import jax.numpy as jnp
import numpy as np
from jax import lax
from jax.experimental import pallas as pl
from jax.experimental.pallas import tpu as pltpu
from jax.sharding import PartitionSpec as P

HEADS = 12
HEAD_DIM = 64
TOP = 2
EPS = 1e-06
MESH = pl.DeviceIdType.MESH
F32 = jnp.float32
BF16 = jnp.bfloat16
VMEM_BYTES = 63 << 20


def place():
    expert, shard = lax.axis_index("expert"), lax.axis_index("shard")
    core, x, y = expert % 2, shard % 2, shard // 2
    return dict(
        expert=expert,
        shard=shard,
        core=core,
        z=expert // 2,
        sx=2 * y + 1 - x,
        sy=2 * (1 - y) + x,
        sd=2 * (1 - y) + 1 - x,
        dev_x=(expert, 2 * y + 1 - x),
        dev_y=(expert, 2 * (1 - y) + x),
        dev_c=(expert + 1 - 2 * core, shard),
        dev_left=(expert - 2, shard),
        dev_right=(expert + 2, shard),
    )


def meet(devices):
    barrier = pltpu.get_barrier_semaphore()
    for device in devices:
        pl.semaphore_signal(barrier, inc=1, device_id=device, device_id_type=MESH)
    pl.semaphore_wait(barrier, len(devices))


def remote(src, dst, send, recv, device):
    return pltpu.make_async_remote_copy(
        src_ref=src, dst_ref=dst, send_sem=send, recv_sem=recv, device_id=device, device_id_type=MESH
    )


class PlaneGather:
    COPIES = 7

    def __init__(self, src, dst, send, recv, local, at):
        self.src, self.dst, self.at = src, dst, at
        self.send, self.recv, self.local = send, recv, local
        self.rows = src.shape[0]
        self.copies = []

    def view(self, shard, start, count):
        return self.dst.at[pl.ds(pl.multiple_of(shard * self.rows + start, 16), count), :]

    def copy(self, part, index, device):
        made = remote(part, part, self.send.at[index], self.recv.at[index], device)
        made.start()
        self.copies.append(made)

    def load(self):
        self.own = pltpu.make_async_copy(self.src, self.view(self.at["shard"], 0, self.rows), self.local)
        self.own.start()

    def first(self):
        at, half = self.at, self.rows // 2
        self.own.wait()
        part = self.view(at["shard"], at["core"] * half, half)
        self.copy(part, 0, at["dev_x"])
        self.copy(part, 1, at["dev_y"])

    def second(self):
        at, half, quarter = self.at, self.rows // 2, self.rows // 4
        start = at["core"] * half
        self.copies[0].wait_recv()
        self.copy(self.view(at["sx"], start, quarter), 2, at["dev_y"])
        self.copy(self.view(at["sx"], start, half), 3, at["dev_c"])
        self.copies[1].wait_recv()
        self.copy(self.view(at["sy"], start + quarter, quarter), 4, at["dev_x"])
        self.copy(self.view(at["sy"], start, half), 5, at["dev_c"])

    def third(self):
        at, half = self.at, self.rows // 2
        self.copies[2].wait_recv()
        self.copies[4].wait_recv()
        self.copy(self.view(at["sd"], at["core"] * half, half), 6, at["dev_c"])

    def finish(self):
        for index in (3, 5, 6):
            self.copies[index].wait_recv()
        for made in self.copies:
            made.wait_send()


class ChainGather:
    @staticmethod
    def copies(chips):
        return 4 * chips

    def __init__(self, src, dst, send, recv, local, at, chips):
        self.src, self.dst, self.send, self.recv, self.local = src, dst, send, recv, local
        self.at, self.chips = at, chips

    def copy(self, block, index, device, first=False):
        part = self.dst.at[block]
        return remote(
            self.src if first else part, part, self.send.at[index], self.recv.at[index], self.at[device]
        )

    def right(self, step):
        at = self.at
        return self.copy((at["z"] - step + 1) * 2 + at["core"], step - 1, "dev_right", step == 1)

    def left(self, step):
        at = self.at
        return self.copy(
            (at["z"] + step - 1) * 2 + at["core"], self.chips + step - 1, "dev_left", step == 1
        )

    def over(self, step):
        at = self.at
        return self.copy(
            (at["z"] - step) * 2 + at["core"], (2 if step >= 0 else 3) * self.chips + abs(step), "dev_c", step == 0
        )

    def arrived(self, step, side):
        at = self.at
        if side == "left":
            return self.copy((at["z"] - step) * 2 + at["core"], step - 1, "dev_right")
        return self.copy((at["z"] + step) * 2 + at["core"], self.chips + step - 1, "dev_left")

    def start(self):
        at = self.at
        pl.when(at["z"] < self.chips - 1)(lambda: self.right(1).start())
        pl.when(at["z"] > 0)(lambda: self.left(1).start())
        self.over(0).start()
        self.own = pltpu.make_async_copy(self.src, self.dst.at[at["expert"]], self.local)
        self.own.start()

    def step(self, step):
        at, chips = self.at, self.chips

        @pl.when(at["z"] - step >= 0)
        def _():
            self.arrived(step, "left").wait_recv()
            if step < chips - 1:
                pl.when(at["z"] < chips - 1)(lambda: self.right(step + 1).start())
            self.over(step).start()

        @pl.when(at["z"] + step < chips)
        def _():
            self.arrived(step, "right").wait_recv()
            if step < chips - 1:
                pl.when(at["z"] > 0)(lambda: self.left(step + 1).start())
            self.over(-step).start()

    def finish(self, step):
        at = self.at
        if step == 0:
            self.over(0).wait()
            self.own.wait()
            return
        pl.when(at["z"] - step >= 0)(lambda: self.over(step).wait())
        pl.when(at["z"] + step < self.chips)(lambda: self.over(-step).wait())

    def sent(self):
        at, chips = self.at, self.chips
        for step in range(1, chips):
            pl.when((at["z"] - step + 1 >= 0) & (at["z"] < chips - 1))(lambda: self.right(step).wait_send())
            pl.when((at["z"] + step - 1 < chips) & (at["z"] > 0))(lambda: self.left(step).wait_send())


def chain_meet(at, chips, others):
    barrier = pltpu.get_barrier_semaphore()
    for device in others:
        pl.semaphore_signal(barrier, inc=1, device_id=device, device_id_type=MESH)

    @pl.when(at["z"] > 0)
    def _():
        pl.semaphore_signal(barrier, inc=1, device_id=at["dev_left"], device_id_type=MESH)

    @pl.when(at["z"] < chips - 1)
    def _():
        pl.semaphore_signal(barrier, inc=1, device_id=at["dev_right"], device_id_type=MESH)

    ends = jnp.where(at["z"] == 0, 1, 0) + jnp.where(at["z"] == chips - 1, 1, 0)
    pl.semaphore_wait(barrier, len(others) + 2 - ends)


def dot_nn(left, right):
    return lax.dot_general(left, right, (((1,), (0,)), ((), ())), preferred_element_type=F32)


def dot_nt(left, right):
    return lax.dot_general(left, right, (((1,), (1,)), ((), ())), preferred_element_type=F32)


def dot_tn(left, right):
    return lax.dot_general(left, right, (((0,), (0,)), ((), ())), preferred_element_type=F32)


def columns(start, count):
    return pl.ds(pl.multiple_of(start, 128), count)


def rope_lanes(length):
    half = HEAD_DIM // 2
    frequency = 10000.0 ** (-np.arange(half) * 2.0 / HEAD_DIM)
    angles = np.arange(length)[:, None] * frequency[None, :]
    cosine, sine = np.cos(angles), np.sin(angles)
    return (
        jnp.asarray(np.concatenate([cosine] * 4, axis=1), F32),
        jnp.asarray(np.concatenate([-sine, sine] * 2, axis=1), F32),
    )


def partner(values):
    lane = lax.broadcasted_iota(jnp.int32, values.shape, 1)
    half = HEAD_DIM // 2
    ahead = pltpu.roll(values, 128 - half, 1)
    behind = pltpu.roll(values, half, 1)
    return jnp.where(lane % HEAD_DIM < half, ahead, behind)


def set_bias(bias_ref, prefix):
    shape = bias_ref.shape
    row = lax.broadcasted_iota(jnp.int32, shape, 0)
    col = lax.broadcasted_iota(jnp.int32, shape, 1)
    bias_ref[...] = jnp.where((col < prefix[0]) | (col <= row), 0.0, -1e30)


def two_heads(values):
    low = lax.broadcasted_iota(jnp.int32, values.shape, 1) < HEAD_DIM
    zero = jnp.zeros_like(values)
    return jnp.concatenate([jnp.where(low, values, zero), jnp.where(low, zero, values)], axis=0)


def front_kernel(*refs, plane, chips):
    (prefix, x_ref, cot_ref, route_ref, weight_ref, cos_ref, sin_ref), refs = refs[:7], refs[7:]
    (one_ref, two_ref), refs = refs[:2], refs[2:]
    weights, refs = (refs[:5], refs[5:]) if plane else (refs[:2], refs[2:])
    (cot_out, table_out, h1_out, rot_out, att_out, resid_out, h2_out, cot_low, lse_ref, gains_ref), refs = refs[:10], refs[10:]
    full_out, refs = (refs[:5], refs[5:]) if plane else ([], refs)
    (h1_ref, rot_ref, att_ref, resid_ref, h2_ref, cot_low_ref), refs = refs[:6], refs[6:]
    (bias_ref, table_ref, table_all, cot_all, out_sem, chain_sem, chain_send, chain_recv, chain_local), refs = refs[:9], refs[9:]
    length, width = x_ref.shape
    experts = table_ref.shape[0] // 2
    at = place()
    if plane:
        gains_src, gains_full, full, (send, recv, local) = refs[0], refs[1], refs[2:7], refs[7:]
        gathers = [
            PlaneGather(a, b, send.at[k], recv.at[k], local.at[k], at)
            for k, (a, b) in enumerate(zip([*weights, gains_src], [*full, gains_full]))
        ]
        first, later = [gathers[5], gathers[1], gathers[0]], gathers[2:5]
        gains_src[:32, :] = jnp.broadcast_to(one_ref[...], (32, one_ref.shape[1]))
        gains_src[32:, :] = jnp.broadcast_to(two_ref[...], (32, two_ref.shape[1]))
        for gather in first + later:
            gather.load()
        qkv_full, out_full = full[:2]
    else:
        qkv_full, out_full = weights
    chain_meet(at, chips, [at["dev_x"], at["dev_y"], at["dev_c"]] if plane else [at["dev_c"]])
    if plane:
        for gather in first:
            gather.first()
    cot_low_ref[...] = cot_ref[...].astype(BF16)
    names = lax.broadcasted_iota(jnp.int32, (experts, length), 0)
    chosen = [route_ref[pl.ds(k, 1), :] == names for k in range(TOP)]
    member = (chosen[0] | chosen[1]).astype(F32)
    earlier = (
        lax.broadcasted_iota(jnp.int32, (length, length), 0)
        < lax.broadcasted_iota(jnp.int32, (length, length), 1)
    ).astype(F32)
    slot = dot_nn(member.astype(BF16), earlier.astype(BF16))
    table_ref[:experts, :] = jnp.where(member > 0, slot, -1.0)
    table_ref[experts:, :] = sum(
        jnp.where(chosen[k], weight_ref[pl.ds(k, 1), :], 0.0) for k in range(TOP)
    )
    chains = [
        ChainGather(a, b, chain_send.at[k], chain_recv.at[k], chain_local.at[k], at, chips)
        for k, (a, b) in enumerate([(table_ref, table_all), (cot_low_ref, cot_all)])
    ]
    for chain in chains:
        chain.start()
    set_bias(bias_ref, prefix)
    keeps = []

    def keep(src, dst):
        made = pltpu.make_async_copy(src, dst, out_sem.at[len(keeps)])
        made.start()
        keeps.append(made)

    def each_kept(step, act):
        for n, side in enumerate((-1, 1) if step else (1,)):
            chip = at["z"] + side * step

            @pl.when((chip >= 0) & (chip < chips))
            def _():
                for k, (src, dst) in enumerate([(table_all, table_out), (cot_all, cot_out)]):
                    part = pl.ds(2 * chip, 2)
                    act(pltpu.make_async_copy(src.at[part], dst.at[part], chain_sem.at[step, n, k]))

    def keep_chain(step):
        each_kept(step, lambda made: made.start())

    keep(cot_low_ref, cot_low)
    if plane:
        for gather in first:
            gather.second()
        for gather in later:
            gather.first()
        for chain in chains:
            chain.step(1)
        for step in ("third", "finish"):
            for gather in first:
                getattr(gather, step)()
        for k in range(2):
            keep(full[k], full_out[k])
        blocks = range(gains_full.shape[0] // 64)
        for k in range(2):
            row = [gains_full[pl.ds(64 * n + 32 * k, 1), :].astype(F32) for n in blocks]
            gains_ref[pl.ds(k, 1), :] = jnp.concatenate(row, axis=1)
    else:
        for chain in chains:
            chain.step(1)
        gains_ref[pl.ds(0, 1), :] = one_ref[...].astype(F32)
        gains_ref[pl.ds(1, 1), :] = two_ref[...].astype(F32)
    x = x_ref[...]
    inverse = lax.rsqrt(jnp.mean(x * x, axis=-1, keepdims=True) + EPS)
    h1_ref[...] = (x * inverse * gains_ref[pl.ds(0, 1), :]).astype(BF16)

    def project(block, turned):
        cols = columns(block * 256, 256)
        part = dot_nn(h1_ref[...], qkv_full[:, cols])
        if turned:
            part = jnp.concatenate(
                [v * cos_ref[...] + partner(v) * sin_ref[...] for v in (part[:, :128], part[:, 128:])], axis=1
            )
        rot_ref[:, cols] = part.astype(BF16)

    pl.loop(0, 2 * width // 256)(lambda block: project(block, True))
    pl.loop(2 * width // 256, 3 * width // 256)(lambda block: project(block, False))
    keep(h1_ref, h1_out)
    keep(rot_ref, rot_out)
    lse_ref[...] = jnp.zeros_like(lse_ref)
    count = length // 2

    def pair(j):
        queries, keys, values = (
            rot_ref[:, columns(part * width + j * 128, 128)] for part in range(3)
        )
        low = lax.broadcasted_iota(jnp.int32, (count, 128), 1) < HEAD_DIM
        lanes = lax.broadcasted_iota(jnp.int32, (count, 128), 1)
        for start in range(0, length, count):
            rows, seen = pl.ds(start, count), start + count
            scores = dot_nt(two_heads(queries[start:seen] * HEAD_DIM**-0.5), keys[:seen])
            bias = bias_ref[rows, :seen]
            scores = jnp.concatenate([scores[:count] + bias, scores[count:] + bias], axis=0)
            peak = jnp.max(scores, axis=-1, keepdims=True)
            exponent = jnp.exp(scores - peak)
            total = jnp.sum(exponent, axis=-1, keepdims=True)
            out = dot_nn(exponent.astype(BF16), values[:seen]) * (1.0 / total)
            att_ref[rows, columns(j * 128, 128)] = jnp.where(low, out[:count], out[count:]).astype(BF16)
            logsum = peak + jnp.log(total)
            lse_ref[rows, :] = jnp.where(
                lanes == 2 * j,
                logsum[:count],
                jnp.where(lanes == 2 * j + 1, logsum[count:], lse_ref[rows, :]),
            )

    pairs = width // 128
    pl.loop(0, pairs // 2)(pair)
    for step in range(2, chips - 1):
        for chain in chains:
            chain.step(step)
    pl.loop(pairs // 2, pairs)(pair)
    keep(att_ref, att_out)
    resid = x_ref[...] + dot_nn(att_ref[...], out_full[...])
    resid_ref[...] = resid
    keep(resid_ref, resid_out)
    inverse = lax.rsqrt(jnp.mean(resid * resid, axis=-1, keepdims=True) + EPS)
    h2_ref[...] = (resid * inverse * gains_ref[pl.ds(1, 1), :]).astype(BF16)
    keep(h2_ref, h2_out)
    for step in range(chips - 1):
        for chain in chains:
            chain.finish(step)
        keep_chain(step)
    if plane:
        for gather in later:
            gather.second()
    for chain in chains:
        chain.step(chips - 1)
    if plane:
        for gather in later:
            gather.third()
    for chain in chains:
        chain.finish(chips - 1)
    keep_chain(chips - 1)
    if plane:
        for k, gather in enumerate(later):
            gather.finish()
            keep(full[2 + k], full_out[2 + k])
    for chain in chains:
        chain.sent()
    for step in range(chips):
        each_kept(step, lambda made: made.wait())
    for made in keeps:
        made.wait()


def front(prefix, inputs, cotangent, route_rows, weight_rows, gains, weights, ident):
    length, width = inputs.shape
    group, shards = lax.axis_size("expert"), lax.axis_size("shard")
    chips, plane = group // 2, shards == 4
    cosine, sine = rope_lanes(length)
    vmem, anywhere = pl.BlockSpec(memory_space=pltpu.VMEM), pl.BlockSpec(memory_space=pl.ANY)
    gains = [v.reshape(1, -1) for v in gains]
    if not plane:
        gains = [lax.all_gather(v, "shard", axis=1, tiled=True) for v in gains]
        weights = [lax.all_gather(v, "shard", axis=0, tiled=True) for v in weights]
    operands = [prefix, inputs, cotangent, route_rows, weight_rows, cosine, sine, *gains]
    in_specs = [pl.BlockSpec(memory_space=pltpu.SMEM)] + [vmem] * 8
    operands += weights if plane else weights[:2]
    in_specs += [anywhere] * 5 if plane else [vmem] * 2
    shape, dma = jax.ShapeDtypeStruct, pltpu.SemaphoreType.DMA
    out_shape = [
        shape((group, length, width), BF16),
        shape((group, 2 * group, length), F32),
        shape((length, width), BF16),
        shape((length, 3 * width), BF16),
        shape((length, width), BF16),
        shape((length, width), F32),
        shape((length, width), BF16),
        shape((length, width), BF16),
        shape((length, 128), F32),
        shape((8, width), F32),
    ]
    out_specs = [anywhere] * 8 + [vmem] * 2
    scratch = [pltpu.VMEM(s.shape, s.dtype) for s in out_shape[2:8]]
    scratch += [
        pltpu.VMEM((length, length), F32),
        pltpu.VMEM((2 * group, length), F32),
        pltpu.VMEM((group, 2 * group, length), F32),
        pltpu.VMEM((group, length, width), BF16),
        dma((11,)),
        dma((chips, 2, 2)),
        dma((2, ChainGather.copies(chips))),
        dma((2, ChainGather.copies(chips))),
        dma((2,)),
    ]
    if plane:
        full = [(shards * v.shape[0], v.shape[1]) for v in weights]
        out_shape += [shape(s, BF16) for s in full]
        out_specs += [anywhere] * 5
        part = gains[0].shape[1]
        scratch += [pltpu.VMEM((64, part), BF16), pltpu.VMEM((64 * shards, part), BF16)]
        scratch += [pltpu.VMEM(s, BF16) for s in full]
        scratch += [dma((6, PlaneGather.COPIES)), dma((6, PlaneGather.COPIES)), dma((6,))]
    outs = pl.pallas_call(
        functools.partial(front_kernel, plane=plane, chips=chips),
        out_shape=out_shape,
        in_specs=in_specs,
        out_specs=out_specs,
        scratch_shapes=scratch,
        compiler_params=pltpu.CompilerParams(
            collective_id=ident, has_side_effects=True, vmem_limit_bytes=VMEM_BYTES
        ),
    )(*operands)
    return outs if plane else [*outs, *weights]


def near_order(chips):
    table = []
    for z in range(chips):
        others = sorted(range(chips), key=lambda s: (abs(s - z), abs(2 * s - chips + 1) * -1))
        table.append(others)
    return table


def pick_static(table, step, z):
    return sum(jnp.where(z == k, row[step], 0) for k, row in enumerate(table))


def gated_block(rows, grad, gate, up, down):
    pre_gate = dot_nn(rows, gate)
    pre_up = dot_nn(rows, up)
    sigmoid = 1.0 / (1.0 + jnp.exp(-pre_gate))
    active = pre_gate * sigmoid
    hidden = (active * pre_up).astype(BF16)
    hidden_grad = dot_nt(grad, down)
    gate_grad = (hidden_grad * pre_up * (sigmoid * (1.0 + pre_gate * (1.0 - sigmoid)))).astype(BF16)
    up_grad = (hidden_grad * active).astype(BF16)
    result = dot_nn(hidden, down)
    back = dot_nt(gate_grad, gate) + dot_nt(up_grad, up)
    return hidden, gate_grad, up_grad, result, back


def middle_kernel(*refs, chips, capacity):
    (h2_ref, table_ref, cot_all, gate_hbm, up_hbm, down_hbm), refs = refs[:6], refs[6:]
    (rows_out, grad_out, hid_out, da_out, db_out, mix_out, back_out), refs = refs[:7], refs[7:]
    dots_out, refs = refs[0], refs[1:]
    (gate_w, up_w, down_w, h2_all, cot_buf, rows_ref, grad_ref, cotr_ref, scale_ref), refs = refs[:9], refs[9:]
    (y_acc, r_acc, stage_f, stage_s, stage_t, got, total), refs = refs[:7], refs[7:]
    w_sem, cot_sem, row_sem, f_sem, tot_sem, core_send, core_recv, chain_send, chain_recv, chain_local = refs
    length, width = h2_ref.shape
    experts = 2 * chips
    hidden_width = gate_w.shape[1]
    unit = stage_f.shape[-1]
    units = hidden_width // unit
    at = place()
    me, core, z = at["expert"], at["core"], at["z"]
    order = near_order(chips)
    chain_meet(at, chips, [at["dev_c"]])
    chain = ChainGather(h2_ref, h2_all, chain_send, chain_recv, chain_local, at, chips)
    chain.start()

    def load_cot(step):
        chip = pick_static(order, step, z)
        return pltpu.make_async_copy(
            cot_all.at[pl.ds(2 * chip, 2)], cot_buf.at[step % 2], cot_sem.at[step % 2]
        )

    load_cot(0).start()
    loads = [
        pltpu.make_async_copy(a, b, w_sem.at[k])
        for k, (a, b) in enumerate([(gate_hbm.at[0], gate_w), (up_hbm.at[0], up_w), (down_hbm.at[0], down_w)])
    ]
    for load in loads:
        load.start()

    def one_hot(source):
        slots = table_ref[source, pl.ds(me, 1), :]
        return lax.broadcasted_iota(jnp.int32, (capacity, length), 0).astype(F32) == slots

    def row_copies(step):
        return [
            pltpu.make_async_copy(rows_ref, rows_out.at[step], row_sem.at[0]),
            pltpu.make_async_copy(grad_ref, grad_out.at[step], row_sem.at[1]),
        ]

    def hidden_copies(step, k, slot):
        return [
            pltpu.make_async_copy(
                stage_f.at[slot, n], out.at[step, :, columns(k * unit, unit)], f_sem.at[slot, n]
            )
            for n, out in enumerate([hid_out, da_out, db_out])
        ]

    def core_copies(step):
        return [
            remote(
                stage.at[1 - core], got.at[n, step], core_send.at[n, step], core_recv.at[n, step], at["dev_c"]
            )
            for n, stage in enumerate([stage_s, stage_t])
        ]

    def total_copies(step):
        chip = pick_static(order, step, z)
        return [
            pltpu.make_async_copy(total.at[n], out.at[chip], tot_sem.at[n])
            for n, out in enumerate([mix_out, back_out])
        ]

    def join(step):
        if step > 0:
            for copy in total_copies(step - 1):
                copy.wait()
        for n, (copy, stage) in enumerate(zip(core_copies(step), [stage_s, stage_t])):
            copy.wait()
            total[n] = (stage[core].astype(F32) + got[n, step].astype(F32)).astype(BF16)
        for copy in total_copies(step):
            copy.start()

    def expert_rows(step):
        chip = pick_static(order, step, z)
        slot = step % 2
        load_cot(step).wait()
        if step + 1 < chips:
            load_cot(step + 1).start()
        if step > 0:
            for copy in row_copies(step - 1):
                copy.wait()
        for d in range(2):
            source, part = 2 * chip + d, pl.ds(d * capacity, capacity)
            chosen = one_hot(source)
            select = chosen.astype(F32).astype(BF16)
            rows_ref[part, :] = dot_nn(select, h2_all[source]).astype(BF16)
            cot_rows = dot_nn(select, cot_buf[slot, d])
            scale = jnp.sum(
                jnp.where(chosen, table_ref[source, pl.ds(experts + me, 1), :], 0.0), axis=1, keepdims=True
            )
            grad_ref[part, :] = (cot_rows * scale).astype(BF16)
            cotr_ref[part, :] = cot_rows.astype(BF16)
            scale_ref[part, :] = scale
        for copy in row_copies(step):
            copy.start()
        y_acc[...] = jnp.zeros_like(y_acc)
        r_acc[...] = jnp.zeros_like(r_acc)
        if step == 0:
            for load in loads:
                load.wait()

        def one_unit(k):
            cols = columns(k * unit, unit)
            hidden, gate_grad, up_grad, result, back = gated_block(
                rows_ref[...], grad_ref[...], gate_w[:, cols], up_w[:, cols],
                down_w[pl.ds(pl.multiple_of(k * unit, unit), unit), :],
            )
            turn = k % 2

            def settle():
                for copy in hidden_copies(step, k, turn):
                    copy.wait()

            if step == 0:
                pl.when(k >= 2)(settle)
            else:
                settle()
            stage_f[turn, 0] = hidden
            stage_f[turn, 1] = gate_grad
            stage_f[turn, 2] = up_grad
            for copy in hidden_copies(step, k, turn):
                copy.start()
            y_acc[...] += result
            r_acc[...] += back

        if step + 1 < chips:
            pl.loop(0, units - 1)(one_unit)
            chain.step(step + 1)
            pl.loop(units - 1, units)(one_unit)
        else:
            pl.loop(0, units)(one_unit)
        if step > 0:
            join(step - 1)
        result = y_acc[...].astype(BF16).astype(F32)
        dots = jnp.sum(result * cotr_ref[...].astype(F32), axis=1, keepdims=True)
        weighted = (result * scale_ref[...]).astype(BF16)
        back = r_acc[...].astype(BF16)
        for d in range(2):
            source = 2 * chip + d
            chosen = one_hot(source)
            select = chosen.astype(F32).astype(BF16)
            part = slice(d * capacity, (d + 1) * capacity)
            stage_s[d] = dot_tn(select, weighted[part]).astype(BF16)
            stage_t[d] = dot_tn(select, back[part]).astype(BF16)
            dots_out[source] = jnp.sum(jnp.where(chosen, dots[part], 0.0), axis=0, keepdims=True)
        for copy in core_copies(step):
            copy.start()

    for step in range(chips):
        chain.finish(step)
        expert_rows(step)
    join(chips - 1)
    for copy in total_copies(chips - 1):
        copy.wait()
    for copy in row_copies(chips - 1):
        copy.wait()
    for k in range(max(0, units - 2), units):
        for copy in hidden_copies(chips - 1, k, k % 2):
            copy.wait()
    chain.sent()


def middle(h2, table_all, cot_all, expert_weights, ident):
    length, width = h2.shape
    group = lax.axis_size("expert")
    chips = group // 2
    capacity = 4 * length // group
    hidden_width = expert_weights[0].shape[2]
    unit = min(512, hidden_width)
    vmem, anywhere = pl.BlockSpec(memory_space=pltpu.VMEM), pl.BlockSpec(memory_space=pl.ANY)
    shape = jax.ShapeDtypeStruct
    both = 2 * capacity
    out_shape = [
        shape((chips, both, width), BF16),
        shape((chips, both, width), BF16),
        shape((chips, both, hidden_width), BF16),
        shape((chips, both, hidden_width), BF16),
        shape((chips, both, hidden_width), BF16),
        shape((chips, length, width), BF16),
        shape((chips, length, width), BF16),
        shape((group, 1, length), F32),
    ]
    dma = pltpu.SemaphoreType.DMA
    scratch = [
        pltpu.VMEM((width, hidden_width), BF16),
        pltpu.VMEM((width, hidden_width), BF16),
        pltpu.VMEM((hidden_width, width), BF16),
        pltpu.VMEM((group, length, width), BF16),
        pltpu.VMEM((2, 2, length, width), BF16),
        pltpu.VMEM((both, width), BF16),
        pltpu.VMEM((both, width), BF16),
        pltpu.VMEM((both, width), BF16),
        pltpu.VMEM((both, 1), F32),
        pltpu.VMEM((both, width), F32),
        pltpu.VMEM((both, width), F32),
        pltpu.VMEM((2, 3, both, unit), BF16),
        pltpu.VMEM((2, length, width), BF16),
        pltpu.VMEM((2, length, width), BF16),
        pltpu.VMEM((2, chips, length, width), BF16),
        pltpu.VMEM((2, length, width), BF16),
        dma((3,)),
        dma((2,)),
        dma((2,)),
        dma((2, 3)),
        dma((2,)),
        dma((2, chips)),
        dma((2, chips)),
        dma((ChainGather.copies(chips),)),
        dma((ChainGather.copies(chips),)),
        dma,
    ]
    return pl.pallas_call(
        functools.partial(middle_kernel, chips=chips, capacity=capacity),
        out_shape=out_shape,
        in_specs=[vmem] * 2 + [anywhere] * 4,
        out_specs=[anywhere] * 7 + [vmem],
        scratch_shapes=scratch,
        compiler_params=pltpu.CompilerParams(
            collective_id=ident, has_side_effects=True, vmem_limit_bytes=VMEM_BYTES
        ),
    )(h2, table_all, cot_all, *expert_weights)


class ChainReduce:
    def __init__(self, own, from_left, from_right, send, recv, at, chips):
        self.own, self.from_left, self.from_right = own, from_left, from_right
        self.send, self.recv, self.at, self.chips = send, recv, at, chips

    @staticmethod
    def scratch(shape):
        return [pltpu.VMEM(shape, BF16)] * 3

    def copy(self, block, right):
        index = block if right else self.chips + block
        landing = self.from_left if right else self.from_right
        return remote(
            self.own.at[block],
            landing.at[block],
            self.send.at[index],
            self.recv.at[index],
            self.at["dev_right" if right else "dev_left"],
        )

    def tick(self, step):
        z, chips = self.at["z"], self.chips

        @pl.when(step >= z)
        def _():
            far = chips - 1 - step + z

            @pl.when(z > 0)
            def _():
                self.copy(far, True).wait_recv()
                self.own[far] = (self.own[far].astype(F32) + self.from_left[far].astype(F32)).astype(BF16)

            self.copy(far, True).start()

        @pl.when(step >= chips - 1 - z)
        def _():
            near = step - (chips - 1 - z)

            @pl.when(z < chips - 1)
            def _():
                self.copy(near, False).wait_recv()
                self.own[near] = (self.own[near].astype(F32) + self.from_right[near].astype(F32)).astype(BF16)

            self.copy(near, False).start()

    def value(self):
        z, chips = self.at["z"], self.chips
        pl.when(z > 0)(lambda: self.copy(z, True).wait_recv())
        pl.when(z < chips - 1)(lambda: self.copy(z, False).wait_recv())
        total = self.own[z].astype(F32)
        total += jnp.where(z > 0, self.from_left[z].astype(F32), 0.0)
        return total + jnp.where(z < chips - 1, self.from_right[z].astype(F32), 0.0)

    def sent(self):
        for step in range(1, self.chips):
            pl.when(self.at["z"] < self.chips - step)(lambda: self.copy(self.chips - step, True).wait_send())
            pl.when(self.at["z"] > step - 1)(lambda: self.copy(step - 1, False).wait_send())


class PlaneReduce:
    COPIES = 6

    def __init__(self, src, got, hold, last, send, recv, at):
        self.src, self.got, self.hold, self.last = src, got, hold, last
        self.send, self.recv, self.at = send, recv, at
        self.half = src.shape[1] // 2

    @staticmethod
    def scratch(shape):
        half = shape[1] // 2
        return [
            pltpu.VMEM((4, half, shape[2]), BF16),
            pltpu.VMEM((2, half, shape[2]), BF16),
            pltpu.VMEM((2, half, shape[2]), BF16),
        ]

    def copy(self, slot):
        at, half = self.at, self.half
        shard = (at["sx"], at["sd"], at["sy"], at["sd"])[slot]
        rows = pl.ds(slot // 2 * half, half)
        device = at["dev_x"] if slot < 2 else at["dev_y"]
        return remote(
            self.src.at[shard, rows, :], self.got.at[slot], self.send.at[slot], self.recv.at[slot], device
        )

    def first(self, slots=(1, 3, 0, 2)):
        for slot in slots:
            self.copy(slot).start()

    def first_of(self, index):
        for k, slots in enumerate(((1, 3), (0,), (2,))):
            pl.when(index == k)(lambda: self.first(slots))

    def onward(self, turn):
        return remote(
            self.hold.at[turn],
            self.last.at[turn],
            self.send.at[4 + turn],
            self.recv.at[4 + turn],
            self.at["dev_x"] if turn else self.at["dev_y"],
        )

    def second(self):
        at, half = self.at, self.half
        for turn, shard in enumerate((at["sy"], at["sx"])):
            slot = 2 * turn + 1
            self.copy(slot).wait_recv()
            mine = self.src[shard, pl.ds(turn * half, half), :]
            self.hold[turn] = (mine.astype(F32) + self.got[slot].astype(F32)).astype(BF16)
            self.onward(turn).start()

    def value(self, turn):
        half = self.half
        self.copy(2 * turn).wait_recv()
        self.onward(turn).wait_recv()
        mine = self.src[self.at["shard"], pl.ds(turn * half, half), :]
        return (mine.astype(F32) + self.got[2 * turn].astype(F32)) + self.last[turn].astype(F32)

    def sent(self):
        for slot in range(4):
            self.copy(slot).wait_send()
        for turn in range(2):
            self.onward(turn).wait_send()


def plane_blocks(at, index, plane):
    if not plane:
        return index
    order = [at["sd"], at["sx"], at["sy"], at["shard"]]
    return sum(jnp.where(index == k, shard, 0) for k, shard in enumerate(order))


def weights_kernel(*refs, plane, chips, shards):
    (dots_ref, route_ref, rows_hbm, grad_hbm, h2_hbm, cot_hbm, hid_hbm, da_hbm, db_hbm, back_hbm), refs = refs[:10], refs[10:]
    (sg_hbm, su_hbm, sd_hbm), refs = refs[:3], refs[3:]
    (down_out, sown, sgot, refs) = refs[0], refs[1:4], refs[4:7], refs[7:]
    (gate_out, up_out, sum_ref, sy_ref, chosen_ref), refs = refs[:5], refs[5:]
    (rows_ref, grad_ref, h2_ref, cot_ref, down_blocks, in_sem, down_sem), refs = refs[:7], refs[7:]
    (sg_w, su_w, sd_w, sgg_s, sug_s, sdg_s, s_sem, sg_sem, sg_send, sg_recv), refs = refs[:10], refs[10:]
    (chunk, own, from_left, from_right, dots_got), refs = refs[:5], refs[5:]
    (own_sem, chunk_sem, dots_send, dots_recv, chain_send, chain_recv), refs = refs[:6], refs[6:]
    block = chunk.shape[-1]
    at = place()
    me, group, core = at["expert"], 2 * chips, at["core"]
    width = h2_ref.shape[1]
    load = pltpu.make_async_copy(back_hbm, own, own_sem)
    load.start()
    inputs = [
        pltpu.make_async_copy(a, b, in_sem.at[k])
        for k, (a, b) in enumerate(
            [(rows_hbm, rows_ref), (grad_hbm, grad_ref), (h2_hbm, h2_ref), (cot_hbm, cot_ref)]
        )
    ]
    for made in inputs:
        made.start()
    peers = [(lax.rem(me + k, group), at["shard"]) for k in range(1, group)]
    meet(peers + ([at["dev_x"], at["dev_y"]] if plane else []))
    if plane:
        send, recv, *work = refs
        reduces = [
            PlaneReduce(work[4 * k], *work[4 * k + 1 : 4 * k + 4], send.at[k], recv.at[k], at) for k in range(2)
        ]
        targets = [work[0], work[4], down_blocks]
    else:
        targets = [gate_out, up_out, down_blocks]
    sources = [da_hbm, db_hbm, hid_hbm]
    dots = [
        remote(dots_ref.at[peer[0]], dots_got.at[me], dots_send.at[k], dots_recv.at[k], peer)
        for k, peer in enumerate(peers)
    ]

    def fetch(array, index):
        shard = plane_blocks(at, index, plane)
        slot = index % 2
        return pltpu.make_async_copy(
            sources[array].at[:, columns(shard * block, block)], chunk.at[slot], chunk_sem.at[slot]
        )

    def make(array, low, high):
        @pl.loop(low, high)
        def _(index):
            fetch(array, index).wait()
            pl.when(index + 1 < shards)(lambda: fetch(array, index + 1).start())
            if array < 2:
                pl.when(index + 1 == shards)(lambda: fetch(array + 1, 0).start())
            shard = plane_blocks(at, index, plane)
            held = chunk[index % 2]
            if array < 2:
                targets[array][shard] = dot_tn(rows_ref[...], held).astype(BF16)
                if plane:
                    reduces[array].first_of(index)
            else:
                targets[array][shard] = dot_tn(held, grad_ref[...]).astype(BF16)

    def load_shared(k, slot):
        return [
            pltpu.make_async_copy(sg_hbm.at[pl.ds(k * width, width), :], sg_w.at[slot], s_sem.at[slot, 0]),
            pltpu.make_async_copy(su_hbm.at[pl.ds(k * width, width), :], su_w.at[slot], s_sem.at[slot, 1]),
            pltpu.make_async_copy(sd_hbm.at[pl.ds(k * block, block), :], sd_w.at[slot], s_sem.at[slot, 2]),
        ]


    sy_ref[...] = jnp.zeros_like(sy_ref)
    sum_ref[...] = jnp.zeros_like(sum_ref)

    def shared_copies(k):
        stay, over = [], []
        for n, held in enumerate((sgg_s, sug_s, sdg_s)):
            half = held.shape[0] // 2
            mine, other = (held.at[pl.ds(pl.multiple_of(c * half, 16), half), :] for c in (core, 1 - core))
            stay.append((mine, sown[n].at[k], sg_sem.at[n]))
            over.append((other, sgot[n].at[k], sg_send.at[n], sg_recv.at[n, k], at["dev_c"]))
        return stay, over

    def shared_settle(k):
        stay, over = shared_copies(k)
        for copy in stay:
            pltpu.make_async_copy(*copy).wait()
        for copy in over:
            remote(*copy).wait_send()

    def shared_block(k):
        slot = k % 2
        for load in load_shared(k, slot):
            load.wait()

        @pl.when(k + 1 < shards)
        def _():
            for load in load_shared(k + 1, 1 - slot):
                load.start()

        hidden, gate_grad, up_grad, result, back = gated_block(
            h2_ref[...], cot_ref[...], sg_w[slot], su_w[slot], sd_w[slot]
        )
        sy_ref[...] += result
        sum_ref[...] += back
        pl.when(k > 0)(lambda: shared_settle(k - 1))
        sgg_s[...] = dot_tn(h2_ref[...], gate_grad).astype(BF16)
        sug_s[...] = dot_tn(h2_ref[...], up_grad).astype(BF16)
        sdg_s[...] = dot_tn(hidden, cot_ref[...]).astype(BF16)
        stay, over = shared_copies(k)
        for copy in stay:
            pltpu.make_async_copy(*copy).start()
        for copy in over:
            remote(*copy).start()

    for made in load_shared(0, 0):
        made.start()
    fetch(0, 0).start()
    chain = ChainReduce(own, from_left, from_right, chain_send, chain_recv, at, chips)
    load.wait()
    chain.tick(0)
    for made in dots:
        made.start()
    dots_got[me] = dots_ref[me]
    for made in inputs[:1]:
        made.wait()
    make(0, 0, shards)
    make(1, 0, shards // 2)
    for step in range(1, chips - 2):
        chain.tick(step)
    make(1, shards // 2, shards)
    for made in inputs[1:]:
        made.wait()
    make(2, 0, shards)
    store_down = pltpu.make_async_copy(down_blocks, down_out, down_sem)
    store_down.start()
    chain.tick(chips - 2)
    if plane:
        reduces[0].second()
    pl.loop(0, shards // 2)(shared_block)
    if plane:
        reduces[1].second()
    pl.loop(shards // 2, shards)(shared_block)
    for made in dots:
        made.wait()
    for k in range(TOP):
        chosen_ref[pl.ds(k, 1), :] = sum(
            jnp.where(route_ref[pl.ds(k, 1), :] == e, dots_got[e], 0.0) for e in range(group)
        )
    if plane:
        for turn in range(2):
            gate_out[pl.ds(turn * reduces[0].half, reduces[0].half), :] = reduces[0].value(turn)
    sum_ref[...] += chain.value()
    chain.sent()
    shared_settle(shards - 1)

    @pl.loop(0, shards)
    def _(k):
        for copy in shared_copies(k)[1]:
            remote(*copy).wait_recv()

    if plane:
        for turn in range(2):
            up_out[pl.ds(turn * reduces[1].half, reduces[1].half), :] = reduces[1].value(turn)
        for reduce in reduces:
            reduce.sent()
    store_down.wait()


def weights(dots, route_rows, rows, grad_rows, h2, cot_low, hidden, gate_grad, up_grad, back_part, shared, ident):
    chips, length, width = back_part.shape
    shards = lax.axis_size("shard")
    plane = shards == 4
    count, hidden_width = hidden.shape
    block, part = hidden_width // shards, shared[0].shape[1]
    vmem, anywhere = pl.BlockSpec(memory_space=pltpu.VMEM), pl.BlockSpec(memory_space=pl.ANY)
    shape, dma = jax.ShapeDtypeStruct, pltpu.SemaphoreType.DMA
    wide = (shards, width, block)
    scratch = [
        pltpu.VMEM((count, width), BF16),
        pltpu.VMEM((count, width), BF16),
        pltpu.VMEM((length, width), BF16),
        pltpu.VMEM((length, width), BF16),
        pltpu.VMEM((shards, block, width), BF16),
        dma((4,)),
        dma,
        pltpu.VMEM((2, width, part), BF16),
        pltpu.VMEM((2, width, part), BF16),
        pltpu.VMEM((2, part, width), BF16),
        pltpu.VMEM((width, part), BF16),
        pltpu.VMEM((width, part), BF16),
        pltpu.VMEM((part, width), BF16),
        dma((2, 3)),
        dma((3,)),
        dma((3,)),
        dma((3, shards)),
        pltpu.VMEM((2, count, block), BF16),
        *ChainReduce.scratch((chips, length, width)),
        pltpu.VMEM(dots.shape, F32),
    ]
    scratch += [dma, dma((2,)), dma((2 * chips - 1,)), dma((2 * chips - 1,)), dma((2 * chips,)), dma((2 * chips,))]
    if plane:
        out_shape = [shape((width, block), F32)] * 2
        scratch += [dma((2, PlaneReduce.COPIES))] * 2
        scratch += ([pltpu.VMEM(wide, BF16)] + PlaneReduce.scratch(wide)) * 2
    else:
        out_shape = [shape(wide, BF16)] * 2
    halves = [shape((shards, width // 2, part), BF16)] * 2 + [shape((shards, part // 2, width), BF16)]
    out_shape = [shape((shards, block, width), BF16), *halves, *halves, *out_shape]
    out_shape += [shape((length, width), F32)] * 2 + [shape((TOP, length), F32)]
    return pl.pallas_call(
        functools.partial(weights_kernel, plane=plane, chips=chips, shards=shards),
        out_shape=out_shape,
        in_specs=[vmem] * 2 + [anywhere] * 11,
        out_specs=[anywhere] * 7 + [vmem] * 5,
        scratch_shapes=scratch,
        compiler_params=pltpu.CompilerParams(
            collective_id=ident, has_side_effects=True, vmem_limit_bytes=VMEM_BYTES
        ),
    )(dots, route_rows, rows, grad_rows, h2, cot_low, hidden, gate_grad, up_grad, back_part, *shared)


def norm_back(source, inverse, gain, grad_in):
    scaled = grad_in * gain
    gain_grad = jnp.sum(grad_in * source * inverse, axis=0, keepdims=True)
    input_part = inverse * scaled - source * inverse**3 * jnp.mean(
        scaled * source, axis=-1, keepdims=True
    )
    return (gain_grad, input_part)


def rear_kernel(*refs, plane, chips, shards):
    (prefix, gains_ref, cos_ref, sin_ref), sources, refs = refs[:4], refs[4:15], refs[15:]
    halves, refs = (refs[:6], refs[6:]) if plane else ([], refs)
    (mix_out, input_grad_out, qkv_grad_out, gain_out), refs = refs[:4], refs[4:]
    pieces, refs = (refs[:4], refs[4:]) if plane else (refs[:1], refs[1:])
    held, refs = refs[:11], refs[11:]
    own, resid_ref, dh_ref, cot_ref, out_ref, att_ref, rot_ref, lse_ref, h1_ref, qkv_ref, x_ref = held
    (bias_ref, dres_ref, datt_ref, dqkv_ref, qkv_grad_ref, out_grad_ref, from_left, from_right), refs = refs[:8], refs[8:]
    (load_sem, store_sem, chain_send, chain_recv), refs = refs[:4], refs[4:]
    length, width = x_ref.shape
    at = place()
    core = at["core"]
    loads = [pltpu.make_async_copy(a, b, load_sem.at[k]) for k, (a, b) in enumerate(zip(sources, held))]
    loads[0].start()
    reduces = []
    if plane:
        (send, recv, half_sem, core_send, core_recv), work = refs[:5], refs[5:]
        work = [work[5 * k : 5 * k + 5] for k in range(4)]
        half_loads = [
            [pltpu.make_async_copy(halves[2 * k + n], work[k][n], half_sem.at[k, n]) for n in range(2)]
            for k in range(3)
        ]
        for two in half_loads:
            for made in two:
                made.start()
        reduces = [PlaneReduce(work[k][0], *work[k][2:], send.at[k], recv.at[k], at) for k in range(4)]
        count = work[3][0].shape[1]
        swaps = [
            remote(
                out_grad_ref.at[k, pl.ds(pl.multiple_of((1 - core) * count, 16), count), :],
                work[3][1].at[k],
                core_send.at[k],
                core_recv.at[k],
                at["dev_c"],
            )
            for k in range(shards)
        ]
    for made in loads[1:]:
        made.start()
    chain_meet(at, chips, [at["dev_x"], at["dev_y"], at["dev_c"]] if plane else [])
    chain = ChainReduce(own, from_left, from_right, chain_send, chain_recv, at, chips)
    loads[0].wait()
    chain.tick(0)
    for made in loads[1:6]:
        made.wait()
    resid = resid_ref[...]
    inverse = lax.rsqrt(jnp.mean(resid * resid, axis=-1, keepdims=True) + EPS)
    gain_two_grad, extra = norm_back(resid, inverse, gains_ref[pl.ds(1, 1), :], dh_ref[...])
    dres = cot_ref[...] + extra
    dres_ref[...] = dres
    low_dres = dres.astype(BF16)
    out_grad = dot_tn(att_ref[...], low_dres).astype(BF16)
    rows = width // shards
    for k in range(shards):
        out_grad_ref[k] = out_grad[k * rows : (k + 1) * rows]

    def add_halves(k):
        @pl.loop(0, shards)
        def _(shard):
            work[k][0][shard] = (
                work[k][0][shard].astype(F32) + work[k][1][shard].astype(F32)
            ).astype(BF16)

        reduces[k].first()

    if plane:
        for made in swaps:
            made.start()
        for k in range(3):
            for made in half_loads[k]:
                made.wait()
            add_halves(k)
        for k in range(shards):
            work[3][0][k] = out_grad_ref[k, pl.ds(pl.multiple_of(core * count, 16), count), :]
        for made in swaps:
            made.wait()
        add_halves(3)
    else:
        store_out = pltpu.make_async_copy(out_grad_ref, pieces[0], store_sem.at[3])
        store_out.start()
    datt_ref[...] = dot_nt(low_dres, out_ref[...]).astype(BF16)
    set_bias(bias_ref, prefix)
    scale = HEAD_DIM**-0.5
    for made in loads[6:]:
        made.wait()

    block = length // 2

    def pair(j):
        queries, keys, values = (
            rot_ref[:, columns(part * width + j * 128, 128)] for part in range(3)
        )
        grads = datt_ref[:, columns(j * 128, 128)]
        low = lax.broadcasted_iota(jnp.int32, (block, 128), 1) < HEAD_DIM
        lanes = lax.broadcasted_iota(jnp.int32, (block, 128), 1)

        def keep(part, rows, value):
            if part < 2:
                value = value * cos_ref[rows, :] - partner(value) * sin_ref[rows, :]
            dqkv_ref[rows, columns(part * width + j * 128, 128)] = value.astype(BF16)

        sums = []
        for start in range(0, length, block):
            rows, seen = pl.ds(start, block), start + block
            query = two_heads(queries[start:seen] * scale)
            grad = two_heads(grads[start:seen])
            bias, lse = bias_ref[rows, :seen], lse_ref[rows, :]
            logsum = jnp.concatenate(
                [
                    jnp.sum(jnp.where(lanes == 2 * j + head, lse, 0.0), axis=1, keepdims=True)
                    for head in range(2)
                ],
                axis=0,
            )
            scores = dot_nt(query, keys[:seen])
            scores = jnp.concatenate([scores[:block] + bias, scores[block:] + bias], axis=0)
            probs = jnp.exp(scores - logsum)
            probs_grad = dot_nt(grad, values[:seen])
            inner = jnp.sum(probs * probs_grad, axis=-1, keepdims=True)
            score_grad = (probs * (probs_grad - inner)).astype(BF16)
            query_grad = dot_nn(score_grad, keys[:seen]) * scale
            keep(0, rows, jnp.where(low, query_grad[:block], query_grad[block:]))
            sums.append((dot_tn(score_grad, query), dot_tn(probs.astype(BF16), grad)))
        for part in range(2):
            keep(1 + part, pl.ds(0, block), sums[0][part] + sums[1][part][:block])
            keep(1 + part, pl.ds(block, block), sums[1][part][block:])

    pairs = width // 128
    pl.loop(0, pairs // 3)(pair)
    for step in range(1, chips - 2):
        chain.tick(step)
    pl.loop(pairs // 3, pairs)(pair)

    @pl.loop(0, 3 * width // 256)
    def _(k):
        cols = columns(k * 256, 256)
        qkv_grad_ref[:, cols] = dot_tn(h1_ref[...], dqkv_ref[:, cols]).astype(BF16)

    stores = [pltpu.make_async_copy(qkv_grad_ref, qkv_grad_out, store_sem.at[0])]
    stores[0].start()
    chain.tick(chips - 2)
    for reduce in reduces:
        reduce.second()
    dh1 = dot_nt(dqkv_ref[...], qkv_ref[...])
    x = x_ref[...]
    inverse = lax.rsqrt(jnp.mean(x * x, axis=-1, keepdims=True) + EPS)
    gain_one_grad, extra = norm_back(x, inverse, gains_ref[pl.ds(0, 1), :], dh1)
    dres_ref[...] += extra
    stores.append(pltpu.make_async_copy(dres_ref, input_grad_out, store_sem.at[1]))
    stores[1].start()
    index = lax.broadcasted_iota(jnp.int32, gain_out.shape[1:], 0)
    gain_rows = jnp.where(index == 0, gain_one_grad, jnp.where(index == 1, gain_two_grad, 0.0)).astype(BF16)
    for k in range(shards):
        gain_out[k] = gain_rows
    for reduce, piece in zip(reduces, pieces):
        count = piece.shape[1]
        both = jnp.concatenate([reduce.value(0), reduce.value(1)], axis=0)
        for k in range(chips):
            piece[k] = both[k * count : (k + 1) * count].astype(BF16)
        reduce.sent()
    resid_ref[...] = chain.value()
    stores.append(pltpu.make_async_copy(resid_ref, mix_out, store_sem.at[2]))
    stores[2].start()
    chain.sent()
    if not plane:
        stores.append(store_out)
    for made in stores:
        made.wait()


def rear(prefix, inputs, cotangent, resid, dh2, gains, kept, full, mix_part, halves, ident):
    length, width = inputs.shape
    chips, shards = mix_part.shape[0], lax.axis_size("shard")
    plane = shards == 4
    cosine, sine = rope_lanes(length)
    turned, attended, normed_one, logsum = kept
    vmem, anywhere = pl.BlockSpec(memory_space=pltpu.VMEM), pl.BlockSpec(memory_space=pl.ANY)
    shape, dma = jax.ShapeDtypeStruct, pltpu.SemaphoreType.DMA
    sources = [mix_part, resid, dh2, cotangent, full[1], attended, turned, logsum, normed_one, full[0], inputs]
    operands = [prefix, gains, cosine, sine, *sources]
    in_specs = [pl.BlockSpec(memory_space=pltpu.SMEM)] + [vmem] * 3 + [anywhere] * 11
    out_blocks = (shards, width // shards, width)
    out_shape = [
        shape((length, width), F32),
        shape((length, width), F32),
        shape((width, 3 * width), BF16),
        shape((shards, 64, width), BF16),
    ]
    out_specs = [anywhere] * 3 + [vmem]
    scratch = [pltpu.VMEM(v.shape, v.dtype) for v in sources]
    scratch += [
        pltpu.VMEM((length, length), F32),
        pltpu.VMEM((length, width), F32),
        pltpu.VMEM((length, width), BF16),
        pltpu.VMEM((length, 3 * width), BF16),
        pltpu.VMEM((width, 3 * width), BF16),
        pltpu.VMEM(out_blocks, BF16),
        *ChainReduce.scratch((chips, length, width))[:2],
        dma((11,)),
        dma((4,)),
        dma((2 * chips,)),
        dma((2 * chips,)),
    ]
    if plane:
        operands += halves
        in_specs += [anywhere] * 6
        out_specs += [vmem] * 4
        scratch += [dma((4, PlaneReduce.COPIES))] * 2 + [dma((3, 2))] + [dma((shards,))] * 2
        half_shapes = [v.shape for v in halves[::2]] + [(shards, out_blocks[1] // 2, width)]
        for s in half_shapes:
            out_shape.append(shape((chips, s[1] // chips, s[2]), BF16))
            scratch += [pltpu.VMEM(s, BF16)] * 2 + PlaneReduce.scratch(s)
    else:
        out_shape.append(shape(out_blocks, BF16))
        out_specs.append(anywhere)
    return pl.pallas_call(
        functools.partial(rear_kernel, plane=plane, chips=chips, shards=shards),
        out_shape=out_shape,
        in_specs=in_specs,
        out_specs=out_specs,
        scratch_shapes=scratch,
        compiler_params=pltpu.CompilerParams(
            collective_id=ident, has_side_effects=True, vmem_limit_bytes=VMEM_BYTES
        ),
    )(*operands)


def last_kernel(*refs, chips, shards):
    (attention, pieces, down_hbm), refs = (refs[:2], refs[2:6], refs[6]), refs[7:]
    alls_out, down_out, refs = refs[:6], refs[6], refs[7:]
    halves, refs = [refs[3 * k : 3 * k + 3] for k in range(2)], refs[6:]
    plane_work, refs = refs[:10], refs[10:]
    chain_work, refs = [refs[4 * k : 4 * k + 4] for k in range(6)], refs[24:]
    load_sem, core_send, core_recv, plane_send, plane_recv, sums_send, sums_recv, all_send, all_recv, all_local = refs
    at = place()
    core = at["core"]
    loads, swaps = [], []
    for k in range(2):
        rows = attention[k].shape[1] // 2
        for n, c in enumerate((core, 1 - core)):
            part = attention[k].at[:, pl.ds(pl.multiple_of(c * rows, 16), rows), :]
            loads.append(pltpu.make_async_copy(part, halves[k][n], load_sem.at[2 * k + n]))
        swaps.append(remote(halves[k][1], halves[k][2], core_send.at[k], core_recv.at[k], at["dev_c"]))
    loads += [pltpu.make_async_copy(pieces[k], chain_work[2 + k][0], load_sem.at[4 + k]) for k in range(4)]
    loads.append(pltpu.make_async_copy(down_hbm, plane_work[0], load_sem.at[8]))
    for made in loads:
        made.start()
    sums = [
        ChainReduce(*chain_work[k][:3], sums_send.at[k], sums_recv.at[k], at, chips) for k in range(6)
    ]
    alls = [
        ChainGather(chain_work[k][3], alls_out[k], all_send.at[k], all_recv.at[k], all_local.at[k], at, chips)
        for k in range(6)
    ]
    planes = [
        PlaneReduce(src, *plane_work[1 + 3 * k : 4 + 3 * k], plane_send.at[k], plane_recv.at[k], at)
        for k, src in enumerate([plane_work[0], halves[0][0], halves[1][0]])
    ]
    shared, attn = (2, 3, 4, 5), (0, 1)
    chain_meet(at, chips, [at["dev_x"], at["dev_y"], at["dev_c"]])
    for k in attn:
        loads[2 * k].wait()
        loads[2 * k + 1].wait()
        swaps[k].start()

    def tick(group, step):
        for k in group:
            sums[k].tick(step)

    def step_all(group, step):
        for k in group:
            alls[k].step(step)

    def total(group):
        for k in group:
            chain_work[k][3][...] = sums[k].value().astype(BF16)
            alls[k].start()

    for k in range(4, 9):
        loads[k].wait()
    tick(shared, 0)
    for k in attn:
        swaps[k].wait()

        @pl.loop(0, shards)
        def _(shard):
            halves[k][0][shard] = (
                halves[k][0][shard].astype(F32) + halves[k][2][shard].astype(F32)
            ).astype(BF16)

        planes[1 + k].first()
    for step in range(1, chips - 1):
        tick(shared, step)
    for k in attn:
        planes[1 + k].second()
    planes[0].first()
    total(shared)
    step_all(shared, 1)
    for k in attn:
        count = chain_work[k][0].shape[1]
        both = jnp.concatenate([planes[1 + k].value(0), planes[1 + k].value(1)], axis=0)
        for n in range(chips):
            sums[k].own[n] = both[n * count : (n + 1) * count].astype(BF16)
    for step in range(chips - 1):
        tick(attn, step)
        if step:
            step_all(shared, step + 1)
    total(attn)
    planes[0].second()
    for step in range(1, chips):
        step_all(attn, step)
    for turn in range(2):
        down_out[pl.ds(turn * planes[0].half, planes[0].half), :] = planes[0].value(turn)
    for k in shared + attn:
        for step in range(chips):
            alls[k].finish(step)
        alls[k].sent()
        sums[k].sent()
    for reduce in planes:
        reduce.sent()


def last(qkv_grad, gain_grads, pieces, down_blocks, ident):
    shards, chips = lax.axis_size("shard"), lax.axis_size("expert") // 2
    vmem, anywhere = pl.BlockSpec(memory_space=pltpu.VMEM), pl.BlockSpec(memory_space=pl.ANY)
    shape, dma = jax.ShapeDtypeStruct, pltpu.SemaphoreType.DMA
    attention = [qkv_grad, gain_grads]
    half_shapes = [(shards, v.shape[1] // 2, v.shape[2]) for v in attention]
    chain_shapes = [(chips, v.shape[1] // 2 // chips, v.shape[2]) for v in attention] + [v.shape for v in pieces]
    out_shape = [shape((2 * chips,) + s[1:], BF16) for s in chain_shapes]
    out_shape.append(shape(down_blocks.shape[1:], F32))
    scratch = []
    for s in half_shapes:
        scratch += [pltpu.VMEM(s, BF16)] * 3
    scratch.append(pltpu.VMEM(down_blocks.shape, BF16))
    for s in [down_blocks.shape] + half_shapes:
        scratch += PlaneReduce.scratch(s)
    for s in chain_shapes:
        scratch += ChainReduce.scratch(s) + [pltpu.VMEM(s[1:], BF16)]
    scratch += [
        dma((9,)),
        dma((2,)),
        dma((2,)),
        dma((3, PlaneReduce.COPIES)),
        dma((3, PlaneReduce.COPIES)),
        dma((6, 2 * chips)),
        dma((6, 2 * chips)),
        dma((6, ChainGather.copies(chips))),
        dma((6, ChainGather.copies(chips))),
        dma((6,)),
    ]
    return pl.pallas_call(
        functools.partial(last_kernel, chips=chips, shards=shards),
        out_shape=out_shape,
        in_specs=[anywhere] * 7,
        out_specs=[vmem] * 7,
        scratch_shapes=scratch,
        compiler_params=pltpu.CompilerParams(
            collective_id=ident, has_side_effects=True, vmem_limit_bytes=VMEM_BYTES
        ),
    )(qkv_grad, gain_grads, *pieces, down_blocks)


def finish_kernel(*refs, chips, counts):
    total, results = sum(counts), sum(counts[:2]) + 1
    inputs, outputs, refs = refs[:total], refs[total : total + results], refs[total + results :]
    held, made, (load_sem, store_sem) = refs[:total], refs[total:-2], refs[-2:]
    plain, sums = counts[:2]
    loads = [pltpu.make_async_copy(a, b, load_sem.at[k]) for k, (a, b) in enumerate(zip(inputs, held))]
    ready = [*held[:plain], *made]
    stores = [
        pltpu.make_async_copy(a, b, store_sem.at[k]) for k, (a, b) in enumerate(zip(ready, outputs))
    ]
    for copy in loads:
        copy.start()
    for k in range(plain):
        loads[k].wait()
        stores[k].start()
    for k in range(plain, plain + sums):
        loads[k].wait()
        count = held[k].shape[1]
        if ready[k].shape[0] == count:
            ready[k][...] = held[k][0].astype(F32)
        else:
            for n in range(chips):
                for c in range(2):
                    ready[k][pl.ds((c * chips + n) * count, count), :] = held[k][2 * n + c].astype(F32)
        stores[k].start()
    for copy in loads[plain + sums :]:
        copy.wait()
    ready[-1][...] = sum(v[...] for v in held[plain + sums :])
    for copy in stores[plain + sums :]:
        copy.start()
    for copy in stores:
        copy.wait()


def finish(plain, sums, summands):
    chips = sums[0].shape[0] // 2
    shape, dma = jax.ShapeDtypeStruct, pltpu.SemaphoreType.DMA
    anywhere = pl.BlockSpec(memory_space=pl.ANY)
    inputs = [*plain, *sums, *summands]
    made = [shape(sums[0].shape[1:], F32)]
    made += [shape((v.shape[0] * v.shape[1], v.shape[2]), F32) for v in sums[1:]]
    made.append(shape(summands[0].shape, F32))
    out_shape = [shape(v.shape, F32) for v in plain] + made
    scratch = [pltpu.VMEM(v.shape, v.dtype) for v in inputs] + [pltpu.VMEM(s.shape, F32) for s in made]
    return pl.pallas_call(
        functools.partial(finish_kernel, chips=chips, counts=(len(plain), len(sums), len(summands))),
        out_shape=out_shape,
        in_specs=[anywhere] * len(inputs),
        out_specs=[anywhere] * len(out_shape),
        scratch_shapes=scratch + [dma((len(inputs),)), dma((len(out_shape),))],
        compiler_params=pltpu.CompilerParams(vmem_limit_bytes=VMEM_BYTES),
    )(*inputs)


def on_device(
    inputs,
    cotangent,
    norm_one,
    qkv_weight,
    out_weight,
    norm_two,
    shared_gate,
    shared_up,
    shared_down,
    expert_gate,
    expert_up,
    expert_down,
    gate_weights,
    routes,
    prefix,
):
    length, width = inputs.shape
    experts, shards = lax.axis_size("expert"), lax.axis_size("shard")
    me, shard = lax.axis_index("expert"), lax.axis_index("shard")
    route_rows = routes.T
    (
        cot_all,
        table_all,
        normed_one,
        turned,
        attended,
        resid,
        normed_two,
        cot_low,
        logsum,
        gains,
        qkv_full,
        out_full,
        gate_blocks,
        up_blocks,
        down_full,
    ) = front(
        prefix,
        inputs,
        cotangent,
        route_rows,
        gate_weights.T,
        [norm_one, norm_two],
        [qkv_weight, out_weight, shared_gate, shared_up, shared_down],
        1,
    )
    (
        rows,
        grad_rows,
        hidden,
        gate_pre_grad,
        up_pre_grad,
        mix_part,
        back_part,
        weight_back,
    ) = middle(normed_two, table_all, cot_all, [expert_gate, expert_up, expert_down], 2)
    rows, grad_rows, hidden, gate_pre_grad, up_pre_grad = (
        v.reshape(-1, v.shape[-1]) for v in (rows, grad_rows, hidden, gate_pre_grad, up_pre_grad)
    )
    down_term, *shared_halves, gate_term, up_term, normed_two_grad, shared_out, gate_weights_grad = weights(
        weight_back,
        route_rows,
        rows,
        grad_rows,
        normed_two,
        cot_low,
        hidden,
        gate_pre_grad,
        up_pre_grad,
        back_part,
        [gate_blocks, up_blocks, down_full],
        3,
    )
    shared_halves = [shared_halves[k + n] for k in range(3) for n in (0, 3)]
    mixture, input_grad, qkv_grad, gain_grads, *pieces = rear(
        prefix,
        inputs,
        cotangent,
        resid,
        normed_two_grad,
        gains,
        [turned, attended, normed_one, logsum],
        [qkv_full, out_full],
        mix_part,
        shared_halves,
        4,
    )
    qkv_grad = qkv_grad.reshape(shards, width // shards, 3 * width)
    if shards == 4:
        qkv_sum, gain_sums, *pieces, down_term = last(qkv_grad, gain_grads, pieces, down_term, 5)
        input_grad, gate_term, up_term, down_term, gain_sums, qkv_sum, *shared_sums, out_sum, output = finish(
            [input_grad, gate_term, up_term, down_term], [gain_sums, qkv_sum, *pieces], [resid, mixture, shared_out]
        )
    else:

        def over_plane(value):
            return lax.psum_scatter(value, "shard", scatter_dimension=0, tiled=True)[0]

        def over_all(value):
            return lax.psum(over_plane(value), "expert").astype(F32)

        output = resid + mixture + shared_out
        gate_term, up_term, down_term = (
            over_plane(v).astype(F32) for v in (gate_term, up_term, down_term)
        )
        qkv_sum, gain_sums, out_sum = over_all(qkv_grad), over_all(gain_grads), over_all(pieces[0])
        shared_sums = []
        for own, got in zip(shared_halves[::2], shared_halves[1::2]):
            half = (own.astype(F32) + got.astype(F32)).astype(BF16)
            both = jnp.concatenate([jnp.where(me % 2 == c, half, 0) for c in range(2)], axis=1)
            shared_sums.append(over_all(both))
    part = width // shards
    gain_sums = lax.dynamic_slice(gain_sums[:2], (0, shard * part), (2, part))
    return (
        output,
        input_grad,
        gain_sums[0],
        qkv_sum,
        out_sum,
        gain_sums[1],
        *shared_sums,
        gate_term[None],
        up_term[None],
        down_term[None],
        gate_weights_grad.T,
    )


def solution(mesh):
    tokens = P(("expert", "shard"), None)
    in_specs = (
        tokens,
        tokens,
        P("shard"),
        P("shard", None),
        P("shard", None),
        P("shard"),
        P(None, "shard"),
        P(None, "shard"),
        P("shard", None),
        P("expert", None, None),
        P("expert", None, None),
        P("expert", None, None),
        tokens,
        tokens,
        P(("expert", "shard")),
    )
    out_specs = (
        tokens,
        tokens,
        P("shard"),
        P("shard", None),
        P("shard", None),
        P("shard"),
        P(None, "shard"),
        P(None, "shard"),
        P("shard", None),
        P("expert", None, "shard"),
        P("expert", None, "shard"),
        P("expert", "shard", None),
        tokens,
    )
    return jax.shard_map(
        on_device, mesh=mesh, in_specs=in_specs, out_specs=out_specs, check_vma=False
    )
```

```python
import functools

import jax
import jax.numpy as jnp
import numpy as np
from jax import lax
from jax.experimental import pallas as pl
from jax.experimental.pallas import tpu as pltpu
from jax.sharding import PartitionSpec as P

HEADS = 12
HEAD_DIM = 64
TOP = 2
EPS = 1e-06
MESH = pl.DeviceIdType.MESH
F32 = jnp.float32
BF16 = jnp.bfloat16
VMEM_BYTES = 63 << 20


def place():
    expert, shard = lax.axis_index("expert"), lax.axis_index("shard")
    core, x, y = expert % 2, shard % 2, shard // 2
    return dict(
        expert=expert,
        shard=shard,
        core=core,
        z=expert // 2,
        sx=2 * y + 1 - x,
        sy=2 * (1 - y) + x,
        sd=2 * (1 - y) + 1 - x,
        dev_x=(expert, 2 * y + 1 - x),
        dev_y=(expert, 2 * (1 - y) + x),
        dev_c=(expert + 1 - 2 * core, shard),
        dev_left=(expert - 2, shard),
        dev_right=(expert + 2, shard),
    )


def meet(devices):
    barrier = pltpu.get_barrier_semaphore()
    for device in devices:
        pl.semaphore_signal(barrier, inc=1, device_id=device, device_id_type=MESH)
    pl.semaphore_wait(barrier, len(devices))


def remote(src, dst, send, recv, device):
    return pltpu.make_async_remote_copy(
        src_ref=src, dst_ref=dst, send_sem=send, recv_sem=recv, device_id=device, device_id_type=MESH
    )


class PlaneGather:
    COPIES = 7

    def __init__(self, src, dst, send, recv, local, at):
        self.src, self.dst, self.at = src, dst, at
        self.send, self.recv, self.local = send, recv, local
        self.rows = src.shape[0]
        self.copies = []

    def view(self, shard, start, count):
        return self.dst.at[pl.ds(pl.multiple_of(shard * self.rows + start, 16), count), :]

    def copy(self, index):
        at, half, quarter = self.at, self.rows // 2, self.rows // 4
        start = at["core"] * half
        shard, low, count, device = (
            (at["shard"], start, half, at["dev_x"]),
            (at["shard"], start, half, at["dev_y"]),
            (at["sx"], start, quarter, at["dev_y"]),
            (at["sx"], start, half, at["dev_c"]),
            (at["sy"], start + quarter, quarter, at["dev_x"]),
            (at["sy"], start, half, at["dev_c"]),
            (at["sd"], start, half, at["dev_c"]),
        )[index]
        part = self.view(shard, low, count)
        return remote(part, part, self.send.at[index], self.recv.at[index], device)

    def own(self):
        return pltpu.make_async_copy(self.src, self.view(self.at["shard"], 0, self.rows), self.local)

    def load(self):
        self.own().start()

    def first(self):
        self.own().wait()
        for index in (0, 1):
            self.copy(index).start()

    def second(self):
        for index, onward in ((0, (2, 3)), (1, (4, 5))):
            self.copy(index).wait_recv()
            for k in onward:
                self.copy(k).start()

    def third(self):
        for index in (2, 4):
            self.copy(index).wait_recv()
        self.copy(6).start()

    def finish(self):
        for index in (3, 5, 6):
            self.copy(index).wait_recv()
        for index in range(self.COPIES):
            self.copy(index).wait_send()


class ChainGather:
    @staticmethod
    def copies(chips):
        return 4 * chips

    def __init__(self, src, dst, send, recv, local, at, chips, rows=None):
        self.src, self.dst, self.send, self.recv, self.local = src, dst, send, recv, local
        self.at, self.chips, self.rows = at, chips, rows
        if rows is not None:
            self.src = src.at[rows, :]

    def part(self, block):
        return self.dst.at[block] if self.rows is None else self.dst.at[block, self.rows, :]

    def copy(self, block, index, device, first=False):
        part = self.part(block)
        return remote(
            self.src if first else part, part, self.send.at[index], self.recv.at[index], self.at[device]
        )

    def right(self, step):
        at = self.at
        return self.copy((at["z"] - step + 1) * 2 + at["core"], step - 1, "dev_right", step == 1)

    def left(self, step):
        at = self.at
        return self.copy(
            (at["z"] + step - 1) * 2 + at["core"], self.chips + step - 1, "dev_left", step == 1
        )

    def over(self, step):
        at = self.at
        return self.copy(
            (at["z"] - step) * 2 + at["core"], (2 if step >= 0 else 3) * self.chips + abs(step), "dev_c", step == 0
        )

    def arrived(self, step, side):
        at = self.at
        if side == "left":
            return self.copy((at["z"] - step) * 2 + at["core"], step - 1, "dev_right")
        return self.copy((at["z"] + step) * 2 + at["core"], self.chips + step - 1, "dev_left")

    def start(self):
        at = self.at
        pl.when(at["z"] < self.chips - 1)(lambda: self.right(1).start())
        pl.when(at["z"] > 0)(lambda: self.left(1).start())
        self.over(0).start()
        self.own = pltpu.make_async_copy(self.src, self.part(at["expert"]), self.local)
        self.own.start()

    def step(self, step):
        at, chips = self.at, self.chips

        @pl.when(at["z"] - step >= 0)
        def _():
            self.arrived(step, "left").wait_recv()
            if step < chips - 1:
                pl.when(at["z"] < chips - 1)(lambda: self.right(step + 1).start())
            self.over(step).start()

        @pl.when(at["z"] + step < chips)
        def _():
            self.arrived(step, "right").wait_recv()
            if step < chips - 1:
                pl.when(at["z"] > 0)(lambda: self.left(step + 1).start())
            self.over(-step).start()

    def finish(self, step):
        at = self.at
        if step == 0:
            self.over(0).wait()
            self.own.wait()
            return
        pl.when(at["z"] - step >= 0)(lambda: self.over(step).wait())
        pl.when(at["z"] + step < self.chips)(lambda: self.over(-step).wait())

    def sent(self):
        at, chips = self.at, self.chips
        for step in range(1, chips):
            pl.when((at["z"] - step + 1 >= 0) & (at["z"] < chips - 1))(lambda: self.right(step).wait_send())
            pl.when((at["z"] + step - 1 < chips) & (at["z"] > 0))(lambda: self.left(step).wait_send())


def chain_meet(at, chips, others):
    barrier = pltpu.get_barrier_semaphore()
    for device in others:
        pl.semaphore_signal(barrier, inc=1, device_id=device, device_id_type=MESH)

    @pl.when(at["z"] > 0)
    def _():
        pl.semaphore_signal(barrier, inc=1, device_id=at["dev_left"], device_id_type=MESH)

    @pl.when(at["z"] < chips - 1)
    def _():
        pl.semaphore_signal(barrier, inc=1, device_id=at["dev_right"], device_id_type=MESH)

    ends = jnp.where(at["z"] == 0, 1, 0) + jnp.where(at["z"] == chips - 1, 1, 0)
    pl.semaphore_wait(barrier, len(others) + 2 - ends)


def dot_nn(left, right):
    return lax.dot_general(left, right, (((1,), (0,)), ((), ())), preferred_element_type=F32)


def dot_nt(left, right):
    return lax.dot_general(left, right, (((1,), (1,)), ((), ())), preferred_element_type=F32)


def dot_tn(left, right):
    return lax.dot_general(left, right, (((0,), (0,)), ((), ())), preferred_element_type=F32)


def columns(start, count):
    return pl.ds(pl.multiple_of(start, 128), count)


def rope_lanes(length):
    half = HEAD_DIM // 2
    frequency = 10000.0 ** (-np.arange(half) * 2.0 / HEAD_DIM)
    angles = np.arange(length)[:, None] * frequency[None, :]
    cosine, sine = np.cos(angles), np.sin(angles)
    return (
        jnp.asarray(np.concatenate([cosine] * 4, axis=1), F32),
        jnp.asarray(np.concatenate([-sine, sine] * 2, axis=1), F32),
    )


def partner(values):
    lane = lax.broadcasted_iota(jnp.int32, values.shape, 1)
    half = HEAD_DIM // 2
    ahead = pltpu.roll(values, 128 - half, 1)
    behind = pltpu.roll(values, half, 1)
    return jnp.where(lane % HEAD_DIM < half, ahead, behind)


def set_bias(bias_ref, prefix):
    shape = bias_ref.shape
    row = lax.broadcasted_iota(jnp.int32, shape, 0)
    col = lax.broadcasted_iota(jnp.int32, shape, 1)
    bias_ref[...] = jnp.where((col < prefix[0]) | (col <= row), 0.0, -1e30)


def two_heads(values):
    low = lax.broadcasted_iota(jnp.int32, values.shape, 1) < HEAD_DIM
    zero = jnp.zeros_like(values)
    return jnp.concatenate([jnp.where(low, values, zero), jnp.where(low, zero, values)], axis=0)


def front_kernel(*refs, plane, chips):
    (prefix, x_ref, cot_ref, route_ref, weight_ref, cos_ref, sin_ref), refs = refs[:7], refs[7:]
    gains_in, refs = refs[0], refs[1:]
    gain_pair = gains_in[...].astype(F32)
    weights, refs = refs[:2], refs[2:]
    (cot_out, table_out, h1_out, rot_out, att_out, resid_out, h2_out, cot_low, lse_ref, gains_ref), refs = refs[:10], refs[10:]
    full_out, refs = (refs[:2], refs[2:]) if plane else ([], refs)
    (h1_ref, rot_ref, att_ref, resid_ref, h2_ref, cot_low_ref), refs = refs[:6], refs[6:]
    (bias_ref, table_ref, table_all, cot_all, out_sem, chain_sem, chain_send, chain_recv, chain_local), refs = refs[:9], refs[9:]
    length, width = x_ref.shape
    experts = table_ref.shape[0] // 2
    at = place()
    if plane:
        gains_src, gains_full, full, (send, recv, local) = refs[0], refs[1], refs[2:4], refs[4:]
        gathers = [
            PlaneGather(a, b, send.at[k], recv.at[k], local.at[k], at)
            for k, (a, b) in enumerate(zip([*weights, gains_src], [*full, gains_full]))
        ]
        first = gathers[::-1]
        for k in range(2):
            gains_src[pl.ds(32 * k, 32), :] = jnp.broadcast_to(
                gain_pair[k : k + 1], (32, gain_pair.shape[1])
            ).astype(BF16)
        for gather in first:
            gather.load()
        qkv_full, out_full = full[:2]
    else:
        qkv_full, out_full = weights
    chain_meet(at, chips, [at["dev_x"], at["dev_y"], at["dev_c"]] if plane else [at["dev_c"]])
    if plane:
        for gather in first:
            gather.first()
    cot_low_ref[...] = cot_ref[...].astype(BF16)
    chains = [
        ChainGather(a, b, chain_send.at[k], chain_recv.at[k], chain_local.at[k], at, chips)
        for k, (a, b) in enumerate([(table_ref, table_all)])
    ]
    halves = [
        ChainGather(
            cot_low_ref, cot_all, chain_send.at[1 + k], chain_recv.at[1 + k], chain_local.at[1 + k], at, chips,
            pl.ds(k * length // 2, length // 2),
        )
        for k in range(2)
    ]
    ahead, behind = [*chains, halves[0]], halves[1:]
    for half in halves:
        half.start()
    names = lax.broadcasted_iota(jnp.int32, (experts, length), 0)
    chosen = [route_ref[pl.ds(k, 1), :] == names for k in range(TOP)]
    member = (chosen[0] | chosen[1]).astype(F32)
    earlier = (
        lax.broadcasted_iota(jnp.int32, (length, length), 0)
        < lax.broadcasted_iota(jnp.int32, (length, length), 1)
    ).astype(F32)
    slot = dot_nn(member.astype(BF16), earlier.astype(BF16))
    table_ref[:experts, :] = jnp.where(member > 0, slot, -1.0)
    table_ref[experts:, :] = sum(
        jnp.where(chosen[k], weight_ref[pl.ds(k, 1), :], 0.0) for k in range(TOP)
    )
    chains[0].start()
    chains += halves
    set_bias(bias_ref, prefix)
    keeps = []

    def keep(src, dst):
        made = pltpu.make_async_copy(src, dst, out_sem.at[len(keeps)])
        made.start()
        keeps.append(made)

    def each_kept(step, act):
        for n, side in enumerate((-1, 1) if step else (1,)):
            chip = at["z"] + side * step

            @pl.when((chip >= 0) & (chip < chips))
            def _():
                for k, (src, dst) in enumerate([(table_all, table_out), (cot_all, cot_out)]):
                    part = pl.ds(2 * chip, 2)
                    act(pltpu.make_async_copy(src.at[part], dst.at[part], chain_sem.at[step, n, k]))

    def keep_chain(step):
        each_kept(step, lambda made: made.start())

    keep(cot_low_ref, cot_low)
    for chain in ahead:
        chain.step(1)
    if plane:
        for gather in first:
            gather.second()
        for chain in behind:
            chain.step(1)
        for step in ("third", "finish"):
            for gather in first:
                getattr(gather, step)()
        for k in range(2):
            keep(full[k], full_out[k])
        blocks = range(gains_full.shape[0] // 64)
        for k in range(2):
            row = [gains_full[pl.ds(64 * n + 32 * k, 1), :].astype(F32) for n in blocks]
            gains_ref[pl.ds(k, 1), :] = jnp.concatenate(row, axis=1)
    else:
        for chain in behind:
            chain.step(1)
        gains_ref[pl.ds(0, 2), :] = gain_pair
    x = x_ref[...]
    inverse = lax.rsqrt(jnp.mean(x * x, axis=-1, keepdims=True) + EPS)
    h1_ref[...] = (x * inverse * gains_ref[pl.ds(0, 1), :]).astype(BF16)

    def project(block, turned):
        cols = columns(block * 256, 256)
        part = dot_nn(h1_ref[...], qkv_full[:, cols])
        if turned:
            part = jnp.concatenate(
                [v * cos_ref[...] + partner(v) * sin_ref[...] for v in (part[:, :128], part[:, 128:])], axis=1
            )
        rot_ref[:, cols] = part.astype(BF16)

    pl.loop(0, 2 * width // 256)(lambda block: project(block, True))
    pl.loop(2 * width // 256, 3 * width // 256)(lambda block: project(block, False))
    keep(h1_ref, h1_out)
    keep(rot_ref, rot_out)
    for chain in ahead:
        chain.step(2)
    lse_ref[...] = jnp.zeros_like(lse_ref)
    count = length // 2

    def pair(j):
        queries, keys, values = (
            rot_ref[:, columns(part * width + j * 128, 128)] for part in range(3)
        )
        low = lax.broadcasted_iota(jnp.int32, (count, 128), 1) < HEAD_DIM
        lanes = lax.broadcasted_iota(jnp.int32, (count, 128), 1)
        for start in range(0, length, count):
            rows, seen = pl.ds(start, count), start + count
            scores = dot_nt(two_heads(queries[start:seen] * HEAD_DIM**-0.5), keys[:seen])
            bias = bias_ref[rows, :seen]
            scores = jnp.concatenate([scores[:count] + bias, scores[count:] + bias], axis=0)
            peak = jnp.max(scores, axis=-1, keepdims=True)
            exponent = jnp.exp(scores - peak)
            total = jnp.sum(exponent, axis=-1, keepdims=True)
            out = dot_nn(exponent.astype(BF16), values[:seen]) * (1.0 / total)
            att_ref[rows, columns(j * 128, 128)] = jnp.where(low, out[:count], out[count:]).astype(BF16)
            logsum = peak + jnp.log(total)
            lse_ref[rows, :] = jnp.where(
                lanes == 2 * j,
                logsum[:count],
                jnp.where(lanes == 2 * j + 1, logsum[count:], lse_ref[rows, :]),
            )

    pairs = width // 128

    @pl.loop(0, pairs)
    def _(j):
        pair(j)

        @pl.when(j == pairs // 2 - 1)
        def _():
            for step in range(2, chips - 1):
                for chain in behind:
                    chain.step(step)
                for chain in ahead:
                    chain.step(step + 1)

    keep(att_ref, att_out)
    resid = x_ref[...] + dot_nn(att_ref[...], out_full[...])
    resid_ref[...] = resid
    keep(resid_ref, resid_out)
    inverse = lax.rsqrt(jnp.mean(resid * resid, axis=-1, keepdims=True) + EPS)
    h2_ref[...] = (resid * inverse * gains_ref[pl.ds(1, 1), :]).astype(BF16)
    keep(h2_ref, h2_out)
    for step in range(chips - 1):
        for chain in chains:
            chain.finish(step)
        keep_chain(step)
    for chain in behind:
        chain.step(chips - 1)
    for chain in chains:
        chain.finish(chips - 1)
    keep_chain(chips - 1)
    for chain in chains:
        chain.sent()
    for step in range(chips):
        each_kept(step, lambda made: made.wait())
    for made in keeps:
        made.wait()


def front(prefix, inputs, cotangent, route_rows, weight_rows, gains, weights, ident):
    length, width = inputs.shape
    group, shards = lax.axis_size("expert"), lax.axis_size("shard")
    chips, plane = group // 2, shards == 4
    cosine, sine = rope_lanes(length)
    vmem, anywhere = pl.BlockSpec(memory_space=pltpu.VMEM), pl.BlockSpec(memory_space=pl.ANY)
    if not plane:
        gains = lax.all_gather(gains, "shard", axis=1, tiled=True)
        weights = [lax.all_gather(v, "shard", axis=0, tiled=True) for v in weights]
    operands = [prefix, inputs, cotangent, route_rows, weight_rows, cosine, sine, gains]
    in_specs = [pl.BlockSpec(memory_space=pltpu.SMEM)] + [vmem] * 7
    operands += weights
    in_specs += [anywhere] * 2 if plane else [vmem] * 2
    shape, dma = jax.ShapeDtypeStruct, pltpu.SemaphoreType.DMA
    out_shape = [
        shape((group, length, width), BF16),
        shape((group, 2 * group, length), F32),
        shape((length, width), BF16),
        shape((length, 3 * width), BF16),
        shape((length, width), BF16),
        shape((length, width), F32),
        shape((length, width), BF16),
        shape((length, width), BF16),
        shape((length, 128), F32),
        shape((8, width), F32),
    ]
    out_specs = [anywhere] * 8 + [vmem] * 2
    scratch = [pltpu.VMEM(s.shape, s.dtype) for s in out_shape[2:8]]
    scratch += [
        pltpu.VMEM((length, length), F32),
        pltpu.VMEM((2 * group, length), F32),
        pltpu.VMEM((group, 2 * group, length), F32),
        pltpu.VMEM((group, length, width), BF16),
        dma((8,)),
        dma((chips, 2, 2)),
        dma((3, ChainGather.copies(chips))),
        dma((3, ChainGather.copies(chips))),
        dma((3,)),
    ]
    if plane:
        full = [(shards * v.shape[0], v.shape[1]) for v in weights]
        out_shape += [shape(s, BF16) for s in full]
        out_specs += [anywhere] * 2
        part = gains.shape[1]
        scratch += [pltpu.VMEM((64, part), BF16), pltpu.VMEM((64 * shards, part), BF16)]
        scratch += [pltpu.VMEM(s, BF16) for s in full]
        scratch += [dma((3, PlaneGather.COPIES)), dma((3, PlaneGather.COPIES)), dma((3,))]
    outs = pl.pallas_call(
        functools.partial(front_kernel, plane=plane, chips=chips),
        out_shape=out_shape,
        in_specs=in_specs,
        out_specs=out_specs,
        scratch_shapes=scratch,
        compiler_params=pltpu.CompilerParams(
            collective_id=ident, has_side_effects=True, vmem_limit_bytes=VMEM_BYTES
        ),
    )(*operands)
    return outs if plane else [*outs, *weights]


def near_order(chips):
    table = []
    for z in range(chips):
        others = sorted(range(chips), key=lambda s: (abs(s - z), abs(2 * s - chips + 1) * -1))
        table.append(others)
    return table


def pick(table, step, z):
    return sum(
        jnp.where((z == k) & (step == n), chip, 0) for k, row in enumerate(table) for n, chip in enumerate(row)
    )


def gated_block(rows, grad, gate, up, down):
    pre_gate = dot_nn(rows, gate)
    pre_up = dot_nn(rows, up)
    sigmoid = 1.0 / (1.0 + jnp.exp(-pre_gate))
    active = pre_gate * sigmoid
    hidden = (active * pre_up).astype(BF16)
    hidden_grad = dot_nt(grad, down)
    gate_grad = (hidden_grad * pre_up * (sigmoid * (1.0 + pre_gate * (1.0 - sigmoid)))).astype(BF16)
    up_grad = (hidden_grad * active).astype(BF16)
    result = dot_nn(hidden, down)
    back = dot_nt(gate_grad, gate) + dot_nt(up_grad, up)
    return hidden, gate_grad, up_grad, result, back


def middle_kernel(*refs, plane, chips, capacity):
    (h2_ref, table_ref, cot_all, gate_hbm, up_hbm, down_hbm), refs = refs[:6], refs[6:]
    shared, refs = (refs[:3], refs[3:]) if plane else ([], refs)
    (rows_out, grad_out, hid_out, da_out, db_out, mix_out, back_out, dots_out), refs = refs[:8], refs[8:]
    shared_out, refs = (refs[:3], refs[3:]) if plane else ([], refs)
    (gate_w, up_w, down_w, h2_all, cot_buf, rows_ref, grad_ref, cotr_ref, scale_ref), refs = refs[:9], refs[9:]
    (y_acc, r_acc, stage_f, stage_s, stage_t, got, total), refs = refs[:7], refs[7:]
    (w_sem, cot_sem, row_sem, f_sem, tot_sem, core_send, core_recv, chain_send, chain_recv, chain_local), refs = refs[:10], refs[10:]
    length, width = h2_ref.shape
    experts = 2 * chips
    unit = stage_f.shape[-1]
    units = gate_w.shape[1] // unit
    at = place()
    me, core, z = at["expert"], at["core"], at["z"]
    order = near_order(chips)
    gathers = []
    if plane:
        full, (send, recv, local, full_sem) = refs[:3], refs[3:]
        gathers = [
            PlaneGather(a, b, send.at[k], recv.at[k], local.at[k], at) for k, (a, b) in enumerate(zip(shared, full))
        ]
        for gather in gathers:
            gather.load()
        keeps = [pltpu.make_async_copy(a, b, full_sem.at[k]) for k, (a, b) in enumerate(zip(full, shared_out))]

    def load_cot(step):
        chip = pick(order, step, z)
        return pltpu.make_async_copy(cot_all.at[pl.ds(2 * chip, 2)], cot_buf, cot_sem)

    load_cot(0).start()
    loads = [
        pltpu.make_async_copy(a, b, w_sem.at[k])
        for k, (a, b) in enumerate([(gate_hbm.at[0], gate_w), (up_hbm.at[0], up_w), (down_hbm.at[0], down_w)])
    ]
    for load in loads:
        load.start()
    chain_meet(at, chips, [at["dev_x"], at["dev_y"], at["dev_c"]] if plane else [at["dev_c"]])
    chains = [
        ChainGather(
            h2_ref, h2_all, chain_send.at[k], chain_recv.at[k], chain_local.at[k], at, chips,
            pl.ds(k * length // 2, length // 2),
        )
        for k in range(2)
    ]
    for chain in chains:
        chain.start()
    for gather in gathers:
        gather.first()

    def one_hot(source):
        slots = table_ref[source, pl.ds(me, 1), :]
        return lax.broadcasted_iota(jnp.int32, (capacity, length), 0).astype(F32) == slots

    def row_copies(step):
        return [
            pltpu.make_async_copy(rows_ref, rows_out.at[step], row_sem.at[0]),
            pltpu.make_async_copy(grad_ref, grad_out.at[step], row_sem.at[1]),
        ]

    def hidden_copies(step, k):
        return [
            pltpu.make_async_copy(
                stage_f.at[k % 2, n], out.at[step, :, columns(k * unit, unit)], f_sem.at[k % 2, n]
            )
            for n, out in enumerate([hid_out, da_out, db_out])
        ]

    def core_copies(step):
        return [
            remote(
                stage.at[1 - core], got.at[n, step], core_send.at[n, step], core_recv.at[n, step], at["dev_c"]
            )
            for n, stage in enumerate([stage_s, stage_t])
        ]

    def total_copies(step):
        chip = pick(order, step, z)
        return [
            pltpu.make_async_copy(total.at[n], out.at[chip], tot_sem.at[n])
            for n, out in enumerate([mix_out, back_out])
        ]

    def each(copies, act):
        for copy in copies:
            getattr(copy, act)()

    def join(step):
        pl.when(step > 0)(lambda: each(total_copies(step - 1), "wait"))
        for n, (copy, stage) in enumerate(zip(core_copies(step), [stage_s, stage_t])):
            copy.wait()
            total[n] = (stage[core].astype(F32) + got[n, step].astype(F32)).astype(BF16)
        each(total_copies(step), "start")

    @pl.loop(0, chips)
    def _(step):
        for k in range(chips):

            @pl.when(step == k)
            def _():
                for chain in chains:
                    chain.finish(k)
                if k == 0:
                    each(loads, "wait")
                for gather in gathers:
                    if k == 1:
                        gather.second()
                    if k == 2:
                        gather.third()
                    if k == 3:
                        gather.finish()
                if plane and k == 3:
                    each(keeps, "start")

        chip = pick(order, step, z)
        load_cot(step).wait()
        pl.when(step > 0)(lambda: each(row_copies(step - 1), "wait"))
        for d in range(2):
            source, part = 2 * chip + d, pl.ds(d * capacity, capacity)
            chosen = one_hot(source)
            select = chosen.astype(F32).astype(BF16)
            rows_ref[part, :] = dot_nn(select, h2_all[source]).astype(BF16)
            cot_rows = dot_nn(select, cot_buf[d])
            scale = jnp.sum(
                jnp.where(chosen, table_ref[source, pl.ds(experts + me, 1), :], 0.0), axis=1, keepdims=True
            )
            grad_ref[part, :] = (cot_rows * scale).astype(BF16)
            cotr_ref[part, :] = cot_rows.astype(BF16)
            scale_ref[part, :] = scale
        pl.when(step + 1 < chips)(lambda: load_cot(step + 1).start())
        each(row_copies(step), "start")
        y_acc[...] = jnp.zeros_like(y_acc)
        r_acc[...] = jnp.zeros_like(r_acc)

        @pl.loop(0, units)
        def _(k):
            cols = columns(k * unit, unit)
            hidden, gate_grad, up_grad, result, back = gated_block(
                rows_ref[...], grad_ref[...], gate_w[:, cols], up_w[:, cols],
                down_w[pl.ds(pl.multiple_of(k * unit, unit), unit), :],
            )
            pl.when((step > 0) | (k >= 2))(lambda: each(hidden_copies(step, k), "wait"))
            stage_f[k % 2, 0] = hidden
            stage_f[k % 2, 1] = gate_grad
            stage_f[k % 2, 2] = up_grad
            each(hidden_copies(step, k), "start")
            y_acc[...] += result
            r_acc[...] += back
            for n in range(chips - 1):
                for event, chain in zip((max(0, units - 4), units - 2), chains):
                    pl.when((step == n) & (k == event))(lambda: chain.step(n + 1))

        pl.when(step > 0)(lambda: join(step - 1))
        result = y_acc[...].astype(BF16).astype(F32)
        dots = jnp.sum(result * cotr_ref[...].astype(F32), axis=1, keepdims=True)
        weighted = (result * scale_ref[...]).astype(BF16)
        back = r_acc[...].astype(BF16)
        for d in range(2):
            source = 2 * chip + d
            chosen = one_hot(source)
            select = chosen.astype(F32).astype(BF16)
            part = slice(d * capacity, (d + 1) * capacity)
            stage_s[d] = dot_tn(select, weighted[part]).astype(BF16)
            stage_t[d] = dot_tn(select, back[part]).astype(BF16)
            dots_out[source] = jnp.sum(jnp.where(chosen, dots[part], 0.0), axis=0, keepdims=True)
        each(core_copies(step), "start")

    join(chips - 1)
    each(total_copies(chips - 1), "wait")
    each(row_copies(chips - 1), "wait")
    for k in range(max(0, units - 2), units):
        each(hidden_copies(chips - 1, k), "wait")
    for chain in chains:
        chain.sent()
    if plane:
        each(keeps, "wait")


def middle(h2, table_all, cot_all, expert_weights, shared, ident):
    length, width = h2.shape
    group, shards = lax.axis_size("expert"), lax.axis_size("shard")
    chips, plane = group // 2, shards == 4
    capacity = 4 * length // group
    hidden_width = expert_weights[0].shape[2]
    unit = min(512, hidden_width)
    vmem, anywhere = pl.BlockSpec(memory_space=pltpu.VMEM), pl.BlockSpec(memory_space=pl.ANY)
    shape = jax.ShapeDtypeStruct
    both = 2 * capacity
    out_shape = [
        shape((chips, both, width), BF16),
        shape((chips, both, width), BF16),
        shape((chips, both, hidden_width), BF16),
        shape((chips, both, hidden_width), BF16),
        shape((chips, both, hidden_width), BF16),
        shape((chips, length, width), BF16),
        shape((chips, length, width), BF16),
        shape((group, 1, length), F32),
    ]
    dma = pltpu.SemaphoreType.DMA
    scratch = [
        pltpu.VMEM((width, hidden_width), BF16),
        pltpu.VMEM((width, hidden_width), BF16),
        pltpu.VMEM((hidden_width, width), BF16),
        pltpu.VMEM((group, length, width), BF16),
        pltpu.VMEM((2, length, width), BF16),
        pltpu.VMEM((both, width), BF16),
        pltpu.VMEM((both, width), BF16),
        pltpu.VMEM((both, width), BF16),
        pltpu.VMEM((both, 1), F32),
        pltpu.VMEM((both, width), F32),
        pltpu.VMEM((both, width), F32),
        pltpu.VMEM((2, 3, both, unit), BF16),
        pltpu.VMEM((2, length, width), BF16),
        pltpu.VMEM((2, length, width), BF16),
        pltpu.VMEM((2, chips, length, width), BF16),
        pltpu.VMEM((2, length, width), BF16),
        dma((3,)),
        dma,
        dma((2,)),
        dma((2, 3)),
        dma((2,)),
        dma((2, chips)),
        dma((2, chips)),
        dma((2, ChainGather.copies(chips))),
        dma((2, ChainGather.copies(chips))),
        dma((2,)),
    ]
    operands = [h2, table_all, cot_all, *expert_weights]
    in_specs = [vmem] * 2 + [anywhere] * 4
    out_specs = [anywhere] * 7 + [vmem]
    if plane:
        operands += shared
        in_specs += [anywhere] * 3
        full = [(shards * v.shape[0], v.shape[1]) for v in shared]
        out_shape += [shape(s, BF16) for s in full]
        out_specs += [anywhere] * 3
        scratch += [pltpu.VMEM(s, BF16) for s in full]
        scratch += [dma((3, PlaneGather.COPIES)), dma((3, PlaneGather.COPIES)), dma((3,)), dma((3,))]
    outs = pl.pallas_call(
        functools.partial(middle_kernel, plane=plane, chips=chips, capacity=capacity),
        out_shape=out_shape,
        in_specs=in_specs,
        out_specs=out_specs,
        scratch_shapes=scratch,
        compiler_params=pltpu.CompilerParams(
            collective_id=ident, has_side_effects=True, vmem_limit_bytes=VMEM_BYTES
        ),
    )(*operands)
    return outs if plane else [*outs, *[lax.all_gather(v, "shard", axis=0, tiled=True) for v in shared]]


class ChainReduce:
    def __init__(self, own, from_left, from_right, send, recv, at, chips):
        self.own, self.from_left, self.from_right = own, from_left, from_right
        self.send, self.recv, self.at, self.chips = send, recv, at, chips

    @staticmethod
    def scratch(shape):
        return [pltpu.VMEM(shape, BF16)] * 3

    def copy(self, block, right):
        index = block if right else self.chips + block
        landing = self.from_left if right else self.from_right
        return remote(
            self.own.at[block],
            landing.at[block],
            self.send.at[index],
            self.recv.at[index],
            self.at["dev_right" if right else "dev_left"],
        )

    def tick(self, step):
        z, chips = self.at["z"], self.chips

        @pl.when(step >= z)
        def _():
            far = chips - 1 - step + z

            @pl.when(z > 0)
            def _():
                self.copy(far, True).wait_recv()
                self.own[far] = (self.own[far].astype(F32) + self.from_left[far].astype(F32)).astype(BF16)

            self.copy(far, True).start()

        @pl.when(step >= chips - 1 - z)
        def _():
            near = step - (chips - 1 - z)

            @pl.when(z < chips - 1)
            def _():
                self.copy(near, False).wait_recv()
                self.own[near] = (self.own[near].astype(F32) + self.from_right[near].astype(F32)).astype(BF16)

            self.copy(near, False).start()

    def value(self):
        z, chips = self.at["z"], self.chips
        pl.when(z > 0)(lambda: self.copy(z, True).wait_recv())
        pl.when(z < chips - 1)(lambda: self.copy(z, False).wait_recv())
        total = self.own[z].astype(F32)
        total += jnp.where(z > 0, self.from_left[z].astype(F32), 0.0)
        return total + jnp.where(z < chips - 1, self.from_right[z].astype(F32), 0.0)

    def sent(self):
        for step in range(1, self.chips):
            pl.when(self.at["z"] < self.chips - step)(lambda: self.copy(self.chips - step, True).wait_send())
            pl.when(self.at["z"] > step - 1)(lambda: self.copy(step - 1, False).wait_send())


class PlaneReduce:
    COPIES = 6

    def __init__(self, src, got, hold, last, send, recv, at):
        self.src, self.got, self.hold, self.last = src, got, hold, last
        self.send, self.recv, self.at = send, recv, at
        self.half = src.shape[1] // 2

    @staticmethod
    def scratch(shape):
        half = shape[1] // 2
        return [
            pltpu.VMEM((4, half, shape[2]), BF16),
            pltpu.VMEM((2, half, shape[2]), BF16),
            pltpu.VMEM((2, half, shape[2]), BF16),
        ]

    def copy(self, slot):
        at, half = self.at, self.half
        shard = (at["sx"], at["sd"], at["sy"], at["sd"])[slot]
        rows = pl.ds(slot // 2 * half, half)
        device = at["dev_x"] if slot < 2 else at["dev_y"]
        return remote(
            self.src.at[shard, rows, :], self.got.at[slot], self.send.at[slot], self.recv.at[slot], device
        )

    def first(self, slots=(1, 3, 0, 2)):
        for slot in slots:
            self.copy(slot).start()

    def first_of(self, index):
        for k, slots in enumerate(((1, 3), (0,), (2,))):
            pl.when(index == k)(lambda: self.first(slots))

    def onward(self, turn):
        return remote(
            self.hold.at[turn],
            self.last.at[turn],
            self.send.at[4 + turn],
            self.recv.at[4 + turn],
            self.at["dev_x"] if turn else self.at["dev_y"],
        )

    def second(self):
        at, half = self.at, self.half
        for turn, shard in enumerate((at["sy"], at["sx"])):
            slot = 2 * turn + 1
            self.copy(slot).wait_recv()
            mine = self.src[shard, pl.ds(turn * half, half), :]
            self.hold[turn] = (mine.astype(F32) + self.got[slot].astype(F32)).astype(BF16)
            self.onward(turn).start()

    def value(self, turn):
        half = self.half
        self.copy(2 * turn).wait_recv()
        self.onward(turn).wait_recv()
        mine = self.src[self.at["shard"], pl.ds(turn * half, half), :]
        return (mine.astype(F32) + self.got[2 * turn].astype(F32)) + self.last[turn].astype(F32)

    def sent(self):
        for slot in range(4):
            self.copy(slot).wait_send()
        for turn in range(2):
            self.onward(turn).wait_send()


def plane_blocks(at, index, plane):
    if not plane:
        return index
    order = [at["sd"], at["sx"], at["sy"], at["shard"]]
    return sum(jnp.where(index == k, shard, 0) for k, shard in enumerate(order))


def weights_kernel(*refs, plane, chips, shards):
    (dots_ref, route_ref, rows_hbm, grad_hbm, h2_hbm, cot_hbm, hid_hbm, da_hbm, db_hbm, back_hbm), refs = refs[:10], refs[10:]
    (sg_hbm, su_hbm, sd_hbm), refs = refs[:3], refs[3:]
    (down_out, sown, sgot, refs) = refs[0], refs[1:4], refs[4:7], refs[7:]
    grads_out, refs = (refs[:2], refs[2:]) if plane else (refs[:1], refs[1:])
    (sum_ref, sy_ref, chosen_ref), refs = refs[:3], refs[3:]
    (rows_ref, grad_ref, h2_ref, cot_ref, down_blocks, in_sem, down_sem), refs = refs[:7], refs[7:]
    (sg_w, su_w, sd_w, sgg_s, sug_s, sdg_s, s_sem, sg_sem, sg_send, sg_recv), refs = refs[:10], refs[10:]
    (chunk, own, from_left, from_right, dots_got), refs = refs[:5], refs[5:]
    (own_sem, chunk_sem, dots_send, dots_recv, chain_send, chain_recv), refs = refs[:6], refs[6:]
    block = chunk.shape[-1]
    at = place()
    me, group, core = at["expert"], 2 * chips, at["core"]
    width = h2_ref.shape[1]
    load = pltpu.make_async_copy(back_hbm, own, own_sem)
    load.start()
    inputs = [
        pltpu.make_async_copy(a, b, in_sem.at[k])
        for k, (a, b) in enumerate(
            [(rows_hbm, rows_ref), (grad_hbm, grad_ref), (h2_hbm, h2_ref), (cot_hbm, cot_ref)]
        )
    ]
    for made in inputs:
        made.start()
    peers = [(lax.rem(me + k, group), at["shard"]) for k in range(1, group)]
    meet(peers + ([at["dev_x"], at["dev_y"]] if plane else []))
    wide = grads_out[0]
    if plane:
        wide, send, recv, *work = refs
        reduces = [
            PlaneReduce(wide.at[n], *work[3 * n : 3 * n + 3], send.at[n], recv.at[n], at) for n in range(2)
        ]
    sources = [da_hbm, db_hbm, hid_hbm]
    dots = [
        remote(dots_ref.at[peer[0]], dots_got.at[me], dots_send.at[k], dots_recv.at[k], peer)
        for k, peer in enumerate(peers)
    ]

    def fetch(array, index):
        shard = plane_blocks(at, index % shards, plane)
        slot = index % 2
        return pltpu.make_async_copy(
            sources[array].at[:, columns(shard * block, block)], chunk.at[slot], chunk_sem.at[slot]
        )

    def fetch_next(index):
        for array in range(3):
            pl.when(index // shards == array)(lambda: fetch(array, index).start())

    def load_shared(k, slot):
        return [
            pltpu.make_async_copy(sg_hbm.at[pl.ds(k * width, width), :], sg_w.at[slot], s_sem.at[slot, 0]),
            pltpu.make_async_copy(su_hbm.at[pl.ds(k * width, width), :], su_w.at[slot], s_sem.at[slot, 1]),
            pltpu.make_async_copy(sd_hbm.at[pl.ds(k * block, block), :], sd_w.at[slot], s_sem.at[slot, 2]),
        ]


    sy_ref[...] = jnp.zeros_like(sy_ref)
    sum_ref[...] = jnp.zeros_like(sum_ref)

    def shared_copies(k):
        stay, over = [], []
        for n, held in enumerate((sgg_s, sug_s, sdg_s)):
            half = held.shape[0] // 2
            mine, other = (held.at[pl.ds(pl.multiple_of(c * half, 16), half), :] for c in (core, 1 - core))
            stay.append((mine, sown[n].at[k], sg_sem.at[n]))
            over.append((other, sgot[n].at[k], sg_send.at[n], sg_recv.at[n, k], at["dev_c"]))
        return stay, over

    def shared_settle(k):
        stay, over = shared_copies(k)
        for copy in stay:
            pltpu.make_async_copy(*copy).wait()
        for copy in over:
            remote(*copy).wait_send()

    def shared_block(k):
        slot = k % 2
        for load in load_shared(k, slot):
            load.wait()

        @pl.when(k + 1 < shards)
        def _():
            for load in load_shared(k + 1, 1 - slot):
                load.start()

        hidden, gate_grad, up_grad, result, back = gated_block(
            h2_ref[...], cot_ref[...], sg_w[slot], su_w[slot], sd_w[slot]
        )
        sy_ref[...] += result
        sum_ref[...] += back
        pl.when(k > 0)(lambda: shared_settle(k - 1))
        sgg_s[...] = dot_tn(h2_ref[...], gate_grad).astype(BF16)
        sug_s[...] = dot_tn(h2_ref[...], up_grad).astype(BF16)
        sdg_s[...] = dot_tn(hidden, cot_ref[...]).astype(BF16)
        stay, over = shared_copies(k)
        for copy in stay:
            pltpu.make_async_copy(*copy).start()
        for copy in over:
            remote(*copy).start()

    for made in load_shared(0, 0):
        made.start()
    fetch(0, 0).start()
    chain = ChainReduce(own, from_left, from_right, chain_send, chain_recv, at, chips)
    load.wait()
    chain.tick(0)
    for made in dots:
        made.start()
    dots_got[me] = dots_ref[me]
    inputs[0].wait()

    @pl.loop(0, 2 * shards)
    def _(index):
        fetch(0, index).wait()
        fetch_next(index + 1)
        array = index // shards
        wide[array, plane_blocks(at, index % shards, plane)] = dot_tn(rows_ref[...], chunk[index % 2]).astype(BF16)
        for n in range(2 if plane else 0):
            pl.when(array == n)(lambda: reduces[n].first_of(index % shards))

        @pl.when(index == 2 * shards - 3)
        def _():
            for step in range(1, chips - 2):
                chain.tick(step)

    for made in inputs[1:]:
        made.wait()

    @pl.loop(2 * shards, 3 * shards)
    def _(index):
        fetch(2, index).wait()
        pl.when(index + 1 < 3 * shards)(lambda: fetch_next(index + 1))
        down_blocks[plane_blocks(at, index % shards, plane)] = dot_tn(chunk[index % 2], grad_ref[...]).astype(BF16)

    store_down = pltpu.make_async_copy(down_blocks, down_out, down_sem)
    store_down.start()
    chain.tick(chips - 2)
    if plane:
        reduces[0].second()

    @pl.loop(0, shards)
    def _(index):
        shared_block(index)
        if plane:
            pl.when(index == shards // 2 - 1)(reduces[1].second)

    for made in dots:
        made.wait()
    for k in range(TOP):
        chosen_ref[pl.ds(k, 1), :] = sum(
            jnp.where(route_ref[pl.ds(k, 1), :] == e, dots_got[e], 0.0) for e in range(group)
        )
    if plane:
        for turn in range(2):
            grads_out[0][pl.ds(turn * reduces[0].half, reduces[0].half), :] = reduces[0].value(turn)
    sum_ref[...] += chain.value()
    chain.sent()
    shared_settle(shards - 1)

    @pl.loop(0, shards)
    def _(k):
        for copy in shared_copies(k)[1]:
            remote(*copy).wait_recv()

    if plane:
        for turn in range(2):
            grads_out[1][pl.ds(turn * reduces[1].half, reduces[1].half), :] = reduces[1].value(turn)
        for reduce in reduces:
            reduce.sent()
    store_down.wait()


def weights(dots, route_rows, rows, grad_rows, h2, cot_low, hidden, gate_grad, up_grad, back_part, shared, ident):
    chips, length, width = back_part.shape
    shards = lax.axis_size("shard")
    plane = shards == 4
    count, hidden_width = hidden.shape
    block, part = hidden_width // shards, shared[0].shape[1]
    vmem, anywhere = pl.BlockSpec(memory_space=pltpu.VMEM), pl.BlockSpec(memory_space=pl.ANY)
    shape, dma = jax.ShapeDtypeStruct, pltpu.SemaphoreType.DMA
    wide = (shards, width, block)
    scratch = [
        pltpu.VMEM((count, width), BF16),
        pltpu.VMEM((count, width), BF16),
        pltpu.VMEM((length, width), BF16),
        pltpu.VMEM((length, width), BF16),
        pltpu.VMEM((shards, block, width), BF16),
        dma((4,)),
        dma,
        pltpu.VMEM((2, width, part), BF16),
        pltpu.VMEM((2, width, part), BF16),
        pltpu.VMEM((2, part, width), BF16),
        pltpu.VMEM((width, part), BF16),
        pltpu.VMEM((width, part), BF16),
        pltpu.VMEM((part, width), BF16),
        dma((2, 3)),
        dma((3,)),
        dma((3,)),
        dma((3, shards)),
        pltpu.VMEM((2, count, block), BF16),
        *ChainReduce.scratch((chips, length, width)),
        pltpu.VMEM(dots.shape, F32),
    ]
    scratch += [dma, dma((2,)), dma((2 * chips - 1,)), dma((2 * chips - 1,)), dma((2 * chips,)), dma((2 * chips,))]
    if plane:
        out_shape = [shape((width, block), F32)] * 2
        scratch += [pltpu.VMEM((2,) + wide, BF16)] + [dma((2, PlaneReduce.COPIES))] * 2
        scratch += PlaneReduce.scratch(wide) * 2
    else:
        out_shape = [shape((2,) + wide, BF16)]
    halves = [shape((shards, width // 2, part), BF16)] * 2 + [shape((shards, part // 2, width), BF16)]
    out_shape = [shape((shards, block, width), BF16), *halves, *halves, *out_shape]
    out_shape += [shape((length, width), F32)] * 2 + [shape((TOP, length), F32)]
    return pl.pallas_call(
        functools.partial(weights_kernel, plane=plane, chips=chips, shards=shards),
        out_shape=out_shape,
        in_specs=[vmem] * 2 + [anywhere] * 11,
        out_specs=[anywhere] * 7 + [vmem] * (len(out_shape) - 7),
        scratch_shapes=scratch,
        compiler_params=pltpu.CompilerParams(
            collective_id=ident, has_side_effects=True, vmem_limit_bytes=VMEM_BYTES
        ),
    )(dots, route_rows, rows, grad_rows, h2, cot_low, hidden, gate_grad, up_grad, back_part, *shared)


def norm_back(source, inverse, gain, grad_in):
    scaled = grad_in * gain
    gain_grad = jnp.sum(grad_in * source * inverse, axis=0, keepdims=True)
    input_part = inverse * scaled - source * inverse**3 * jnp.mean(
        scaled * source, axis=-1, keepdims=True
    )
    return (gain_grad, input_part)


def rear_kernel(*refs, plane, chips, shards):
    (prefix, gains_ref, cos_ref, sin_ref), sources, refs = refs[:4], refs[4:16], refs[16:]
    halves, refs = (refs[:6], refs[6:]) if plane else ([], refs)
    (mix_out, input_grad_out, qkv_grad_out, gain_out), refs = refs[:4], refs[4:]
    pieces, refs = (refs[:4], refs[4:]) if plane else (refs[:1], refs[1:])
    held, refs = refs[:11], refs[11:]
    own, resid_ref, dh_ref, cot_ref, out_ref, att_ref, rot_ref, lse_ref, h1_ref, qkv_ref, x_ref = held
    held = [*held, cot_ref]
    (bias_ref, dres_ref, datt_ref, dqkv_ref, qkv_grad_ref, out_grad_ref, from_left, from_right), refs = refs[:8], refs[8:]
    (load_sem, store_sem, chain_send, chain_recv), refs = refs[:4], refs[4:]
    length, width = x_ref.shape
    at = place()
    core = at["core"]
    loads = [pltpu.make_async_copy(a, b, load_sem.at[k]) for k, (a, b) in enumerate(zip(sources, held))]
    loads[0].start()
    reduces = []
    if plane:
        (send, recv, half_sem, core_send, core_recv), work = refs[:5], refs[5:]
        work = [work[5 * k : 5 * k + 5] for k in range(4)]
        half_loads = [
            [pltpu.make_async_copy(halves[2 * k + n], work[k][n], half_sem.at[k, n]) for n in range(2)]
            for k in range(3)
        ]
        for two in half_loads:
            for made in two:
                made.start()
        reduces = [PlaneReduce(work[k][0], *work[k][2:], send.at[k], recv.at[k], at) for k in range(4)]
        count = work[3][0].shape[1]
        swaps = [
            remote(
                out_grad_ref.at[k, pl.ds(pl.multiple_of((1 - core) * count, 16), count), :],
                work[3][1].at[k],
                core_send.at[k],
                core_recv.at[k],
                at["dev_c"],
            )
            for k in range(shards)
        ]
    for made in loads[1:11]:
        made.start()
    chain_meet(at, chips, [at["dev_x"], at["dev_y"], at["dev_c"]] if plane else [])
    chain = ChainReduce(own, from_left, from_right, chain_send, chain_recv, at, chips)
    loads[0].wait()
    chain.tick(0)
    for made in loads[1:6]:
        made.wait()
    resid = resid_ref[...]
    inverse = lax.rsqrt(jnp.mean(resid * resid, axis=-1, keepdims=True) + EPS)
    gain_two_grad, extra = norm_back(resid, inverse, gains_ref[pl.ds(1, 1), :], dh_ref[...])
    dres = cot_ref[...] + extra
    dres_ref[...] = dres
    loads[11].start()
    low_dres = dres.astype(BF16)
    out_grad = dot_tn(att_ref[...], low_dres).astype(BF16)
    rows = width // shards
    for k in range(shards):
        out_grad_ref[k] = out_grad[k * rows : (k + 1) * rows]

    def add_halves(k):
        @pl.loop(0, shards)
        def _(shard):
            work[k][0][shard] = (
                work[k][0][shard].astype(F32) + work[k][1][shard].astype(F32)
            ).astype(BF16)

        reduces[k].first()

    if plane:
        for made in swaps:
            made.start()
        for k in range(3):
            for made in half_loads[k]:
                made.wait()
            add_halves(k)
        for k in range(shards):
            work[3][0][k] = out_grad_ref[k, pl.ds(pl.multiple_of(core * count, 16), count), :]
        for made in swaps:
            made.wait()
        add_halves(3)
    else:
        store_out = pltpu.make_async_copy(out_grad_ref, pieces[0], store_sem.at[3])
        store_out.start()
    datt_ref[...] = dot_nt(low_dres, out_ref[...]).astype(BF16)
    set_bias(bias_ref, prefix)
    scale = HEAD_DIM**-0.5
    for made in loads[6:11]:
        made.wait()

    block = length // 2

    def pair(j):
        queries, keys, values = (
            rot_ref[:, columns(part * width + j * 128, 128)] for part in range(3)
        )
        grads = datt_ref[:, columns(j * 128, 128)]
        low = lax.broadcasted_iota(jnp.int32, (block, 128), 1) < HEAD_DIM
        lanes = lax.broadcasted_iota(jnp.int32, (block, 128), 1)

        def keep(part, rows, value):
            if part < 2:
                value = value * cos_ref[rows, :] - partner(value) * sin_ref[rows, :]
            dqkv_ref[rows, columns(part * width + j * 128, 128)] = value.astype(BF16)

        sums = []
        for start in range(0, length, block):
            rows, seen = pl.ds(start, block), start + block
            query = two_heads(queries[start:seen] * scale)
            grad = two_heads(grads[start:seen])
            bias, lse = bias_ref[rows, :seen], lse_ref[rows, :]
            logsum = jnp.concatenate(
                [
                    jnp.sum(jnp.where(lanes == 2 * j + head, lse, 0.0), axis=1, keepdims=True)
                    for head in range(2)
                ],
                axis=0,
            )
            scores = dot_nt(query, keys[:seen])
            scores = jnp.concatenate([scores[:block] + bias, scores[block:] + bias], axis=0)
            probs = jnp.exp(scores - logsum)
            probs_grad = dot_nt(grad, values[:seen])
            inner = jnp.sum(probs * probs_grad, axis=-1, keepdims=True)
            score_grad = (probs * (probs_grad - inner)).astype(BF16)
            query_grad = dot_nn(score_grad, keys[:seen]) * scale
            keep(0, rows, jnp.where(low, query_grad[:block], query_grad[block:]))
            sums.append((dot_tn(score_grad, query), dot_tn(probs.astype(BF16), grad)))
        for part in range(2):
            keep(1 + part, pl.ds(0, block), sums[0][part] + sums[1][part][:block])
            keep(1 + part, pl.ds(block, block), sums[1][part][block:])

    pairs = width // 128

    @pl.loop(0, pairs)
    def _(j):
        pair(j)

        @pl.when(j == pairs // 3 - 1)
        def _():
            for step in range(1, chips - 2):
                chain.tick(step)


    @pl.loop(0, 3 * width // 256)
    def _(k):
        cols = columns(k * 256, 256)
        qkv_grad_ref[:, cols] = dot_tn(h1_ref[...], dqkv_ref[:, cols]).astype(BF16)

    stores = [pltpu.make_async_copy(qkv_grad_ref, qkv_grad_out, store_sem.at[0])]
    stores[0].start()
    chain.tick(chips - 2)
    for reduce in reduces:
        reduce.second()
    dh1 = dot_nt(dqkv_ref[...], qkv_ref[...])
    x = x_ref[...]
    inverse = lax.rsqrt(jnp.mean(x * x, axis=-1, keepdims=True) + EPS)
    gain_one_grad, extra = norm_back(x, inverse, gains_ref[pl.ds(0, 1), :], dh1)
    dres_ref[...] += extra
    stores.append(pltpu.make_async_copy(dres_ref, input_grad_out, store_sem.at[1]))
    stores[1].start()
    index = lax.broadcasted_iota(jnp.int32, gain_out.shape[1:], 0)
    gain_rows = jnp.where(index == 0, gain_one_grad, jnp.where(index == 1, gain_two_grad, 0.0)).astype(BF16)
    for k in range(shards):
        gain_out[k] = gain_rows
    for reduce, piece in zip(reduces, pieces):
        count = piece.shape[1]
        both = jnp.concatenate([reduce.value(0), reduce.value(1)], axis=0)
        for k in range(chips):
            piece[k] = both[k * count : (k + 1) * count].astype(BF16)
        reduce.sent()
    loads[11].wait()
    resid_ref[...] += cot_ref[...] + chain.value()
    stores.append(pltpu.make_async_copy(resid_ref, mix_out, store_sem.at[2]))
    stores[2].start()
    chain.sent()
    if not plane:
        stores.append(store_out)
    for made in stores:
        made.wait()


def rear(prefix, inputs, cotangent, resid, dh2, shared_out, gains, kept, full, mix_part, halves, ident):
    length, width = inputs.shape
    chips, shards = mix_part.shape[0], lax.axis_size("shard")
    plane = shards == 4
    cosine, sine = rope_lanes(length)
    turned, attended, normed_one, logsum = kept
    vmem, anywhere = pl.BlockSpec(memory_space=pltpu.VMEM), pl.BlockSpec(memory_space=pl.ANY)
    shape, dma = jax.ShapeDtypeStruct, pltpu.SemaphoreType.DMA
    sources = [mix_part, resid, dh2, cotangent, full[1], attended, turned, logsum, normed_one, full[0], inputs]
    sources.append(shared_out)
    operands = [prefix, gains, cosine, sine, *sources]
    in_specs = [pl.BlockSpec(memory_space=pltpu.SMEM)] + [vmem] * 3 + [anywhere] * 12
    out_blocks = (shards, width // shards, width)
    out_shape = [
        shape((length, width), F32),
        shape((length, width), F32),
        shape((width, 3 * width), BF16),
        shape((shards, 64, width), BF16),
    ]
    out_specs = [anywhere] * 3 + [vmem]
    scratch = [pltpu.VMEM(v.shape, v.dtype) for v in sources[:11]]
    scratch += [
        pltpu.VMEM((length, length), F32),
        pltpu.VMEM((length, width), F32),
        pltpu.VMEM((length, width), BF16),
        pltpu.VMEM((length, 3 * width), BF16),
        pltpu.VMEM((width, 3 * width), BF16),
        pltpu.VMEM(out_blocks, BF16),
        *ChainReduce.scratch((chips, length, width))[:2],
        dma((12,)),
        dma((4,)),
        dma((2 * chips,)),
        dma((2 * chips,)),
    ]
    if plane:
        operands += halves
        in_specs += [anywhere] * 6
        out_specs += [vmem] * 4
        scratch += [dma((4, PlaneReduce.COPIES))] * 2 + [dma((3, 2))] + [dma((shards,))] * 2
        half_shapes = [v.shape for v in halves[::2]] + [(shards, out_blocks[1] // 2, width)]
        for s in half_shapes:
            out_shape.append(shape((chips, s[1] // chips, s[2]), BF16))
            scratch += [pltpu.VMEM(s, BF16)] * 2 + PlaneReduce.scratch(s)
    else:
        out_shape.append(shape(out_blocks, BF16))
        out_specs.append(anywhere)
    return pl.pallas_call(
        functools.partial(rear_kernel, plane=plane, chips=chips, shards=shards),
        out_shape=out_shape,
        in_specs=in_specs,
        out_specs=out_specs,
        scratch_shapes=scratch,
        compiler_params=pltpu.CompilerParams(
            collective_id=ident, has_side_effects=True, vmem_limit_bytes=VMEM_BYTES
        ),
    )(*operands)


def last_kernel(*refs, chips, shards):
    (attention, pieces, down_hbm), refs = (refs[:2], refs[2:6], refs[6]), refs[7:]
    alls_out, down_out, refs = refs[:6], refs[6], refs[7:]
    halves, refs = [refs[3 * k : 3 * k + 3] for k in range(2)], refs[6:]
    plane_work, refs = refs[:10], refs[10:]
    chain_work, refs = [refs[4 * k : 4 * k + 4] for k in range(6)], refs[24:]
    load_sem, core_send, core_recv, plane_send, plane_recv, sums_send, sums_recv, all_send, all_recv, all_local = refs
    at = place()
    core = at["core"]
    loads, swaps = [], []
    for k in range(2):
        rows = attention[k].shape[1] // 2
        for n, c in enumerate((core, 1 - core)):
            part = attention[k].at[:, pl.ds(pl.multiple_of(c * rows, 16), rows), :]
            loads.append(pltpu.make_async_copy(part, halves[k][n], load_sem.at[2 * k + n]))
        swaps.append(remote(halves[k][1], halves[k][2], core_send.at[k], core_recv.at[k], at["dev_c"]))
    loads += [pltpu.make_async_copy(pieces[k], chain_work[2 + k][0], load_sem.at[4 + k]) for k in range(4)]
    loads.append(pltpu.make_async_copy(down_hbm, plane_work[0], load_sem.at[8]))
    for made in loads:
        made.start()
    sums = [
        ChainReduce(*chain_work[k][:3], sums_send.at[k], sums_recv.at[k], at, chips) for k in range(6)
    ]
    alls = [
        ChainGather(chain_work[k][3], alls_out[k], all_send.at[k], all_recv.at[k], all_local.at[k], at, chips)
        for k in range(6)
    ]
    planes = [
        PlaneReduce(src, *plane_work[1 + 3 * k : 4 + 3 * k], plane_send.at[k], plane_recv.at[k], at)
        for k, src in enumerate([plane_work[0], halves[0][0], halves[1][0]])
    ]
    shared, attn = (2, 3, 4, 5), (0, 1)
    chain_meet(at, chips, [at["dev_x"], at["dev_y"], at["dev_c"]])
    for k in attn:
        loads[2 * k].wait()
        loads[2 * k + 1].wait()
        swaps[k].start()

    def tick(group, step):
        for k in group:
            sums[k].tick(step)

    def step_all(group, step):
        for k in group:
            alls[k].step(step)

    def total(group):
        for k in group:
            chain_work[k][3][...] = sums[k].value().astype(BF16)
            alls[k].start()

    for k in range(4, 9):
        loads[k].wait()
    tick(shared, 0)
    for k in attn:
        swaps[k].wait()

        @pl.loop(0, shards)
        def _(shard):
            halves[k][0][shard] = (
                halves[k][0][shard].astype(F32) + halves[k][2][shard].astype(F32)
            ).astype(BF16)

        planes[1 + k].first()
    for step in range(1, chips - 1):
        tick(shared, step)
    for k in attn:
        planes[1 + k].second()
    planes[0].first()
    for k in attn:
        count = chain_work[k][0].shape[1]
        both = jnp.concatenate([planes[1 + k].value(0), planes[1 + k].value(1)], axis=0)
        for n in range(chips):
            sums[k].own[n] = both[n * count : (n + 1) * count].astype(BF16)
    tick(attn, 0)
    total(shared)
    for step in range(1, chips - 1):
        tick(attn, step)
        step_all(shared, step)
    total(attn)
    step_all(shared, chips - 1)
    planes[0].second()
    for step in range(1, chips):
        step_all(attn, step)
    for turn in range(2):
        down_out[pl.ds(turn * planes[0].half, planes[0].half), :] = planes[0].value(turn)
    for k in shared + attn:
        for step in range(chips):
            alls[k].finish(step)
        alls[k].sent()
        sums[k].sent()
    for reduce in planes:
        reduce.sent()


def last(qkv_grad, gain_grads, pieces, down_blocks, ident):
    shards, chips = lax.axis_size("shard"), lax.axis_size("expert") // 2
    vmem, anywhere = pl.BlockSpec(memory_space=pltpu.VMEM), pl.BlockSpec(memory_space=pl.ANY)
    shape, dma = jax.ShapeDtypeStruct, pltpu.SemaphoreType.DMA
    attention = [qkv_grad, gain_grads]
    half_shapes = [(shards, v.shape[1] // 2, v.shape[2]) for v in attention]
    chain_shapes = [(chips, v.shape[1] // 2 // chips, v.shape[2]) for v in attention] + [v.shape for v in pieces]
    out_shape = [shape((2 * chips,) + s[1:], BF16) for s in chain_shapes]
    out_shape.append(shape(down_blocks.shape[1:], F32))
    scratch = []
    for s in half_shapes:
        scratch += [pltpu.VMEM(s, BF16)] * 3
    scratch.append(pltpu.VMEM(down_blocks.shape, BF16))
    for s in [down_blocks.shape] + half_shapes:
        scratch += PlaneReduce.scratch(s)
    for s in chain_shapes:
        scratch += ChainReduce.scratch(s) + [pltpu.VMEM(s[1:], BF16)]
    scratch += [
        dma((9,)),
        dma((2,)),
        dma((2,)),
        dma((3, PlaneReduce.COPIES)),
        dma((3, PlaneReduce.COPIES)),
        dma((6, 2 * chips)),
        dma((6, 2 * chips)),
        dma((6, ChainGather.copies(chips))),
        dma((6, ChainGather.copies(chips))),
        dma((6,)),
    ]
    return pl.pallas_call(
        functools.partial(last_kernel, chips=chips, shards=shards),
        out_shape=out_shape,
        in_specs=[anywhere] * 7,
        out_specs=[vmem] * 7,
        scratch_shapes=scratch,
        compiler_params=pltpu.CompilerParams(
            collective_id=ident, has_side_effects=True, vmem_limit_bytes=VMEM_BYTES
        ),
    )(qkv_grad, gain_grads, *pieces, down_blocks)


def finish_kernel(*refs, chips, counts):
    total = sum(counts)
    inputs, outputs, refs = refs[:total], refs[total : 2 * total], refs[2 * total :]
    held, made, (load_sem, store_sem) = refs[:total], refs[total:-2], refs[-2:]
    plain, sums = counts
    loads = [pltpu.make_async_copy(a, b, load_sem.at[k]) for k, (a, b) in enumerate(zip(inputs, held))]
    ready = [*held[:plain], *made]
    stores = [
        pltpu.make_async_copy(a, b, store_sem.at[k]) for k, (a, b) in enumerate(zip(ready, outputs))
    ]
    for copy in loads:
        copy.start()
    for k in range(plain):
        loads[k].wait()
        stores[k].start()
    for k in range(plain, plain + sums):
        loads[k].wait()
        count = held[k].shape[1]
        if k == plain:
            part, shard = ready[k].shape[1], lax.axis_index("shard")
            rows = held[k][0].astype(F32)
            ready[k][...] = sum(
                jnp.where(shard == n, rows[:, n * part : (n + 1) * part], 0.0) for n in range(rows.shape[1] // part)
            )
        else:
            for n in range(chips):
                for c in range(2):
                    ready[k][pl.ds((c * chips + n) * count, count), :] = held[k][2 * n + c].astype(F32)
        stores[k].start()
    for copy in stores:
        copy.wait()


def finish(plain, sums):
    chips = sums[0].shape[0] // 2
    shape, dma = jax.ShapeDtypeStruct, pltpu.SemaphoreType.DMA
    anywhere = pl.BlockSpec(memory_space=pl.ANY)
    inputs = [*plain, *sums]
    made = [shape((sums[0].shape[1], sums[0].shape[2] // lax.axis_size("shard")), F32)]
    made += [shape((v.shape[0] * v.shape[1], v.shape[2]), F32) for v in sums[1:]]
    out_shape = [shape(v.shape, F32) for v in plain] + made
    scratch = [pltpu.VMEM(v.shape, v.dtype) for v in inputs] + [pltpu.VMEM(s.shape, F32) for s in made]
    return pl.pallas_call(
        functools.partial(finish_kernel, chips=chips, counts=(len(plain), len(sums))),
        out_shape=out_shape,
        in_specs=[anywhere] * len(inputs),
        out_specs=[anywhere] * len(out_shape),
        scratch_shapes=scratch + [dma((len(inputs),)), dma((len(out_shape),))],
        compiler_params=pltpu.CompilerParams(vmem_limit_bytes=VMEM_BYTES),
    )(*inputs)


def on_device(
    inputs,
    cotangent,
    norm_one,
    qkv_weight,
    out_weight,
    norm_two,
    shared_gate,
    shared_up,
    shared_down,
    expert_gate,
    expert_up,
    expert_down,
    gate_weights,
    routes,
    prefix,
):
    length, width = inputs.shape
    experts, shards = lax.axis_size("expert"), lax.axis_size("shard")
    me, shard = lax.axis_index("expert"), lax.axis_index("shard")
    route_rows = routes.T
    (
        cot_all,
        table_all,
        normed_one,
        turned,
        attended,
        resid,
        normed_two,
        cot_low,
        logsum,
        gains,
        qkv_full,
        out_full,
    ) = front(
        prefix,
        inputs,
        cotangent,
        route_rows,
        gate_weights.T,
        jnp.stack([norm_one, norm_two]),
        [qkv_weight, out_weight],
        1,
    )
    (
        rows,
        grad_rows,
        hidden,
        gate_pre_grad,
        up_pre_grad,
        mix_part,
        back_part,
        weight_back,
        *shared_full,
    ) = middle(
        normed_two,
        table_all,
        cot_all,
        [expert_gate, expert_up, expert_down],
        [shared_gate, shared_up, shared_down],
        2,
    )
    rows, grad_rows, hidden, gate_pre_grad, up_pre_grad = (
        v.reshape(-1, v.shape[-1]) for v in (rows, grad_rows, hidden, gate_pre_grad, up_pre_grad)
    )
    down_term, *shared_halves, normed_two_grad, shared_out, gate_weights_grad = weights(
        weight_back,
        route_rows,
        rows,
        grad_rows,
        normed_two,
        cot_low,
        hidden,
        gate_pre_grad,
        up_pre_grad,
        back_part,
        shared_full,
        3,
    )
    gate_up = shared_halves[6:]
    shared_halves = [shared_halves[k + n] for k in range(3) for n in (0, 3)]
    output, input_grad, qkv_grad, gain_grads, *pieces = rear(
        prefix,
        inputs,
        cotangent,
        resid,
        normed_two_grad,
        shared_out,
        gains,
        [turned, attended, normed_one, logsum],
        [qkv_full, out_full],
        mix_part,
        shared_halves,
        4,
    )
    qkv_grad = qkv_grad.reshape(shards, width // shards, 3 * width)
    if shards == 4:
        qkv_sum, gain_sums, *pieces, down_term = last(qkv_grad, gain_grads, pieces, down_term, 5)
        gate_term, up_term = gate_up
        output, input_grad, gate_term, up_term, down_term, gain_sums, qkv_sum, *shared_sums, out_sum = finish(
            [output, input_grad, gate_term, up_term, down_term], [gain_sums, qkv_sum, *pieces]
        )
    else:

        def over_plane(value):
            return lax.psum_scatter(value, "shard", scatter_dimension=0, tiled=True)[0]

        def over_all(value):
            return lax.psum(over_plane(value), "expert").astype(F32)

        gate_term, up_term, down_term = (
            over_plane(v).astype(F32) for v in (*gate_up[0], down_term)
        )
        qkv_sum, gain_sums, out_sum = over_all(qkv_grad), over_all(gain_grads), over_all(pieces[0])
        part = width // shards
        gain_sums = lax.dynamic_slice(gain_sums, (0, shard * part), (gain_sums.shape[0], part))
        shared_sums = []
        for own, got in zip(shared_halves[::2], shared_halves[1::2]):
            half = (own.astype(F32) + got.astype(F32)).astype(BF16)
            both = jnp.concatenate([jnp.where(me % 2 == c, half, 0) for c in range(2)], axis=1)
            shared_sums.append(over_all(both))
    return (
        output,
        input_grad,
        gain_sums[0],
        qkv_sum,
        out_sum,
        gain_sums[1],
        *shared_sums,
        gate_term[None],
        up_term[None],
        down_term[None],
        gate_weights_grad.T,
    )


def solution(mesh):
    tokens = P(("expert", "shard"), None)
    in_specs = (
        tokens,
        tokens,
        P("shard"),
        P("shard", None),
        P("shard", None),
        P("shard"),
        P(None, "shard"),
        P(None, "shard"),
        P("shard", None),
        P("expert", None, None),
        P("expert", None, None),
        P("expert", None, None),
        tokens,
        tokens,
        P(("expert", "shard")),
    )
    out_specs = (
        tokens,
        tokens,
        P("shard"),
        P("shard", None),
        P("shard", None),
        P("shard"),
        P(None, "shard"),
        P(None, "shard"),
        P("shard", None),
        P("expert", None, "shard"),
        P("expert", None, "shard"),
        P("expert", "shard", None),
        tokens,
    )
    return jax.shard_map(
        on_device, mesh=mesh, in_specs=in_specs, out_specs=out_specs, check_vma=False
    )
```
